32 devices in a mesh: groups: 2 (over y), tok: 4 (over z), head: 2 (over x), rep: 2 (over core).
Axes of the slice: x: 2, y: 2, z: 4, core: 2. Of those that a mesh axis runs over, the one named last changes fastest.
Arguments:
- keys: bfloat16 [1024, 1024], P(('groups', 'tok'), 'head'), parts along dimension 0, may hold values from -6 to 6
- values: bfloat16 [1024, 1024], P(('groups', 'tok'), 'head'), parts along dimension 0, may hold values from -6 to 6
- rates: float32 [1024, 2], P(('groups', 'tok'), 'head'), parts along dimension 0, may hold values from 0.0003 to 0.006
- queries: bfloat16 [1024, 1024], P(('groups', 'tok'), 'head'), parts along dimension 0, may hold values from -6 to 6
- stream: bfloat16 [1024, 1024], P(('groups', 'tok'), 'head'), parts along dimension 0, may hold values from -16 to 16
- gain: float32 [1024], P('head'), may hold values from 0.1 to 1.9
- counts: int32 [8], P(('groups', 'tok')), parts along dimension 0, may hold values from 1 to 128, 307 in all
- fw_one: float32 [2, 512, 1024], P('head', None, 'rep'), may hold values from -0.25 to 0.25
- fw_three: float32 [2, 512, 1024], P('head', None, 'rep'), may hold values from -0.25 to 0.25
- fw_two: float32 [2, 1024, 512], P('head', 'rep'), may hold values from -1 to 1
- mlp_up: bfloat16 [1024, 4096], P('tok', ('head', 'rep')), may hold values from -0.1875 to 0.1875
- mlp_down: bfloat16 [4096, 1024], P(('head', 'rep'), 'tok'), may hold values from -0.09375 to 0.09375
Outputs:
- result: bfloat16 [1024, 1024], P(('groups', 'tok'), ('head', 'rep')), parts along dimension 0
The draws below stay inside these ranges and needn't reach their ends.
There are 2 independent parts, one for each index of `groups`. The reference program is written for one: setup_inputs(seed, part) draws one part's arguments, and reference() takes and returns one part's arrays. A program takes and returns all parts, laid end to end along the dimension named above; an argument that names none is the same for every part. Nothing has to cross between parts.
Inputs may be any that keep to these rules, and one draw needn't show every extreme that they name: counts sum to 307, and one index of tok is full.
All inputs are finite; a program needn't handle non-finite values. No bound on the sum of `counts` on one device may be relied on, other than what follows from the above.
Results may differ from the reference program's by a relative error of at most 0.04.
Values may be sent and summed in bfloat16 or wider, within the bound.
No kernel may reach another device: no remote copies, remote signals or barrier semaphores. Data moves between devices by JAX's collectives and lax.ppermute only.
A program may use at most 64 MiB of HBM per device.

```python
import math
import jax
import jax.numpy as jnp
import numpy as np
from jax import lax

DH = 512
DF = 1024
TGT_CAP = 128
HEADS = 2
D = 1024
MLP_HID = 4096
IN_TOKENS = 512
TGT_ROWS = 512
N_TOK = 4
N_HEAD = 2
N_REP = 2


def draw_stream(key, part):
    position = jnp.arange(D, dtype=jnp.float32) / (D - 1.0)
    base = jnp.clip(jax.random.normal(key, (TGT_ROWS, D), jnp.float32), -4.0, 4.0)
    col_scale = jnp.exp(math.log(0.4) + position * math.log(6.25))
    return (base * col_scale[None, :]).astype(jnp.bfloat16)


def draw_fw_two(key, part):
    position = jnp.arange(DF, dtype=jnp.float32) / (DF - 1.0)
    base = jnp.clip(jax.random.normal(key, (HEADS, DF, DH), jnp.float32), -4.0, 4.0)
    row_scale = jnp.exp(math.log(0.3) + position * math.log(10.0))
    scaled = base * row_scale[None, :, None] / math.sqrt(DF)
    return jnp.clip(scaled, -1.0, 1.0).astype(jnp.float32)


def steps_of(rng, dims, pieces, least, top_value):
    loudness, own = 1.0, jax.random.fold_in(rng, 6)
    for axis_at, shards_of in pieces:
        steps = jnp.exp(jax.random.uniform(jax.random.fold_in(own, axis_at), (shards_of,), jnp.float32, least / len(pieces), top_value / len(pieces)))
        loudness = loudness * jnp.repeat(steps, dims[axis_at] // shards_of).reshape([-1 if axis == axis_at else 1 for axis in range(len(dims))])
    return loudness


def profile(amount, total, most, lean):
    portions = [(1 << 20) // math.isqrt(standing ** lean) + 1 for standing in range(2, amount + 1)]
    rest, given = total - most - (amount - 1), [1] * (amount - 1)
    while rest > 0:
        free = [i for i in range(amount - 1) if given[i] < most]
        whole, budget = sum([portions[i] for i in free]), rest
        for i in free:
            extra = min(most - given[i], max(1, budget * portions[i] // whole), rest)
            given[i] = given[i] + extra
            rest = rest - extra
    return np.array([most] + given)


def uneven(own_key, amount, total, bound, skew):
    if amount == 2:
        one = jax.random.randint(own_key, (), max(1, total - bound), min(bound, total - 1) + 1)
        return jnp.stack([one, total - one])
    sizes = jnp.asarray(profile(amount, total, bound, skew), jnp.int32)
    twos = (amount - 1) // 2
    giver, receiver = sizes[1:1 + 2 * twos:2], sizes[2:2 + 2 * twos:2]
    margin = jnp.minimum(giver - 1, bound - receiver)
    moved = jax.random.randint(jax.random.fold_in(own_key, 1), (twos,), 0, 1 << 20) % (margin + 1)
    sizes = sizes.at[1:1 + 2 * twos:2].set(giver - moved).at[2:2 + 2 * twos:2].set(receiver + moved)
    return sizes[jax.random.permutation(jax.random.fold_in(own_key, 2), amount)]


def scatter_about(own_key, dims, scale, most, shards=(), kind=jnp.bfloat16):
    factor_of = steps_of(own_key, dims, shards, -0.22, 0.18) if shards else 1.0
    entries = jax.random.normal(own_key, dims, jnp.float32) * scale * factor_of
    return jnp.minimum(jnp.maximum(entries, -most), most).astype(kind)


def setup_inputs(seed: int = 0, part: int = 0) -> dict:
    splits = jax.random.split(jax.random.key(seed), 13)
    own_keys = jax.random.split(jax.random.fold_in(splits[12], part), 13)
    keys = scatter_about(own_keys[0], (IN_TOKENS, D), 1.0, 6.0, ((0, 4), (1, 2)))
    values = scatter_about(own_keys[1], (IN_TOKENS, D), 1.0, 6.0, ((0, 4), (1, 2)))
    rates = jnp.clip(jnp.exp(math.log(0.006) - 2.9957322 * jax.random.uniform(own_keys[2], (IN_TOKENS, HEADS), jnp.float32) ** steps_of(own_keys[2], (IN_TOKENS, HEADS), ((0, 4), (1, 2)), -0.2, 0.2)), 0.0003, 0.006)
    queries = scatter_about(own_keys[3], (TGT_ROWS, D), 1.0, 6.0, ((0, 4), (1, 2)))
    stream = draw_stream(jax.random.fold_in(jax.random.fold_in(splits[12], part), 71), part)
    gain = jnp.clip(1.0 + 0.18 * jax.random.normal(splits[5], (D,), jnp.float32), 0.1, 1.9)
    counts = uneven(own_keys[6], N_TOK, N_TOK * TGT_CAP * 3 // 5, TGT_CAP, 2).astype(jnp.int32)
    fw_one = scatter_about(splits[7], (HEADS, DH, DF), DH ** -0.5, 0.25, ((0, 2), (2, 2)), jnp.float32)
    fw_three = scatter_about(splits[8], (HEADS, DH, DF), DH ** -0.5, 0.25, ((0, 2), (2, 2)), jnp.float32)
    fw_two = draw_fw_two(jax.random.fold_in(splits[12], 71), part)
    mlp_up = scatter_about(splits[10], (D, MLP_HID), D ** -0.5, 0.1875, ((0, 4), (1, 4)))
    mlp_down = scatter_about(splits[11], (MLP_HID, D), MLP_HID ** -0.5, 0.09375, ((0, 4), (1, 4)))
    return {"keys": keys, "values": values, "rates": rates, "queries": queries, "stream": stream, "gain": gain, "counts": counts, "fw_one": fw_one, "fw_three": fw_three, "fw_two": fw_two, "mlp_up": mlp_up, "mlp_down": mlp_down}


def swish_parts(pre_act):
    sigmoid_val = jax.nn.sigmoid(pre_act)
    return (pre_act * sigmoid_val, sigmoid_val * (1.0 + pre_act * (1.0 - sigmoid_val)))

def weight_norm(former, updated):
    scale_old = jnp.sqrt(lax.optimization_barrier(jnp.sum(former * former, axis=0)))
    scale_new = lax.rsqrt(lax.optimization_barrier(jnp.sum(updated * updated, axis=0)) + 1e-06)
    return updated * scale_old * scale_new

def reference(keys, values, rates, queries, stream, gain, counts, fw_one, fw_three, fw_two, mlp_up, mlp_down):
    head_rows = []
    for head_id in range(HEADS):
        low_col = head_id * DH
        high_col = low_col + DH
        key_head = keys[:, low_col:high_col]
        value_head = values[:, low_col:high_col]
        query_head = queries[:, low_col:high_col]
        rate_head = rates[:, head_id:head_id + 1]
        first_pre = jnp.dot(key_head, fw_one[head_id].astype(jnp.bfloat16), preferred_element_type=jnp.float32)
        third_pre = jnp.dot(key_head, fw_three[head_id].astype(jnp.bfloat16), preferred_element_type=jnp.float32)
        act_first, slope_first = swish_parts(first_pre)
        hidden_in = (act_first * third_pre).astype(jnp.bfloat16)
        scaled_val = (rate_head * value_head.astype(jnp.float32)).astype(jnp.bfloat16)
        back_hidden = jnp.dot(scaled_val, fw_two[head_id].astype(jnp.bfloat16).T, preferred_element_type=jnp.float32)
        err_first = (back_hidden * third_pre * slope_first).astype(jnp.bfloat16)
        err_third = (back_hidden * act_first).astype(jnp.bfloat16)
        grad_first = jnp.dot(key_head.T, err_first, preferred_element_type=jnp.float32)
        grad_third = jnp.dot(key_head.T, err_third, preferred_element_type=jnp.float32)
        grad_second = jnp.dot(hidden_in.T, scaled_val, preferred_element_type=jnp.float32)
        new_first = weight_norm(fw_one[head_id], fw_one[head_id] + grad_first).astype(jnp.bfloat16)
        new_third = weight_norm(fw_three[head_id], fw_three[head_id] + grad_third).astype(jnp.bfloat16)
        new_second = weight_norm(fw_two[head_id], fw_two[head_id] + grad_second).astype(jnp.bfloat16)
        query_first = jnp.dot(query_head, new_first, preferred_element_type=jnp.float32)
        query_third = jnp.dot(query_head, new_third, preferred_element_type=jnp.float32)
        query_act, unused_slope = swish_parts(query_first)
        query_hidden = (query_act * query_third).astype(jnp.bfloat16)
        head_out = jnp.dot(query_hidden, new_second, preferred_element_type=jnp.float32)
        head_rows.append(stream[:, low_col:high_col].astype(jnp.float32) + head_out)
    mixed_rows = jnp.concatenate(head_rows, axis=1)
    inv_rms = lax.rsqrt(lax.optimization_barrier(jnp.mean(mixed_rows * mixed_rows, axis=1, keepdims=True)) + 1e-06)
    normed = (mixed_rows * inv_rms * gain).astype(jnp.bfloat16)
    expanded = jax.nn.gelu(jnp.dot(normed, mlp_up, preferred_element_type=jnp.float32), approximate=False).astype(jnp.bfloat16)
    block_width = MLP_HID // (N_HEAD * N_REP)

    def add_block(block_id, running):
        offset = (block_id * block_width).astype(jnp.int32)
        part_hidden = lax.dynamic_slice_in_dim(expanded, offset, block_width, 1)
        part_down = lax.dynamic_slice_in_dim(mlp_down, offset, block_width, 0)
        product = jnp.dot(part_hidden, part_down, preferred_element_type=jnp.float32)
        return running + lax.optimization_barrier(product.astype(jnp.bfloat16)).astype(jnp.float32)
    summed = lax.fori_loop(0, N_HEAD * N_REP, add_block, jnp.zeros((TGT_ROWS, D), jnp.float32))
    slot_index = jnp.arange(TGT_ROWS, dtype=jnp.int32) % TGT_CAP
    limits = jnp.repeat(counts, TGT_CAP, total_repeat_length=TGT_ROWS)
    live_rows = slot_index < limits
    return jnp.where(live_rows[:, None], mixed_rows + summed, 0.0).astype(jnp.bfloat16)
```

```python
import functools

import jax
import jax.numpy as jnp
import numpy as np
from jax import lax
from jax.experimental import pallas as pl
from jax.experimental.pallas import tpu as pltpu
from jax.sharding import PartitionSpec as P

BF, F32 = jnp.bfloat16, jnp.float32
VMEM_BYTES = 48 << 20


def dot(a, b, dims=((1,), (0,))):
    return lax.dot_general(a, b, (dims, ((), ())), preferred_element_type=F32)


def shifted(x, axes, shifts):
    sizes = [lax.axis_size(a) for a in axes]
    pairs = []
    for here in range(int(np.prod(sizes))):
        at = np.unravel_index(here, sizes)
        there = [(a + s) % n for a, s, n in zip(at, shifts, sizes)]
        pairs.append((int(np.ravel_multi_index(there, sizes)), here))
    return lax.ppermute(x, axes, pairs)


def call(kernel, outs, args, scratch=(), flops=0):
    moved = sum(int(np.prod(x.shape)) * x.dtype.itemsize for x in (*args, *outs))
    return pl.pallas_call(
        kernel,
        out_shape=outs,
        in_specs=[pl.BlockSpec(memory_space=pltpu.VMEM)] * len(args),
        out_specs=[pl.BlockSpec(memory_space=pltpu.VMEM)] * len(outs),
        scratch_shapes=list(scratch),
        compiler_params=pltpu.CompilerParams(vmem_limit_bytes=VMEM_BYTES),
        cost_estimate=pl.CostEstimate(flops=flops, bytes_accessed=moved, transcendentals=0),
    )(*args)


def shape(dims, dtype):
    return jax.ShapeDtypeStruct(dims, dtype)


def half(ref_width):
    return ref_width // lax.axis_size("rep")


def fast_kernel(n_pieces, *refs):
    pieces, refs = refs[:n_pieces], refs[n_pieces:]
    w1, w3, w2, q, own_out, own_sq, send, ks, es, hp = refs
    dh, hidden = w1.shape
    at = 0
    for p in pieces:
        n = p.shape[0]
        ks[at : at + n, :] = p[:, :dh]
        es[at : at + n, :] = p[:, dh:]
        at += n
    tokens, step, block = at, min(at, 512), min(hidden, 256)
    old_sq = jnp.zeros((1, dh), F32)
    new_sq = jnp.zeros((1, dh), F32)
    for j in range(0, hidden, block):
        w1j, w3j, w2j = w1[:, j : j + block], w3[:, j : j + block], w2[j : j + block, :]
        w1b, w3b, w2b = w1j.astype(BF), w3j.astype(BF), w2j.astype(BF)

        def grads(i, sums):
            rows = pl.ds(pl.multiple_of(i * step, step), step)
            k, e = ks[rows, :], es[rows, :]
            a1, a3, b = dot(k, w1b), dot(k, w3b), dot(e, w2b, ((1,), (1,)))
            sig = jax.nn.sigmoid(a1)
            act = a1 * sig
            g = (act * a3).astype(BF)
            r1 = (b * a3 * (sig * (1.0 + a1 * (1.0 - sig)))).astype(BF)
            r3 = (b * act).astype(BF)
            first = ((0,), (0,))
            return sums[0] + dot(k, r1, first), sums[1] + dot(k, r3, first), sums[2] + dot(g, e, first)

        sums = (w1j, w3j, w2j)
        if tokens == step:
            u1, u3, u2 = grads(0, sums)
        else:
            u1, u3, u2 = lax.fori_loop(0, tokens // step, grads, sums)

        def normed(old, new):
            top = jnp.sqrt(jnp.sum(old * old, axis=0, keepdims=True))
            return (new * (top * lax.rsqrt(jnp.sum(new * new, axis=0, keepdims=True) + 1e-06))).astype(BF)

        old_sq = old_sq + jnp.sum(w2j * w2j, axis=0, keepdims=True)
        new_sq = new_sq + jnp.sum(u2 * u2, axis=0, keepdims=True)
        qa, qc = dot(q[...], normed(w1j, u1)), dot(q[...], normed(w3j, u3))
        part = dot((qa * jax.nn.sigmoid(qa) * qc).astype(BF), u2.astype(BF))
        hp[...] = part if j == 0 else hp[...] + part
    wide = half(dh)
    me = lax.axis_index("rep")
    mine = pl.ds(pl.multiple_of(me * wide, wide), wide)
    other = pl.ds(pl.multiple_of((1 - me) * wide, wide), wide)
    n = q.shape[0]
    own_out[...] = hp[:, mine]
    send[:n, :] = hp[:, other].astype(BF)
    row = lax.broadcasted_iota(jnp.int32, (8, dh), 0)
    hp[:8, :] = jnp.where(row == 0, old_sq, jnp.where(row == 1, new_sq, 0.0))
    own_sq[...] = hp[:8, mine]
    sq = hp[:8, other]
    top = sq.astype(BF).astype(F32)
    send[n:, :] = jnp.concatenate([top, sq - top], axis=0).astype(BF)


def mix_kernel(own, own_sq, got, stream, mixed, mixed_low):
    n, wide = own.shape
    mine = pl.ds(pl.multiple_of(lax.axis_index("rep") * wide, wide), wide)
    tail = got[n:, :].astype(F32)
    sq = own_sq[...] + tail[:8] + tail[8:]
    scale = jnp.sqrt(sq[0:1]) * lax.rsqrt(sq[1:2] + 1e-06)
    y = stream[:, mine].astype(F32) + (own[...] + got[:n, :].astype(F32)) * scale
    mixed[...] = y
    mixed_low[...] = y.astype(BF)


def take(parts, step):
    if len(parts) == 1:
        return parts[0][...]
    me, n = lax.axis_index("tok"), lax.axis_size("tok")
    direct = me >= step if step == 1 else me < step
    return jnp.where(direct, parts[0][...], parts[1][...])


def split(refs, counts):
    out = []
    for c in counts:
        out.append(refs[:c])
        refs = refs[c:]
    return out, refs


def up_kernel(places, counts, *refs):
    pieces, refs = refs[: len(places)], refs[len(places) :]
    n_head = lax.axis_size("head")
    gains, refs = refs[:n_head], refs[n_head:]
    blocks, (out, zs) = split(refs, counts)
    me_h, me_r, me_t = lax.axis_index("head"), lax.axis_index("rep"), lax.axis_index("tok")
    n, wide = pieces[0].shape
    groups = lax.axis_size("groups")
    width = zs.shape[1]
    for dg in range(groups):
        here = [(p, dh, dr) for p, (g, dh, dr) in zip(pieces, places) if g == dg]
        total = jnp.zeros((n, 1), F32)
        for p, _, _ in here:
            x = p[...].astype(F32)
            total = total + jnp.sum(x * x, axis=1, keepdims=True)
        inv = lax.rsqrt(total / width + 1e-06)
        for p, dh, dr in here:
            r = lax.rem(me_r + dr, 2)
            head = lax.rem(me_h + dh, n_head)
            cols = pl.ds(pl.multiple_of(head * 2 * wide + r * wide, wide), wide)
            gain = gains[dh][:, pl.ds(pl.multiple_of(r * wide, wide), wide)]
            zs[dg * n : (dg + 1) * n, cols] = (p[...].astype(F32) * inv * gain).astype(BF)
    total = None
    for s, parts in enumerate(blocks):
        deep = parts[0].shape[0]
        if len(blocks) == 1:
            z = zs[...]
        else:
            z = zs[:, pl.ds(pl.multiple_of(lax.rem(me_t + len(blocks) - s, len(blocks)) * deep, deep), deep)]
        term = dot(z, take(parts, s))
        total = term if total is None else total + term
    out[...] = (0.5 * total * (1.0 + lax.erf(total * np.float32(0.5**0.5)))).astype(BF)


def down_kernel(counts, h, *refs):
    blocks, (own, send, os) = split(refs, counts)
    me_h, me_r, me_t = lax.axis_index("head"), lax.axis_index("rep"), lax.axis_index("tok")
    n_head = lax.axis_size("head")
    for s, parts in enumerate(blocks):
        wide = parts[0].shape[1]
        term = dot(h[...], take(parts, s))
        if len(blocks) == 1:
            os[...] = term
        else:
            os[:, pl.ds(pl.multiple_of(lax.rem(me_t + len(blocks) - s, len(blocks)) * wide, wide), wide)] = term
    wide = own.shape[1] // n_head
    for dh in range(n_head):
        at = lax.rem(me_h + dh, n_head) * 2 * wide
        there = slice(dh * wide, (dh + 1) * wide)
        own[:, there] = os[:, pl.ds(pl.multiple_of(at + me_r * wide, wide), wide)]
        send[:, there] = os[:, pl.ds(pl.multiple_of(at + (1 - me_r) * wide, wide), wide)].astype(BF)


def pair_kernel(own, got, mixed, *outs):
    n, wide = mixed.shape
    n_head = lax.axis_size("head")
    for i, out in enumerate(outs):
        dg, dh = divmod(i, n_head)
        rows, cols = slice(dg * n, (dg + 1) * n), slice(dh * wide, (dh + 1) * wide)
        total = own[rows, cols] + got[rows, cols].astype(F32)
        out[...] = mixed[...] + total if i == 0 else total.astype(BF)


def spread(x):
    def along(y, pairs):
        return lax.ppermute(y, "tok", pairs)

    up = along(x, [(0, 1), (1, 2), (2, 3)])
    down = along(x, [(1, 0), (2, 1), (3, 2)])
    far = along(x, [(0, 2), (1, 3), (2, 0), (3, 1)])
    last = along(far, [(2, 3), (1, 0)])
    return [[x], [up, last], [far], [down, last]]


def on_device(
    keys, values, rates, queries, stream, gain, counts, fw_one, fw_three, fw_two, mlp_up, mlp_down
):
    n_tok, n_head = lax.axis_size("tok"), lax.axis_size("head")
    groups, reps = lax.axis_size("groups"), lax.axis_size("rep")
    me_g, me_r = lax.axis_index("groups"), lax.axis_index("rep")
    dh, n_key, n = keys.shape[1], keys.shape[0], queries.shape[0]
    wide = dh // reps
    scaled = (rates * values.astype(F32)).astype(BF)
    pair = jnp.concatenate([keys, scaled], axis=1)
    units = mlp_up.shape[1] // groups
    up_own = lax.dynamic_slice_in_dim(mlp_up, me_g * units, units, 1)
    down_own = lax.dynamic_slice_in_dim(mlp_down, me_g * units, units, 0)
    if n_tok == 4:
        piece = lax.dynamic_slice_in_dim(pair, me_r * (n_key // reps), n_key // reps, 0)
        near = [shifted(piece, ("tok",), (s,)) for s in range(1, n_tok)]
        near, up_own, down_own, gain = lax.optimization_barrier((near, up_own, down_own, gain))
        tokens = [pair, *near, *[shifted(x, ("rep",), (1,)) for x in near]]
        up_blocks, down_blocks = spread(up_own), spread(down_own)
    else:
        tokens = [lax.all_gather(pair, "tok", axis=0, tiled=True)]
        up_blocks = [[lax.all_gather(up_own, "tok", axis=0, tiled=True)]]
        down_blocks = [[lax.all_gather(down_own, "tok", axis=1, tiled=True)]]
    gain = gain[None, :]
    gains = [gain] + [shifted(gain, ("head",), (s,)) for s in range(1, n_head)]

    n_all = sum(x.shape[0] for x in tokens)
    hidden = fw_one.shape[2]
    own, own_sq, send = call(
        functools.partial(fast_kernel, len(tokens)),
        [shape((n, wide), F32), shape((8, wide), F32), shape((n + 16, wide), BF)],
        [*tokens, fw_one[0], fw_three[0], fw_two[0], queries],
        [pltpu.VMEM((n_all, dh), BF), pltpu.VMEM((n_all, dh), BF), pltpu.VMEM((n, dh), F32)],
        flops=12 * n_all * dh * hidden + 6 * n * dh * hidden,
    )
    got = shifted(send, ("rep",), (1,))
    mixed, low = call(
        mix_kernel, [shape((n, wide), F32), shape((n, wide), BF)], [own, own_sq, got, stream]
    )
    moves = [(dg, h) for dg in range(groups) for h in range(n_head)]
    across = {m: low if m == (0, 0) else shifted(low, ("groups", "head"), m) for m in moves}
    pieces, places = [], []
    for m, x in across.items():
        pieces += [x, shifted(x, ("rep",), (1,))]
        places += [(*m, 0), (*m, 1)]
    up_counts, down_counts = [len(b) for b in up_blocks], [len(b) for b in down_blocks]
    rows, model = groups * n, n_head * dh
    (act,) = call(
        functools.partial(up_kernel, places, up_counts),
        [shape((rows, units), BF)],
        [*pieces, *gains, *[x for b in up_blocks for x in b]],
        [pltpu.VMEM((rows, model), BF)],
        flops=2 * rows * units * model,
    )
    own, send = call(
        functools.partial(down_kernel, down_counts),
        [shape((rows, n_head * wide), F32), shape((rows, n_head * wide), BF)],
        [act, *[x for b in down_blocks for x in b]],
        [pltpu.VMEM((rows, model), F32)],
        flops=2 * rows * units * model,
    )
    got = shifted(send, ("rep",), (1,))
    total, *parts = call(
        pair_kernel,
        [shape((n, wide), F32 if m == (0, 0) else BF) for m in moves],
        [own, got, mixed],
    )
    for m, x in zip(moves[1:], parts):
        back = (groups - m[0], n_head - m[1])
        total = total + shifted(x, ("groups", "head"), back).astype(F32)
    live = jnp.arange(n, dtype=jnp.int32) < counts[0]
    return jnp.where(live[:, None], total, 0.0).astype(BF)


def solution(mesh):
    placed = (
        P(("groups", "tok"), "head"),
        P(("groups", "tok"), "head"),
        P(("groups", "tok"), "head"),
        P(("groups", "tok"), "head"),
        P(("groups", "tok"), "head"),
        P("head"),
        P(("groups", "tok")),
        P("head", None, "rep"),
        P("head", None, "rep"),
        P("head", "rep", None),
        P("tok", ("head", "rep")),
        P(("head", "rep"), "tok"),
    )
    return jax.shard_map(
        on_device,
        mesh=mesh,
        in_specs=placed,
        out_specs=P(("groups", "tok"), ("head", "rep")),
        check_vma=False,
    )
```

```python
import functools

import jax
import jax.numpy as jnp
import numpy as np
from jax import lax
from jax.experimental import pallas as pl
from jax.experimental.pallas import tpu as pltpu
from jax.sharding import PartitionSpec as P

BF, F32 = jnp.bfloat16, jnp.float32


def dot(a, b, dims=((1,), (0,))):
    return lax.dot_general(a, b, (dims, ((), ())), preferred_element_type=F32)


def shifted(x, axes, shifts):
    sizes = [lax.axis_size(a) for a in axes]
    pairs = []
    for here in range(int(np.prod(sizes))):
        at = np.unravel_index(here, sizes)
        there = [(a + s) % n for a, s, n in zip(at, shifts, sizes)]
        pairs.append((int(np.ravel_multi_index(there, sizes)), here))
    return lax.ppermute(x, axes, pairs)


def call(kernel, outs, args, scratch=(), flops=0, far=()):
    moved = sum(int(np.prod(x.shape)) * x.dtype.itemsize for x in (*args, *outs))
    kept = sum(int(np.prod(x.shape)) * 4 for x in scratch if x.dtype in (BF, F32))
    return pl.pallas_call(
        kernel,
        out_shape=outs,
        in_specs=[pl.BlockSpec(memory_space=pltpu.HBM if i in far else pltpu.VMEM) for i in range(len(args))],
        out_specs=[pl.BlockSpec(memory_space=pltpu.VMEM)] * len(outs),
        scratch_shapes=list(scratch),
        compiler_params=pltpu.CompilerParams(vmem_limit_bytes=moved + kept + (10 << 20)),
        cost_estimate=pl.CostEstimate(flops=flops, bytes_accessed=moved, transcendentals=0),
    )(*args)


def shape(dims, dtype):
    return jax.ShapeDtypeStruct(dims, dtype)


def half(ref_width):
    return ref_width // lax.axis_size("rep")


def pair_up_kernel(keys, values, rates, pair, *message):
    n, dh = keys.shape
    rate = jnp.broadcast_to(rates[...], (128, n)).T
    pair[:, :dh] = keys[...]
    for c in range(0, dh, 128):
        pair[:, dh + c : dh + c + 128] = (values[:, c : c + 128].astype(F32) * rate).astype(BF)
    for m in message:
        rows = m.shape[0]
        m[...] = pair[pl.ds(pl.multiple_of(lax.axis_index("rep") * rows, rows), rows), :]


def fast_kernel(n_pieces, *refs):
    pieces, refs = refs[:n_pieces], refs[n_pieces:]
    w1, w3, w2_far, q, own_out, own_sq, send, ks, es, hp, w2, sem = refs
    fetch = pltpu.make_async_copy(w2_far, w2, sem)
    fetch.start()
    dh, hidden = w1.shape
    at = 0
    for p in pieces:
        n = p.shape[0]
        ks[at : at + n, :] = p[:, :dh]
        es[at : at + n, :] = p[:, dh:]
        at += n
    tokens, step, block = at, min(at, 512), min(hidden, 256)
    fetch.wait()
    old_sq = jnp.zeros((1, dh), F32)
    new_sq = jnp.zeros((1, dh), F32)
    for j in range(0, hidden, block):
        w1j, w3j, w2j = w1[:, j : j + block], w3[:, j : j + block], w2[j : j + block, :]
        w1b, w3b, w2b = w1j.astype(BF), w3j.astype(BF), w2j.astype(BF)

        def grads(i, sums):
            rows = pl.ds(pl.multiple_of(i * step, step), step)
            k, e = ks[rows, :], es[rows, :]
            a1, a3, b = dot(k, w1b), dot(k, w3b), dot(e, w2b, ((1,), (1,)))
            sig = jax.nn.sigmoid(a1)
            act = a1 * sig
            g = (act * a3).astype(BF)
            r1 = (b * a3 * (sig * (1.0 + a1 * (1.0 - sig)))).astype(BF)
            r3 = (b * act).astype(BF)
            first = ((0,), (0,))
            return sums[0] + dot(k, r1, first), sums[1] + dot(k, r3, first), sums[2] + dot(g, e, first)

        sums = (w1j, w3j, w2j)
        if tokens == step:
            u1, u3, u2 = grads(0, sums)
        else:
            u1, u3, u2 = lax.fori_loop(0, tokens // step, grads, sums)

        def normed(old, new):
            top = jnp.sqrt(jnp.sum(old * old, axis=0, keepdims=True))
            return (new * (top * lax.rsqrt(jnp.sum(new * new, axis=0, keepdims=True) + 1e-06))).astype(BF)

        old_sq = old_sq + jnp.sum(w2j * w2j, axis=0, keepdims=True)
        new_sq = new_sq + jnp.sum(u2 * u2, axis=0, keepdims=True)
        qa, qc = dot(q[...], normed(w1j, u1)), dot(q[...], normed(w3j, u3))
        part = dot((qa * jax.nn.sigmoid(qa) * qc).astype(BF), u2.astype(BF))
        hp[...] = part if j == 0 else hp[...] + part
    wide = half(dh)
    me = lax.axis_index("rep")
    mine = pl.ds(pl.multiple_of(me * wide, wide), wide)
    other = pl.ds(pl.multiple_of((1 - me) * wide, wide), wide)
    n = q.shape[0]
    own_out[...] = hp[:, mine]
    send[:n, :] = hp[:, other].astype(BF)
    row = lax.broadcasted_iota(jnp.int32, (8, dh), 0)
    hp[:8, :] = jnp.where(row == 0, old_sq, jnp.where(row == 1, new_sq, 0.0))
    own_sq[...] = hp[:8, mine]
    sq = hp[:8, other]
    top = sq.astype(BF).astype(F32)
    send[n:, :] = jnp.concatenate([top, sq - top], axis=0).astype(BF)


def mix_kernel(own, own_sq, got, stream, mixed, mixed_low):
    n, wide = own.shape
    mine = pl.ds(pl.multiple_of(lax.axis_index("rep") * wide, wide), wide)
    tail = got[n:, :].astype(F32)
    sq = own_sq[...] + tail[:8] + tail[8:]
    scale = jnp.sqrt(sq[0:1]) * lax.rsqrt(sq[1:2] + 1e-06)
    y = stream[:, mine].astype(F32) + (own[...] + got[:n, :].astype(F32)) * scale
    mixed[...] = y
    mixed_low[...] = y.astype(BF)


def take(parts, rows=None):
    x = [p[...] if rows is None else p[rows, :] for p in parts]
    return x[0] if len(x) == 1 else jnp.where(inner(), *x)


def inner():
    me = lax.axis_index("tok")
    return jnp.logical_and(me > 0, me < lax.axis_size("tok") - 1)


def split(refs, counts):
    out = []
    for c in counts:
        out.append(refs[:c])
        refs = refs[c:]
    return out, refs


def up_kernel(places, counts, *refs):
    pieces, refs = refs[: len(places)], refs[len(places) :]
    n_head = lax.axis_size("head")
    gains, refs = refs[:n_head], refs[n_head:]
    blocks, (out, zs) = split(refs, counts)
    me_h, me_r, me_t = lax.axis_index("head"), lax.axis_index("rep"), lax.axis_index("tok")
    n, wide = pieces[0].shape
    groups = lax.axis_size("groups")
    width = zs.shape[1]
    for dg in range(groups):
        here = [(p, dh, dr) for p, (g, dh, dr) in zip(pieces, places) if g == dg]
        total = jnp.zeros((n, 1), F32)
        for p, _, _ in here:
            x = p[...].astype(F32)
            total = total + jnp.sum(x * x, axis=1, keepdims=True)
        inv = lax.rsqrt(total / width + 1e-06)
        for p, dh, dr in here:
            r = lax.rem(me_r + dr, 2)
            head = lax.rem(me_h + dh, n_head)
            cols = pl.ds(pl.multiple_of(head * 2 * wide + r * wide, wide), wide)
            gain = gains[dh][:, pl.ds(pl.multiple_of(r * wide, wide), wide)]
            zs[dg * n : (dg + 1) * n, cols] = (p[...].astype(F32) * inv * gain).astype(BF)
    total = None
    for s, parts in enumerate(blocks):
        if len(blocks) == 1:
            term = dot(zs[...], take(parts))
        else:
            deep = width // len(blocks)
            z = zs[:, pl.ds(pl.multiple_of(lax.bitwise_xor(me_t, s) * deep, deep), deep)]
            term = dot(z, take(parts, slice(0, deep)))
        total = term if total is None else total + term
    out[...] = (0.5 * total * (1.0 + lax.erf(total * np.float32(0.5**0.5)))).astype(BF)


def down_kernel(counts, h, *refs):
    blocks, (own, send, os) = split(refs, counts)
    me_h, me_r, me_t = lax.axis_index("head"), lax.axis_index("rep"), lax.axis_index("tok")
    n_head = lax.axis_size("head")
    for s, parts in enumerate(blocks):
        if len(blocks) == 1:
            os[...] = dot(h[...], take(parts))
        else:
            wide = os.shape[1] // len(blocks)
            x = take(parts, slice(wide, parts[0].shape[0]))
            term = None
            for at in range(0, h.shape[1], wide):
                part = dot(h[:, at : at + wide], x[:, at : at + wide])
                term = part if term is None else term + part
            os[:, pl.ds(pl.multiple_of(lax.bitwise_xor(me_t, s) * wide, wide), wide)] = term
    wide = own.shape[1] // n_head
    for dh in range(n_head):
        at = lax.rem(me_h + dh, n_head) * 2 * wide
        there = slice(dh * wide, (dh + 1) * wide)
        own[:, there] = os[:, pl.ds(pl.multiple_of(at + me_r * wide, wide), wide)]
        send[:, there] = os[:, pl.ds(pl.multiple_of(at + (1 - me_r) * wide, wide), wide)].astype(BF)


def pair_kernel(own, got, mixed, *outs):
    n, wide = mixed.shape
    n_head = lax.axis_size("head")
    for i, out in enumerate(outs):
        dg, dh = divmod(i, n_head)
        rows, cols = slice(dg * n, (dg + 1) * n), slice(dh * wide, (dh + 1) * wide)
        total = own[rows, cols] + got[rows, cols].astype(F32)
        out[...] = mixed[...] + total if i == 0 else total.astype(BF)


def along(x, pairs):
    return lax.ppermute(x, "tok", pairs)


def first_phase(x):
    return along(x, [(0, 1), (1, 0), (2, 3), (3, 2)]), along(x, [(0, 2), (2, 0), (1, 3), (3, 1)])


def second_phase(x, far):
    return along(x, [(1, 2), (2, 1)]), along(far, [(1, 0), (2, 3)])


def on_device(
    keys, values, rates, queries, stream, gain, counts, fw_one, fw_three, fw_two, mlp_up, mlp_down
):
    n_tok, n_head = lax.axis_size("tok"), lax.axis_size("head")
    groups, reps = lax.axis_size("groups"), lax.axis_size("rep")
    me_g, me_r = lax.axis_index("groups"), lax.axis_index("rep")
    dh, n_key, n = keys.shape[1], keys.shape[0], queries.shape[0]
    wide = dh // reps
    units = mlp_up.shape[1] // groups
    up_own = lax.dynamic_slice_in_dim(mlp_up, me_g * units, units, 1)
    down_own = lax.dynamic_slice_in_dim(mlp_down, me_g * units, units, 0)
    share = [shape((n_key // reps, 2 * dh), BF)] if n_tok == 4 else []
    pair, *message = call(
        pair_up_kernel, [shape((n_key, 2 * dh), BF), *share], [keys, values, rates.reshape(1, n_key)]
    )
    gain = gain[None, :]
    if n_tok == 4:
        flip = functools.partial(shifted, axes=("rep",), shifts=(1,))
        near, far = first_phase(message[0])
        wide_down = down_own.shape[1]
        low_rows = [down_own[i : i + wide_down] for i in range(0, units, wide_down)]
        packed = jnp.concatenate([up_own, jnp.concatenate(low_rows, axis=1)], axis=0)
        near, far, own, gain, packed = lax.optimization_barrier((near, far, message[0], gain, packed))
        middle, end = second_phase(own, far)
        w_near, w_far = first_phase(packed)
        gains = [gain] + [shifted(gain, ("head",), (s,)) for s in range(1, n_head)]
        late = jnp.where(inner(), middle, end)
        tokens = [pair, near, far, late, flip(near), flip(far), flip(late)]
        tokens, gains = lax.optimization_barrier((tokens, gains))
    else:
        tokens = [lax.all_gather(pair, "tok", axis=0, tiled=True)]
        up_blocks = [[lax.all_gather(up_own, "tok", axis=0, tiled=True)]]
        down_blocks = [[lax.all_gather(down_own, "tok", axis=1, tiled=True)]]
        gains = [gain] + [shifted(gain, ("head",), (s,)) for s in range(1, n_head)]

    n_all = sum(x.shape[0] for x in tokens)
    hidden = fw_one.shape[2]
    own, own_sq, send = call(
        functools.partial(fast_kernel, len(tokens)),
        [shape((n, wide), F32), shape((8, wide), F32), shape((n + 16, wide), BF)],
        [*tokens, fw_one[0], fw_three[0], fw_two[0], queries],
        [
            pltpu.VMEM((n_all, dh), BF),
            pltpu.VMEM((n_all, dh), BF),
            pltpu.VMEM((n, dh), F32),
            pltpu.VMEM((hidden, dh), F32),
            pltpu.SemaphoreType.DMA,
        ],
        flops=12 * n_all * dh * hidden + 6 * n * dh * hidden,
        far=(len(tokens) + 2,),
    )
    got = shifted(send, ("rep",), (1,))
    mixed, low = call(
        mix_kernel, [shape((n, wide), F32), shape((n, wide), BF)], [own, own_sq, got, stream]
    )
    moves = [(dg, h) for dg in range(groups) for h in range(n_head)]
    across = {m: low if m == (0, 0) else shifted(low, ("groups", "head"), m) for m in moves}
    if n_tok == 4:
        w_own, w_there, w_near, _ = lax.optimization_barrier((packed, w_far, w_near, list(across.values())))
        up_blocks = down_blocks = [[packed], [w_near], [w_far], list(second_phase(w_own, w_there))]
    pieces, places = [], []
    for m, x in across.items():
        pieces += [x, shifted(x, ("rep",), (1,))]
        places += [(*m, 0), (*m, 1)]
    up_counts, down_counts = [len(b) for b in up_blocks], [len(b) for b in down_blocks]
    rows, model = groups * n, n_head * dh
    (act,) = call(
        functools.partial(up_kernel, places, up_counts),
        [shape((rows, units), BF)],
        [*pieces, *gains, *[x for b in up_blocks for x in b]],
        [pltpu.VMEM((rows, model), BF)],
        flops=2 * rows * units * model,
    )
    own, send = call(
        functools.partial(down_kernel, down_counts),
        [shape((rows, n_head * wide), F32), shape((rows, n_head * wide), BF)],
        [act, *[x for b in down_blocks for x in b]],
        [pltpu.VMEM((rows, model), F32)],
        flops=2 * rows * units * model,
    )
    got = shifted(send, ("rep",), (1,))
    total, *parts = call(
        pair_kernel,
        [shape((n, wide), F32 if m == (0, 0) else BF) for m in moves],
        [own, got, mixed],
    )
    for m, x in zip(moves[1:], parts):
        back = (groups - m[0], n_head - m[1])
        total = total + shifted(x, ("groups", "head"), back).astype(F32)
    live = jnp.arange(n, dtype=jnp.int32) < counts[0]
    return jnp.where(live[:, None], total, 0.0).astype(BF)


def solution(mesh):
    placed = (
        P(("groups", "tok"), "head"),
        P(("groups", "tok"), "head"),
        P(("groups", "tok"), "head"),
        P(("groups", "tok"), "head"),
        P(("groups", "tok"), "head"),
        P("head"),
        P(("groups", "tok")),
        P("head", None, "rep"),
        P("head", None, "rep"),
        P("head", "rep", None),
        P("tok", ("head", "rep")),
        P(("head", "rep"), "tok"),
    )
    return jax.shard_map(
        on_device,
        mesh=mesh,
        in_specs=placed,
        out_specs=P(("groups", "tok"), ("head", "rep")),
        check_vma=False,
    )
```

```python
import functools
import itertools

import jax
import jax.numpy as jnp
import numpy as np
from jax import lax
from jax.experimental import pallas as pl
from jax.experimental.pallas import tpu as pltpu
from jax.sharding import PartitionSpec as P

BF, F32 = jnp.bfloat16, jnp.float32


def dot(a, b, dims=((1,), (0,))):
    return lax.dot_general(a, b, (dims, ((), ())), preferred_element_type=F32)


def moved(x, groups=0, tok=0, head=0, rep=0):
    shifts = {"groups": groups, "tok": tok, "head": head, "rep": rep}
    axes = [a for a, s in shifts.items() if s]
    if not axes:
        return x
    sizes = [lax.axis_size(a) for a in axes]
    pairs = []
    for here in range(int(np.prod(sizes))):
        at = np.unravel_index(here, sizes)
        there = [i ^ tok if a == "tok" else (i + shifts[a]) % n for a, i, n in zip(axes, at, sizes)]
        pairs.append((int(np.ravel_multi_index(there, sizes)), here))
    return lax.ppermute(x, tuple(axes), pairs)


def shape(dims, dtype):
    return jax.ShapeDtypeStruct(dims, dtype)


def call(kernel, outs, args, scratch=(), flops=0):
    touched = sum(int(np.prod(x.shape)) * x.dtype.itemsize for x in (*args, *outs))
    kept = sum(int(np.prod(x.shape)) * 4 for x in scratch)
    return pl.pallas_call(
        kernel,
        out_shape=outs,
        in_specs=[pl.BlockSpec(memory_space=pltpu.VMEM)] * len(args),
        out_specs=[pl.BlockSpec(memory_space=pltpu.VMEM)] * len(outs),
        scratch_shapes=list(scratch),
        compiler_params=pltpu.CompilerParams(vmem_limit_bytes=touched + kept + (10 << 20)),
        cost_estimate=pl.CostEstimate(flops=1, bytes_accessed=1, transcendentals=0),
    )(*args)


def window(index, size):
    return pl.ds(pl.multiple_of(index * size, size), size)


def message_kernel(keys, values, rates, queries, stream, pair, *messages):
    n, dh = keys.shape
    me = lax.axis_index("rep")
    rate = jnp.broadcast_to(rates[...], (128, n)).T
    pair[:, :dh] = keys[...]
    for c in range(0, dh, 128):
        pair[:, dh + c : dh + c + 128] = (values[:, c : c + 128].astype(F32) * rate).astype(BF)
    if messages:
        share, ask = messages
        share[...] = pair[window(me, share.shape[0]), :]
        ask[:, :dh] = queries[...]
        ask[:, dh:] = stream[:, window(me, ask.shape[1] - dh)]


def pack_kernel(up, down, same, other):
    deep, wide = up.shape[0], same.shape[1]
    bit = lax.bitwise_and(lax.axis_index("tok"), 1)
    for out, b in ((same, bit), (other, 1 - bit)):
        part = window(lax.axis_index("groups") * 2 + b, wide)
        out[:deep, :] = up[:, part]
        out[deep:, :] = down[part, :]


def gradients(k, e, w1b, w3b, w2b):
    a1, a3, b = dot(k, w1b), dot(k, w3b), dot(e, w2b, ((1,), (1,)))
    sig = jax.nn.sigmoid(a1)
    act = a1 * sig
    g = (act * a3).astype(BF)
    r1 = (b * a3 * (sig * (1.0 + a1 * (1.0 - sig)))).astype(BF)
    r3 = (b * act).astype(BF)
    first = ((0,), (0,))
    return dot(k, r1, first), dot(k, r3, first), dot(g, e, first)


def squares(x):
    return jnp.sum(x * x, axis=0, keepdims=True)


def own_kernel(take_own, pair, w1, w3, w2, b1, b3, b2, u1, u3, u2, sq13, sq2):
    dh, hidden = w1.shape
    block = min(hidden, 256)
    sq2[...] = jnp.broadcast_to(squares(w2[...]), sq2.shape)
    for j in range(0, hidden, block):
        js = slice(j, j + block)
        x1, x3, x2 = w1[:, js], w3[:, js], w2[js, :]
        b1[:, js], b3[:, js], b2[js, :] = x1.astype(BF), x3.astype(BF), x2.astype(BF)
        sq13[0:8, js] = jnp.broadcast_to(squares(x1), (8, block))
        sq13[8:16, js] = jnp.broadcast_to(squares(x3), (8, block))
        if take_own:
            d1, d3, d2 = gradients(pair[:, :dh], pair[:, dh:], b1[:, js], b3[:, js], b2[js, :])
            x1, x3, x2 = x1 + d1, x3 + d3, x2 + d2
        u1[:, js], u3[:, js], u2[js, :] = x1, x3, x2


def fast_kernel(n_pieces, n_ask, *refs):
    pieces, refs = refs[:n_pieces], refs[n_pieces:]
    asks, refs = refs[:n_ask], refs[n_ask:]
    b1, b3, b2, u1, u3, u2, sq13, sq2, own_out, own_sq, send, ks, es, hp = refs
    dh, hidden = b1.shape
    at = 0
    for p in pieces:
        n = p.shape[0]
        ks[at : at + n, :] = p[:, :dh]
        es[at : at + n, :] = p[:, dh:]
        at += n
    tokens, step, block = at, min(at, 512), min(hidden, 256)
    asked = [q[:, :dh] for q in asks]
    asked = asked[0] if n_ask == 1 else jnp.concatenate(asked, axis=0)
    new_sq = jnp.zeros((1, dh), F32)
    for j in range(0, hidden, block):
        js = slice(j, j + block)

        def add(i, sums):
            rows = pl.ds(pl.multiple_of(i * step, step), step)
            parts = gradients(ks[rows, :], es[rows, :], b1[:, js], b3[:, js], b2[js, :])
            return tuple(s + p for s, p in zip(sums, parts))

        sums = (u1[:, js], u3[:, js], u2[js, :])
        sums = add(0, sums) if tokens == step else lax.fori_loop(0, tokens // step, add, sums)

        def normed(old_sq, new):
            return (new * (jnp.sqrt(old_sq) * lax.rsqrt(squares(new) + 1e-06))).astype(BF)

        new_sq = new_sq + squares(sums[2])
        qa = dot(asked, normed(sq13[0:1, js], sums[0]))
        qc = dot(asked, normed(sq13[8:9, js], sums[1]))
        part = dot((qa * jax.nn.sigmoid(qa) * qc).astype(BF), sums[2].astype(BF))
        hp[...] = part if j == 0 else hp[...] + part
    me, wide = lax.axis_index("rep"), own_out.shape[1]
    n = own_out.shape[0]
    own_out[...] = hp[:, window(me, wide)]
    send[:n, :] = hp[:, window(1 - me, wide)].astype(BF)
    row = lax.broadcasted_iota(jnp.int32, (8, dh), 0)
    hp[:8, :] = jnp.where(row == 0, sq2[...], jnp.where(row == 1, new_sq, 0.0))
    own_sq[...] = hp[:8, window(me, wide)]
    sq = hp[:8, window(1 - me, wide)]
    top = sq.astype(BF).astype(F32)
    send[n:, :] = jnp.concatenate([top, sq - top], axis=0).astype(BF)


def mix_kernel(own, own_sq, got, stream, gain, *refs):
    *asks, mixed, low = refs
    n, wide = mixed.shape
    rows = own.shape[0]
    tail = got[rows:, :].astype(F32)
    sq = own_sq[...] + tail[:8] + tail[8:]
    scale = jnp.sqrt(sq[0:1]) * lax.rsqrt(sq[1:2] + 1e-06)
    for z in range(rows // n):
        part = slice(z * n, (z + 1) * n)
        base = stream[:, window(lax.axis_index("rep"), wide)] if z == 0 else asks[0][:, asks[0].shape[1] - wide :]
        y = base.astype(F32) + (own[part, :] + got[part, :].astype(F32)) * scale
        low[part, :] = y.astype(BF)
        if z == 0:
            mixed[...] = y
    g = jnp.broadcast_to(gain[:, window(lax.axis_index("rep"), wide)], (16, wide))
    row = lax.broadcasted_iota(jnp.int32, (16, wide), 0)
    top = g.astype(BF).astype(F32)
    mid = (g - top).astype(BF).astype(F32)
    low[rows:, :] = jnp.where(row == 0, top, jnp.where(row == 1, mid, jnp.where(row == 2, g - top - mid, 0.0))).astype(BF)


def up_kernel(places, n_blocks, *refs):
    pieces, refs = refs[: len(places)], refs[len(places) :]
    n_head = lax.axis_size("head")
    blocks, (out, zs) = refs[:n_blocks], refs[n_blocks:]
    me_h, me_r, me_t = lax.axis_index("head"), lax.axis_index("rep"), lax.axis_index("tok")
    n, wide = pieces[0].shape[0] - 16, pieces[0].shape[1]
    width = zs.shape[1]
    for dg in range(lax.axis_size("groups")):
        here = [(p, dh, dr) for p, (g, dh, dr) in zip(pieces, places) if g == dg]
        total = jnp.zeros((n, 1), F32)
        for p, _, _ in here:
            x = p[:n, :].astype(F32)
            total = total + jnp.sum(x * x, axis=1, keepdims=True)
        inv = lax.rsqrt(total / width + 1e-06)
        for p, dh, dr in here:
            r = lax.rem(me_r + dr, 2)
            head = lax.rem(me_h + dh, n_head)
            gain = jnp.sum(p[n:, :].astype(F32), axis=0, keepdims=True)
            zs[dg * n : (dg + 1) * n, window(head * 2 + r, wide)] = (p[:n, :].astype(F32) * inv * gain).astype(BF)
    total = None
    deep = width // n_blocks
    for s, x in enumerate(blocks):
        z = zs[...] if n_blocks == 1 else zs[:, window(lax.bitwise_xor(me_t, s), deep)]
        term = dot(z, x[:deep, :])
        total = term if total is None else total + term
    out[...] = (0.5 * total * (1.0 + lax.erf(total * np.float32(0.5**0.5)))).astype(BF)


def down_kernel(n_blocks, h, *refs):
    blocks, (own, send, os) = refs[:n_blocks], refs[n_blocks:]
    me_h, me_r, me_t = lax.axis_index("head"), lax.axis_index("rep"), lax.axis_index("tok")
    n_head = lax.axis_size("head")
    units = h.shape[1]
    for s, x in enumerate(blocks):
        term = dot(h[...], x[x.shape[0] - units :, :])
        if n_blocks == 1:
            os[...] = term
        else:
            os[:, window(lax.bitwise_xor(me_t, s), term.shape[1])] = term
    wide = own.shape[1] // n_head
    for dh in range(n_head):
        at = lax.rem(me_h + dh, n_head) * 2
        there = slice(dh * wide, (dh + 1) * wide)
        own[:, there] = os[:, window(at + me_r, wide)]
        send[:, there] = os[:, window(at + 1 - me_r, wide)].astype(BF)


def pair_kernel(moves, near, own, got, mixed, *outs):
    n, wide = mixed.shape
    for (dg, dz, dh), out in zip(moves, outs):
        at = (dg * near + dz) * n
        rows, cols = slice(at, at + n), slice(dh * wide, (dh + 1) * wide)
        total = own[rows, cols] + got[rows, cols].astype(F32)
        out[...] = mixed[...] + total if (dg, dz, dh) == (0, 0, 0) else total.astype(BF)


def on_device(
    keys, values, rates, queries, stream, gain, counts, fw_one, fw_three, fw_two, mlp_up, mlp_down
):
    n_tok, n_head = lax.axis_size("tok"), lax.axis_size("head")
    groups, reps = lax.axis_size("groups"), lax.axis_size("rep")
    dh, n_key, n = keys.shape[1], keys.shape[0], queries.shape[0]
    hidden = fw_one.shape[2]
    wide = dh // reps
    paired = n_tok == 4
    near = 2 if paired else 1
    units = mlp_up.shape[1] // groups // near
    barrier = lax.optimization_barrier

    messages = [shape((n_key // reps, 2 * dh), BF), shape((n, dh + wide), BF)] if paired else []
    pair, *messages = call(
        message_kernel,
        [shape((n_key, 2 * dh), BF), *messages],
        [keys, values, rates.reshape(1, n_key), queries, stream],
    )
    asks = []
    if paired:
        share, ask = messages
        others = [moved(share, tok=s) for s in (1, 2, 3)]
        same, other = call(
            pack_kernel, [shape((mlp_up.shape[0] + units, units), BF)] * 2, [mlp_up, mlp_down]
        )
        first, ask, other_1 = barrier((others[0], ask, other))
        asks = [moved(ask, tok=1)]
        w_first = moved(other_1, tok=1)
        far, same_2 = barrier((others[1:], same))
        w_second = moved(same_2, tok=2)
        w_third = moved(barrier((other, w_second))[0], tok=3)
        tokens = [first, *far]
        tokens = tokens + [moved(x, rep=1) for x in tokens]
    else:
        me_g = lax.axis_index("groups")
        up_own = lax.dynamic_slice_in_dim(mlp_up, me_g * units, units, 1)
        down_own = lax.dynamic_slice_in_dim(mlp_down, me_g * units, units, 0)
        tokens = [lax.all_gather(pair, "tok", axis=0, tiled=True)]
        up_blocks = [lax.all_gather(up_own, "tok", axis=0, tiled=True)]
        down_blocks = [lax.all_gather(down_own, "tok", axis=1, tiled=True)]
    square = [shape((dh, hidden), F32), shape((dh, hidden), F32), shape((hidden, dh), F32)]
    prepared = call(
        functools.partial(own_kernel, paired),
        [
            *[shape(x.shape, BF) for x in square],
            *square,
            shape((16, hidden), F32),
            shape((8, dh), F32),
        ],
        [pair, fw_one[0], fw_three[0], fw_two[0]],
        flops=12 * n_key * dh * hidden,
    )
    n_all = sum(x.shape[0] for x in tokens)
    tokens, asks = barrier((tokens, asks))
    own, own_sq, send = call(
        functools.partial(fast_kernel, len(tokens), near),
        [shape((near * n, wide), F32), shape((8, wide), F32), shape((near * n + 16, wide), BF)],
        [*tokens, queries, *asks, *prepared],
        [pltpu.VMEM((n_all, dh), BF), pltpu.VMEM((n_all, dh), BF), pltpu.VMEM((near * n, dh), F32)],
        flops=12 * n_all * dh * hidden + 6 * near * n * dh * hidden,
    )
    got = moved(send, rep=1)
    if paired:
        got, w_first, w_second = barrier((got, w_first, w_second))
    mixed, low = call(
        mix_kernel,
        [shape((n, wide), F32), shape((near * n + 16, wide), BF)],
        [own, own_sq, got, stream, gain[None, :], *asks],
    )
    pieces, places = [], []
    for dg, h in itertools.product(range(groups), range(n_head)):
        x = moved(low, groups=dg, head=h)
        pieces += [x, moved(x, rep=1)]
        places += [(dg, h, 0), (dg, h, 1)]
    if paired:
        up_blocks = down_blocks = [same, w_first, w_second, w_third]
    rows, model = groups * near * n, n_head * dh
    (act,) = call(
        functools.partial(up_kernel, places, len(up_blocks)),
        [shape((rows, units), BF)],
        [*pieces, *up_blocks],
        [pltpu.VMEM((rows, model), BF)],
        flops=2 * rows * units * model,
    )
    own, send = call(
        functools.partial(down_kernel, len(down_blocks)),
        [shape((rows, n_head * wide), F32), shape((rows, n_head * wide), BF)],
        [act, *down_blocks],
        [pltpu.VMEM((rows, model), F32)],
        flops=2 * rows * units * model,
    )
    got = moved(send, rep=1)
    moves = list(itertools.product(range(groups), range(near), range(n_head)))
    total, *parts = call(
        functools.partial(pair_kernel, moves, near),
        [shape((n, wide), F32), *[shape((n, wide), BF)] * (len(moves) - 1)],
        [own, got, mixed],
    )
    for (dg, dz, h), x in zip(moves[1:], parts):
        total = total + moved(x, groups=(groups - dg) % groups, tok=dz, head=(n_head - h) % n_head).astype(F32)
    live = jnp.arange(n, dtype=jnp.int32) < counts[0]
    return jnp.where(live[:, None], total, 0.0).astype(BF)


def solution(mesh):
    placed = (
        P(("groups", "tok"), "head"),
        P(("groups", "tok"), "head"),
        P(("groups", "tok"), "head"),
        P(("groups", "tok"), "head"),
        P(("groups", "tok"), "head"),
        P("head"),
        P(("groups", "tok")),
        P("head", None, "rep"),
        P("head", None, "rep"),
        P("head", "rep", None),
        P("tok", ("head", "rep")),
        P(("head", "rep"), "tok"),
    )
    return jax.shard_map(
        on_device,
        mesh=mesh,
        in_specs=placed,
        out_specs=P(("groups", "tok"), ("head", "rep")),
        check_vma=False,
    )
```

```python
import functools
import itertools

import jax
import jax.numpy as jnp
import numpy as np
from jax import lax
from jax.experimental import pallas as pl
from jax.experimental.pallas import tpu as pltpu
from jax.sharding import PartitionSpec as P

BF, F32 = jnp.bfloat16, jnp.float32


def dot(a, b, dims=((1,), (0,))):
    return lax.dot_general(a, b, (dims, ((), ())), preferred_element_type=F32)


def moved(x, groups=0, tok=0, head=0, rep=0):
    shifts = {"groups": groups, "tok": tok, "head": head, "rep": rep}
    axes = [a for a, s in shifts.items() if s]
    if not axes:
        return x
    sizes = [lax.axis_size(a) for a in axes]
    pairs = []
    for here in range(int(np.prod(sizes))):
        at = np.unravel_index(here, sizes)
        there = [i ^ tok if a == "tok" else (i + shifts[a]) % n for a, i, n in zip(axes, at, sizes)]
        pairs.append((int(np.ravel_multi_index(there, sizes)), here))
    return lax.ppermute(x, tuple(axes), pairs)


def shape(dims, dtype):
    return jax.ShapeDtypeStruct(dims, dtype)


def call(kernel, outs, args, scratch=(), fetched=0):
    touched = sum(int(np.prod(x.shape)) * x.dtype.itemsize for x in (*args, *outs))
    kept = sum(int(np.prod(x.shape)) * 4 for x in scratch if hasattr(x, "shape"))
    args = [pltpu.with_memory_space_constraint(x, pltpu.HBM) if i < fetched else x for i, x in enumerate(args)]
    return pl.pallas_call(
        kernel,
        out_shape=outs,
        in_specs=[pl.BlockSpec(memory_space=pltpu.HBM if i < fetched else pltpu.VMEM) for i in range(len(args))],
        out_specs=[pl.BlockSpec(memory_space=pltpu.VMEM)] * len(outs),
        scratch_shapes=list(scratch),
        compiler_params=pltpu.CompilerParams(vmem_limit_bytes=touched + kept + (10 << 20)),
        cost_estimate=pl.CostEstimate(flops=1, bytes_accessed=1, transcendentals=0),
    )(*args)


def window(index, size):
    return pl.ds(pl.multiple_of(index * size, size), size)


def fetch(pairs, sems):
    copies = [pltpu.make_async_copy(src, dst, sems.at[i]) for i, (src, dst) in enumerate(pairs)]
    for c in copies:
        c.start()
    return copies


def message_kernel(keys, values, rates, *refs):
    n, dh = keys.shape
    n_far = 2 if len(refs) > 4 else 0
    far, (pair, *messages) = refs[:n_far], refs[n_far:]
    *messages, v, rate_row, sems = messages
    me = lax.axis_index("rep")
    pairs = [(keys, pair.at[:, :dh]), (values, v), (rates, rate_row)]
    if n_far:
        share, full, *messages = messages
        q, s = messages
        pairs += [(far[0], q), (far[1], s)]
    copies = fetch(pairs, sems)
    for c in copies:
        c.wait()
    rate = jnp.broadcast_to(rate_row[...], (128, n)).T
    for c in range(0, dh, 128):
        pair[:, dh + c : dh + c + 128] = (v[:, c : c + 128].astype(F32) * rate).astype(BF)
    if n_far:
        rows = share.shape[0]
        wide = dh // 2
        part = pair[window(me, rows), :]
        share[...] = part
        full[:, : 2 * dh] = part
        for i in range(n // rows):
            at = 2 * dh + i * (dh + wide)
            there = slice(i * rows, (i + 1) * rows)
            full[:, at : at + dh] = q[there, :]
            full[:, at + dh : at + dh + wide] = s[there, window(me, wide)]


def pack_kernel(up, down, same, other):
    deep, wide = up.shape[0], same.shape[1]
    bit = lax.bitwise_and(lax.axis_index("tok"), 1)
    for out, b in ((same, bit), (other, 1 - bit)):
        part = window(lax.axis_index("groups") * 2 + b, wide)
        out[:deep, :] = up[:, part]
        out[deep:, :] = down[part, :]


def gradients(k, e, w1b, w3b, w2b):
    a1, a3, b = dot(k, w1b), dot(k, w3b), dot(e, w2b, ((1,), (1,)))
    sig = jax.nn.sigmoid(a1)
    act = a1 * sig
    g = (act * a3).astype(BF)
    r1 = (b * a3 * (sig * (1.0 + a1 * (1.0 - sig)))).astype(BF)
    r3 = (b * act).astype(BF)
    first = ((0,), (0,))
    return dot(k, r1, first), dot(k, r3, first), dot(g, e, first)


def squares(x):
    return jnp.sum(x * x, axis=0, keepdims=True)


def own_kernel(take_own, pair, w1, w3, w2, b1, b3, b2, u1, u3, u2, sq13, sq2):
    dh, hidden = w1.shape
    block = min(hidden, 256)
    sq2[...] = jnp.broadcast_to(squares(w2[...]), sq2.shape)
    for j in range(0, hidden, block):
        js = slice(j, j + block)
        x1, x3, x2 = w1[:, js], w3[:, js], w2[js, :]
        b1[:, js], b3[:, js], b2[js, :] = x1.astype(BF), x3.astype(BF), x2.astype(BF)
        sq13[0:8, js] = jnp.broadcast_to(squares(x1), (8, block))
        sq13[8:16, js] = jnp.broadcast_to(squares(x3), (8, block))
        if take_own:
            d1, d3, d2 = gradients(pair[:, :dh], pair[:, dh:], b1[:, js], b3[:, js], b2[js, :])
            x1, x3, x2 = x1 + d1, x3 + d3, x2 + d2
        u1[:, js], u3[:, js], u2[js, :] = x1, x3, x2


def asked_part(message, dh, wide, i):
    at = 2 * dh + i * (dh + wide)
    return message[:, at : at + dh], message[:, at + dh : at + dh + wide]


def fast_kernel(n_pieces, near, *refs):
    pieces, refs = refs[:n_pieces], refs[n_pieces:]
    q, b1, b3, b2, u1, u3, u2, sq13, sq2, own_out, own_sq, send, ks, es, hp = refs
    dh, hidden = b1.shape
    wide = own_out.shape[1]
    at = 0
    for p in pieces:
        n = p.shape[0]
        ks[at : at + n, :] = p[:, :dh]
        es[at : at + n, :] = p[:, dh : 2 * dh]
        at += n
    tokens, step, block = at, min(at, 512), min(hidden, 256)
    asked = q[...]
    if near > 1:
        times = q.shape[0] // pieces[0].shape[0]
        asked = jnp.concatenate([asked, *[asked_part(pieces[0], dh, wide, i)[0] for i in range(times)]], axis=0)
    new_sq = jnp.zeros((1, dh), F32)
    for j in range(0, hidden, block):
        js = slice(j, j + block)

        def add(i, sums):
            rows = pl.ds(pl.multiple_of(i * step, step), step)
            parts = gradients(ks[rows, :], es[rows, :], b1[:, js], b3[:, js], b2[js, :])
            return tuple(s + p for s, p in zip(sums, parts))

        sums = (u1[:, js], u3[:, js], u2[js, :])
        sums = add(0, sums) if tokens == step else lax.fori_loop(0, tokens // step, add, sums)

        def normed(old_sq, new):
            return (new * (jnp.sqrt(old_sq) * lax.rsqrt(squares(new) + 1e-06))).astype(BF)

        new_sq = new_sq + squares(sums[2])
        qa = dot(asked, normed(sq13[0:1, js], sums[0]))
        qc = dot(asked, normed(sq13[8:9, js], sums[1]))
        part = dot((qa * jax.nn.sigmoid(qa) * qc).astype(BF), sums[2].astype(BF))
        hp[...] = part if j == 0 else hp[...] + part
    me, n = lax.axis_index("rep"), own_out.shape[0]
    own_out[...] = hp[:, window(me, wide)]
    send[:n, :] = hp[:, window(1 - me, wide)].astype(BF)
    row = lax.broadcasted_iota(jnp.int32, (8, dh), 0)
    hp[:8, :] = jnp.where(row == 0, sq2[...], jnp.where(row == 1, new_sq, 0.0))
    own_sq[...] = hp[:8, window(me, wide)]
    sq = hp[:8, window(1 - me, wide)]
    top = sq.astype(BF).astype(F32)
    send[n:, :] = jnp.concatenate([top, sq - top], axis=0).astype(BF)


def mix_kernel(own, own_sq, got, stream, gain, *refs):
    *asks, mixed, low = refs
    n, wide = mixed.shape
    rows = own.shape[0]
    tail = got[rows:, :].astype(F32)
    sq = own_sq[...] + tail[:8] + tail[8:]
    scale = jnp.sqrt(sq[0:1]) * lax.rsqrt(sq[1:2] + 1e-06)
    dh = stream.shape[1]
    y = (own[...] + got[:rows, :].astype(F32)) * scale
    mixed[...] = y[:n] + stream[:, window(lax.axis_index("rep"), wide)].astype(F32)
    low[:n, :] = mixed[...].astype(BF)
    if asks:
        rest = asks[0].shape[0]
        for i in range(n // rest):
            part = slice(n + i * rest, n + (i + 1) * rest)
            low[part, :] = (y[part] + asked_part(asks[0], dh, wide, i)[1].astype(F32)).astype(BF)
    g = jnp.broadcast_to(gain[:, window(lax.axis_index("rep"), wide)], (16, wide))
    row = lax.broadcasted_iota(jnp.int32, (16, wide), 0)
    top = g.astype(BF).astype(F32)
    mid = (g - top).astype(BF).astype(F32)
    low[rows:, :] = jnp.where(row == 0, top, jnp.where(row == 1, mid, jnp.where(row == 2, g - top - mid, 0.0))).astype(BF)


def up_kernel(places, n_blocks, *refs):
    pieces, refs = refs[: len(places)], refs[len(places) :]
    n_head = lax.axis_size("head")
    blocks, (out, zs) = refs[:n_blocks], refs[n_blocks:]
    me_h, me_r, me_t = lax.axis_index("head"), lax.axis_index("rep"), lax.axis_index("tok")
    n, wide = pieces[0].shape[0] - 16, pieces[0].shape[1]
    width = zs.shape[1]
    for dg in range(lax.axis_size("groups")):
        here = [(p, dh, dr) for p, (g, dh, dr) in zip(pieces, places) if g == dg]
        total = jnp.zeros((n, 1), F32)
        for p, _, _ in here:
            x = p[:n, :].astype(F32)
            total = total + jnp.sum(x * x, axis=1, keepdims=True)
        inv = lax.rsqrt(total / width + 1e-06)
        for p, dh, dr in here:
            r = lax.rem(me_r + dr, 2)
            head = lax.rem(me_h + dh, n_head)
            gain = jnp.sum(p[n:, :].astype(F32), axis=0, keepdims=True)
            zs[dg * n : (dg + 1) * n, window(head * 2 + r, wide)] = (p[:n, :].astype(F32) * inv * gain).astype(BF)
    total = None
    deep = width // n_blocks
    for s, x in enumerate(blocks):
        z = zs[...] if n_blocks == 1 else zs[:, window(lax.bitwise_xor(me_t, s), deep)]
        term = dot(z, x[:deep, :])
        total = term if total is None else total + term
    out[...] = (0.5 * total * (1.0 + lax.erf(total * np.float32(0.5**0.5)))).astype(BF)


def down_kernel(n_blocks, h, *refs):
    blocks, (own, send, os) = refs[:n_blocks], refs[n_blocks:]
    me_h, me_r, me_t = lax.axis_index("head"), lax.axis_index("rep"), lax.axis_index("tok")
    n_head = lax.axis_size("head")
    units = h.shape[1]
    for s, x in enumerate(blocks):
        term = dot(h[...], x[x.shape[0] - units :, :])
        if n_blocks == 1:
            os[...] = term
        else:
            os[:, window(lax.bitwise_xor(me_t, s), term.shape[1])] = term
    wide = own.shape[1] // n_head
    for dh in range(n_head):
        at = lax.rem(me_h + dh, n_head) * 2
        there = slice(dh * wide, (dh + 1) * wide)
        own[:, there] = os[:, window(at + me_r, wide)]
        send[:, there] = os[:, window(at + 1 - me_r, wide)].astype(BF)


def pair_kernel(moves, near, own, got, mixed, *outs):
    n, wide = mixed.shape
    for (dg, dz, dh), out in zip(moves, outs):
        at = (dg * near + dz) * n
        rows, cols = slice(at, at + n), slice(dh * wide, (dh + 1) * wide)
        total = own[rows, cols] + got[rows, cols].astype(F32)
        out[...] = mixed[...] + total if (dg, dz, dh) == (0, 0, 0) else total.astype(BF)


def on_device(
    keys, values, rates, queries, stream, gain, counts, fw_one, fw_three, fw_two, mlp_up, mlp_down
):
    n_tok, n_head = lax.axis_size("tok"), lax.axis_size("head")
    groups, reps = lax.axis_size("groups"), lax.axis_size("rep")
    dh, n_key, n = keys.shape[1], keys.shape[0], queries.shape[0]
    hidden = fw_one.shape[2]
    wide = dh // reps
    paired = n_tok == 4
    near = 2 if paired else 1
    units = mlp_up.shape[1] // groups // near
    barrier = lax.optimization_barrier

    rows = n_key // reps
    messages, far, fetches = [], [], [pltpu.VMEM((n_key, dh), BF), pltpu.VMEM((1, n_key), F32)]
    if paired:
        messages = [shape((rows, 2 * dh), BF), shape((rows, 2 * dh + (n // rows) * (dh + wide)), BF)]
        far = [queries, stream]
        fetches = [pltpu.VMEM((n, dh), BF), pltpu.VMEM((n, dh), BF), *fetches]
    pair, *messages = call(
        message_kernel,
        [shape((n_key, 2 * dh), BF), *messages],
        [keys, values, rates.reshape(1, n_key), *far],
        [*fetches, pltpu.SemaphoreType.DMA((5,))],
        fetched=3 + len(far),
    )
    square = [shape((dh, hidden), F32), shape((dh, hidden), F32), shape((hidden, dh), F32)]
    prepared = call(
        functools.partial(own_kernel, paired),
        [
            *[shape(x.shape, BF) for x in square],
            *square,
            shape((16, hidden), F32),
            shape((8, dh), F32),
        ],
        [pair, fw_one[0], fw_three[0], fw_two[0]],
    )
    asks = []
    if paired:
        share, full = messages
        others = [moved(full, tok=1), moved(share, tok=2), moved(share, tok=3)]
        same, other = call(
            pack_kernel, [shape((mlp_up.shape[0] + units, units), BF)] * 2, [mlp_up, mlp_down]
        )
        same_2, _ = barrier((same, prepared))
        w_second = moved(same_2, tok=2)
        others, other_1, prepared = barrier((others, other, prepared))
        first = others[0]
        w_first = moved(other_1, tok=1)
        tokens = [first, *others[1:]]
        tokens = tokens + [moved(x, rep=1) for x in (first[:, : 2 * dh], *others[1:])]
        asks = [first]
        w_third = moved(barrier((other, w_second))[0], tok=3)
    else:
        me_g = lax.axis_index("groups")
        up_own = lax.dynamic_slice_in_dim(mlp_up, me_g * units, units, 1)
        down_own = lax.dynamic_slice_in_dim(mlp_down, me_g * units, units, 0)
        tokens = [lax.all_gather(pair, "tok", axis=0, tiled=True)]
        up_blocks = [lax.all_gather(up_own, "tok", axis=0, tiled=True)]
        down_blocks = [lax.all_gather(down_own, "tok", axis=1, tiled=True)]
    n_all = sum(x.shape[0] for x in tokens)
    tokens = barrier(tokens)
    own, own_sq, send = call(
        functools.partial(fast_kernel, len(tokens), near),
        [shape((near * n, wide), F32), shape((8, wide), F32), shape((near * n + 16, wide), BF)],
        [*tokens, queries, *prepared],
        [pltpu.VMEM((n_all, dh), BF), pltpu.VMEM((n_all, dh), BF), pltpu.VMEM((near * n, dh), F32)],
    )
    got = moved(send, rep=1)
    if paired:
        got, w_first, w_second = barrier((got, w_first, w_second))
    mixed, low = call(
        mix_kernel,
        [shape((n, wide), F32), shape((near * n + 16, wide), BF)],
        [own, own_sq, got, stream, gain[None, :], *asks],
    )
    pieces, places = [], []
    for dg, h in itertools.product(range(groups), range(n_head)):
        x = moved(low, groups=dg, head=h)
        pieces += [x, moved(x, rep=1)]
        places += [(dg, h, 0), (dg, h, 1)]
    if paired:
        up_blocks = down_blocks = [same, w_first, w_second, w_third]
    rows, model = groups * near * n, n_head * dh
    (act,) = call(
        functools.partial(up_kernel, places, len(up_blocks)),
        [shape((rows, units), BF)],
        [*pieces, *up_blocks],
        [pltpu.VMEM((rows, model), BF)],
    )
    own, send = call(
        functools.partial(down_kernel, len(down_blocks)),
        [shape((rows, n_head * wide), F32), shape((rows, n_head * wide), BF)],
        [act, *down_blocks],
        [pltpu.VMEM((rows, model), F32)],
    )
    got = moved(send, rep=1)
    moves = list(itertools.product(range(groups), range(near), range(n_head)))
    total, *parts = call(
        functools.partial(pair_kernel, moves, near),
        [shape((n, wide), F32), *[shape((n, wide), BF)] * (len(moves) - 1)],
        [own, got, mixed],
    )
    for (dg, dz, h), x in zip(moves[1:], parts):
        total = total + moved(x, groups=(groups - dg) % groups, tok=dz, head=(n_head - h) % n_head).astype(F32)
    live = jnp.arange(n, dtype=jnp.int32) < counts[0]
    return jnp.where(live[:, None], total, 0.0).astype(BF)


def solution(mesh):
    placed = (
        P(("groups", "tok"), "head"),
        P(("groups", "tok"), "head"),
        P(("groups", "tok"), "head"),
        P(("groups", "tok"), "head"),
        P(("groups", "tok"), "head"),
        P("head"),
        P(("groups", "tok")),
        P("head", None, "rep"),
        P("head", None, "rep"),
        P("head", "rep", None),
        P("tok", ("head", "rep")),
        P(("head", "rep"), "tok"),
    )
    return jax.shard_map(
        on_device,
        mesh=mesh,
        in_specs=placed,
        out_specs=P(("groups", "tok"), ("head", "rep")),
        check_vma=False,
    )
```

```python
import functools
import itertools

import jax
import jax.numpy as jnp
import numpy as np
from jax import lax
from jax.experimental import pallas as pl
from jax.experimental.pallas import tpu as pltpu
from jax.sharding import PartitionSpec as P

BF, F32 = jnp.bfloat16, jnp.float32


def dot(a, b, dims=((1,), (0,))):
    return lax.dot_general(a, b, (dims, ((), ())), preferred_element_type=F32)


def moved(x, groups=0, tok=0, head=0, rep=0):
    shifts = {"groups": groups, "tok": tok, "head": head, "rep": rep}
    axes = [a for a, s in shifts.items() if s]
    if not axes:
        return x
    sizes = [lax.axis_size(a) for a in axes]
    pairs = []
    for here in range(int(np.prod(sizes))):
        at = np.unravel_index(here, sizes)
        there = [i ^ tok if a == "tok" else (i + shifts[a]) % n for a, i, n in zip(axes, at, sizes)]
        pairs.append((int(np.ravel_multi_index(there, sizes)), here))
    return lax.ppermute(x, tuple(axes), pairs)


def shape(dims, dtype):
    return jax.ShapeDtypeStruct(dims, dtype)


def call(kernel, outs, args, scratch=(), fetched=0):
    touched = sum(int(np.prod(x.shape)) * x.dtype.itemsize for x in (*args, *outs))
    kept = sum(int(np.prod(x.shape)) * 4 for x in scratch if hasattr(x, "shape"))
    args = [pltpu.with_memory_space_constraint(x, pltpu.HBM) if i < fetched else x for i, x in enumerate(args)]
    return pl.pallas_call(
        kernel,
        out_shape=outs,
        in_specs=[pl.BlockSpec(memory_space=pltpu.HBM if i < fetched else pltpu.VMEM) for i in range(len(args))],
        out_specs=[pl.BlockSpec(memory_space=pltpu.VMEM)] * len(outs),
        scratch_shapes=list(scratch),
        compiler_params=pltpu.CompilerParams(vmem_limit_bytes=touched + kept + (10 << 20)),
        cost_estimate=pl.CostEstimate(flops=1, bytes_accessed=1, transcendentals=0),
    )(*args)


def window(index, size):
    return pl.ds(pl.multiple_of(index * size, size), size)


def fetch(pairs, sems):
    copies = [pltpu.make_async_copy(src, dst, sems.at[i]) for i, (src, dst) in enumerate(pairs)]
    for c in copies:
        c.start()
    return copies


def message_kernel(keys, values, rates, stream, gain, *refs):
    n, dh = keys.shape
    *_, v, rate_row, s, g, sems = refs
    copies = [(keys, None), (values, v), (rates, rate_row), (stream, s), (gain, g)]
    if len(refs) == 8:
        pair, base, gains = refs[:3]
    else:
        queries, pair, base, gains, share, full, q = refs[:7]
        copies.append((queries, q))
    copies[0] = (keys, pair.at[:, :dh])
    for c in fetch(copies, sems):
        c.wait()
    me, wide = lax.axis_index("rep"), base.shape[1]
    rate = jnp.broadcast_to(rate_row[...], (128, n)).T
    for c in range(0, dh, 128):
        pair[:, dh + c : dh + c + 128] = (v[:, c : c + 128].astype(F32) * rate).astype(BF)
    base[...] = s[:, window(me, wide)]
    x = jnp.broadcast_to(g[:, window(me, wide)], gains.shape)
    row = lax.broadcasted_iota(jnp.int32, gains.shape, 0)
    top = x.astype(BF).astype(F32)
    mid = (x - top).astype(BF).astype(F32)
    gains[...] = jnp.where(row == 0, top, jnp.where(row == 1, mid, jnp.where(row == 2, x - top - mid, 0.0))).astype(BF)
    if len(refs) > 8:
        rows = share.shape[0]
        part = pair[window(me, rows), :]
        share[...] = part
        full[:, : 2 * dh] = part
        full[:, 2 * dh : 3 * dh] = q[window(me, rows), :]
        for i in range(n // rows):
            full[:, 3 * dh + i * wide : 3 * dh + (i + 1) * wide] = base[i * rows : (i + 1) * rows, :]


def pack_kernel(up, down, same, other):
    deep, wide = up.shape[0], same.shape[1]
    bit = lax.bitwise_and(lax.axis_index("tok"), 1)
    for out, b in ((same, bit), (other, 1 - bit)):
        part = window(lax.axis_index("groups") * 2 + b, wide)
        out[:deep, :] = up[:, part]
        out[deep:, :] = down[part, :]


def gradients(k, e, w1b, w3b, w2b):
    a1, a3, b = dot(k, w1b), dot(k, w3b), dot(e, w2b, ((1,), (1,)))
    sig = jax.nn.sigmoid(a1)
    act = a1 * sig
    g = (act * a3).astype(BF)
    r1 = (b * a3 * (sig * (1.0 + a1 * (1.0 - sig)))).astype(BF)
    r3 = (b * act).astype(BF)
    first = ((0,), (0,))
    return dot(k, r1, first), dot(k, r3, first), dot(g, e, first)


def squares(x):
    return jnp.sum(x * x, axis=0, keepdims=True)


def own_kernel(take_own, pair, w1, w3, w2, b1, b3, b2, u1, u3, u2, sq13, sq2):
    dh, hidden = w1.shape
    block = min(hidden, 256)
    sq2[...] = jnp.broadcast_to(squares(w2[...]), sq2.shape)
    for j in range(0, hidden, block):
        js = slice(j, j + block)
        x1, x3, x2 = w1[:, js], w3[:, js], w2[js, :]
        b1[:, js], b3[:, js], b2[js, :] = x1.astype(BF), x3.astype(BF), x2.astype(BF)
        sq13[0:8, js] = jnp.broadcast_to(squares(x1), (8, block))
        sq13[8:16, js] = jnp.broadcast_to(squares(x3), (8, block))
        if take_own:
            d1, d3, d2 = gradients(pair[:, :dh], pair[:, dh:], b1[:, js], b3[:, js], b2[js, :])
            x1, x3, x2 = x1 + d1, x3 + d3, x2 + d2
        u1[:, js], u3[:, js], u2[js, :] = x1, x3, x2


def fast_kernel(n_pieces, near, *refs):
    pieces, refs = refs[:n_pieces], refs[n_pieces:]
    q, b1, b3, b2, u1, u3, u2, sq13, sq2, own_out, own_sq, send, ks, es, hp, qs = refs
    dh, hidden = b1.shape
    me = lax.axis_index("rep")
    at = 0
    for p in pieces:
        n = p.shape[0]
        ks[at : at + n, :] = p[:, :dh]
        es[at : at + n, :] = p[:, dh : 2 * dh]
        at += n
    tokens, step, block = at, min(at, 512), min(hidden, 256)
    n = q.shape[0]
    qs[:n, :] = q[...]
    if near > 1:
        mine, theirs = pieces[0], pieces[n_pieces // 2]
        rows = mine.shape[0]
        qs[pl.ds(pl.multiple_of(n + me * rows, rows), rows), :] = mine[:, 2 * dh : 3 * dh]
        qs[pl.ds(pl.multiple_of(n + (1 - me) * rows, rows), rows), :] = theirs[:, 2 * dh : 3 * dh]
    asked = qs[...]
    new_sq = jnp.zeros((1, dh), F32)
    for j in range(0, hidden, block):
        js = slice(j, j + block)

        def add(i, sums):
            rows = pl.ds(pl.multiple_of(i * step, step), step)
            parts = gradients(ks[rows, :], es[rows, :], b1[:, js], b3[:, js], b2[js, :])
            return tuple(s + p for s, p in zip(sums, parts))

        sums = (u1[:, js], u3[:, js], u2[js, :])
        sums = add(0, sums) if tokens == step else lax.fori_loop(0, tokens // step, add, sums)

        def normed(old_sq, new):
            return (new * (jnp.sqrt(old_sq) * lax.rsqrt(squares(new) + 1e-06))).astype(BF)

        new_sq = new_sq + squares(sums[2])
        qa = dot(asked, normed(sq13[0:1, js], sums[0]))
        qc = dot(asked, normed(sq13[8:9, js], sums[1]))
        part = dot((qa * jax.nn.sigmoid(qa) * qc).astype(BF), sums[2].astype(BF))
        hp[...] = part if j == 0 else hp[...] + part
    n, wide = own_out.shape
    own_out[...] = hp[:, window(me, wide)]
    send[:n, :] = hp[:, window(1 - me, wide)].astype(BF)
    row = lax.broadcasted_iota(jnp.int32, (8, dh), 0)
    hp[:8, :] = jnp.where(row == 0, sq2[...], jnp.where(row == 1, new_sq, 0.0))
    own_sq[...] = hp[:8, window(me, wide)]
    sq = hp[:8, window(1 - me, wide)]
    top = sq.astype(BF).astype(F32)
    send[n:, :] = jnp.concatenate([top, sq - top], axis=0).astype(BF)


def mix_kernel(own, own_sq, got, base, gains, *refs):
    *asks, mixed, low = refs
    n, wide = mixed.shape
    rows = own.shape[0]
    tail = got[rows:, :].astype(F32)
    sq = own_sq[...] + tail[:8] + tail[8:]
    y = (own[...] + got[:rows, :].astype(F32)) * (jnp.sqrt(sq[0:1]) * lax.rsqrt(sq[1:2] + 1e-06))
    mixed[...] = y[:n] + base[...].astype(F32)
    low[:n, :] = mixed[...].astype(BF)
    for message in asks:
        part = message.shape[0]
        for i in range(n // part):
            at, there = n + i * part, message.shape[1] - n // part * wide + i * wide
            low[at : at + part, :] = (y[at : at + part] + message[:, there : there + wide].astype(F32)).astype(BF)
    low[rows:, :] = gains[...]


def up_kernel(places, first, n_blocks, *refs):
    pieces, refs = refs[: len(places)], refs[len(places) :]
    blocks, (zs, total) = refs[:-2], refs[-2:]
    me_h, me_r, me_t = lax.axis_index("head"), lax.axis_index("rep"), lax.axis_index("tok")
    n_head = lax.axis_size("head")
    n, wide = pieces[0].shape[0] - 16, pieces[0].shape[1]
    width = zs.shape[1]
    for dg in range(lax.axis_size("groups")):
        here = [(p, dh, dr) for p, (g, dh, dr) in zip(pieces, places) if g == dg]
        norm = jnp.zeros((n, 1), F32)
        for p, _, _ in here:
            x = p[:n, :].astype(F32)
            norm = norm + jnp.sum(x * x, axis=1, keepdims=True)
        inv = lax.rsqrt(norm / width + 1e-06)
        for p, dh, dr in here:
            r = lax.rem(me_r + dr, 2)
            head = lax.rem(me_h + dh, n_head)
            gain = jnp.sum(p[n:, :].astype(F32), axis=0, keepdims=True)
            zs[dg * n : (dg + 1) * n, window(head * 2 + r, wide)] = (p[:n, :].astype(F32) * inv * gain).astype(BF)
    total[...] = up_terms(zs, first, n_blocks, blocks)


def up_terms(zs, first, n_blocks, blocks):
    deep = zs.shape[1] // n_blocks
    total = None
    for s, x in enumerate(blocks, first):
        z = zs[...] if n_blocks == 1 else zs[:, window(lax.bitwise_xor(lax.axis_index("tok"), s), deep)]
        term = dot(z, x[:deep, :])
        total = term if total is None else total + term
    return total


def down_kernel(n_late, n_blocks, zs, total, *refs):
    blocks, (own, send, os) = refs[:-3], refs[-3:]
    me_h, me_r, me_t = lax.axis_index("head"), lax.axis_index("rep"), lax.axis_index("tok")
    n_head = lax.axis_size("head")
    x = total[...]
    if n_late:
        x = x + up_terms(zs, n_blocks - n_late, n_blocks, blocks[n_blocks - n_late :])
    h = (0.5 * x * (1.0 + lax.erf(x * np.float32(0.5**0.5)))).astype(BF)
    units = h.shape[1]
    for s, x in enumerate(blocks):
        term = dot(h, x[x.shape[0] - units :, :])
        if n_blocks == 1:
            os[...] = term
        else:
            os[:, window(lax.bitwise_xor(me_t, s), term.shape[1])] = term
    rows, wide = own.shape[0], own.shape[1] // n_head
    for dh in range(n_head):
        there = slice(dh * wide, (dh + 1) * wide)
        cols = window(lax.rem(me_h + dh, n_head), wide)
        own[:, there] = os[window(me_r, rows), cols]
        send[:, there] = os[window(1 - me_r, rows), cols].astype(BF)


def pair_kernel(moves, own, got, *outs):
    n, wide = outs[0].shape
    for (dz, dh), out in zip(moves, outs):
        rows, cols = slice(dz * n, (dz + 1) * n), slice(dh * wide, (dh + 1) * wide)
        out[...] = (own[rows, cols] + got[rows, cols].astype(F32)).astype(BF)


def sum_kernel(*refs):
    *parts, mixed, keep, send, acc = refs
    total = parts[0][...].astype(F32)
    for p in parts[1:]:
        total = total + p[...].astype(F32)
    acc[...] = total
    me, wide = lax.axis_index("rep"), keep.shape[1]
    keep[...] = mixed[...] + acc[:, window(me, wide)]
    send[...] = acc[:, window(1 - me, wide)].astype(BF)


def dealt(x, tok, head):
    axes = ("groups", "tok", "head", "rep")
    sizes = [lax.axis_size(a) for a in axes]
    pairs = []
    for here in range(int(np.prod(sizes))):
        g, t, h, r = np.unravel_index(here, sizes)
        there = ((g + r) % sizes[0], t ^ tok, (h + head) % sizes[2], r)
        pairs.append((here, int(np.ravel_multi_index(there, sizes))))
    return lax.ppermute(x, axes, pairs)


def on_device(
    keys, values, rates, queries, stream, gain, counts, fw_one, fw_three, fw_two, mlp_up, mlp_down
):
    n_tok, n_head = lax.axis_size("tok"), lax.axis_size("head")
    groups, reps = lax.axis_size("groups"), lax.axis_size("rep")
    dh, n_key, n = keys.shape[1], keys.shape[0], queries.shape[0]
    hidden = fw_one.shape[2]
    wide = dh // reps
    paired = n_tok == 4 and n_key == n
    near = 2 if paired else 1
    units = mlp_up.shape[1] // groups // near
    barrier = lax.optimization_barrier

    rows = n_key // reps
    outs = [shape((n_key, 2 * dh), BF), shape((n, wide), BF), shape((16, wide), BF)]
    fetches = [((n_key, dh), BF), ((1, n_key), F32), ((n, dh), BF), ((1, dh), F32)]
    sources = [keys, values, rates.reshape(1, n_key), stream, gain[None, :]]
    if paired:
        outs += [shape((rows, 2 * dh), BF), shape((rows, 4 * dh), BF)]
        fetches = [((n, dh), BF), *fetches]
        sources += [queries]
    pair, base, gains, *messages = call(
        message_kernel,
        outs,
        sources,
        [*[pltpu.VMEM(*f) for f in fetches], pltpu.SemaphoreType.DMA((len(sources),))],
        fetched=len(sources),
    )
    square = [shape((dh, hidden), F32), shape((dh, hidden), F32), shape((hidden, dh), F32)]
    prepared = call(
        functools.partial(own_kernel, paired),
        [
            *[shape(x.shape, BF) for x in square],
            *square,
            shape((16, hidden), F32),
            shape((8, dh), F32),
        ],
        [pair, fw_one[0], fw_three[0], fw_two[0]],
    )
    asks = []
    if paired:
        share, full = messages
        others = [moved(full, tok=1), moved(share, tok=2), moved(share, tok=3)]
        same, other = call(
            pack_kernel, [shape((mlp_up.shape[0] + units, units), BF)] * 2, [mlp_up, mlp_down]
        )
        others, w_same, w_other, prepared = barrier((others, same, other, prepared))
        tokens = [*others, *[moved(x, rep=1) for x in others]]
        w_second, w_third, w_first = moved(w_same, tok=2), moved(w_other, tok=3), moved(w_other, tok=1)
        asks = others[:1]
    else:
        me_g = lax.axis_index("groups")
        up_own = lax.dynamic_slice_in_dim(mlp_up, me_g * units, units, 1)
        down_own = lax.dynamic_slice_in_dim(mlp_down, me_g * units, units, 0)
        tokens = [lax.all_gather(pair, "tok", axis=0, tiled=True)]
        up_blocks = [lax.all_gather(up_own, "tok", axis=0, tiled=True)]
        down_blocks = [lax.all_gather(down_own, "tok", axis=1, tiled=True)]
    n_all = sum(x.shape[0] for x in tokens)
    tokens = barrier(tokens)
    own, own_sq, send = call(
        functools.partial(fast_kernel, len(tokens), near),
        [shape((near * n, wide), F32), shape((8, wide), F32), shape((near * n + 16, wide), BF)],
        [*tokens, queries, *prepared],
        [pltpu.VMEM((n_all, dh), BF), pltpu.VMEM((n_all, dh), BF), pltpu.VMEM((near * n, dh), F32), pltpu.VMEM((near * n, dh), BF)],
    )
    got = moved(send, rep=1)
    mixed, low = call(
        mix_kernel,
        [shape((n, wide), F32), shape((near * n + 16, wide), BF)],
        [own, own_sq, got, base, gains, *asks],
    )
    across = {}
    for dg, h in itertools.product(range(groups), range(n_head)):
        x = low
        if paired and dg and h:
            x, w_first, w_second = barrier((x, w_first, w_second))
        across[dg, h] = moved(x, groups=dg, head=h)
    if paired:
        across, w_third = barrier((across, w_third))
    pieces, places = [], []
    for m, x in across.items():
        pieces += [x, moved(x, rep=1)]
        places += [(*m, 0), (*m, 1)]
    early, late = [], []
    if paired:
        early, late = [same, w_first, w_second], [w_third]
        up_blocks = down_blocks = [*early, *late]
    else:
        early = up_blocks
    count = len(up_blocks)
    model = n_head * dh
    zs, act = call(
        functools.partial(up_kernel, places, 0, count),
        [shape((groups * near * n, model), BF), shape((groups * near * n, units), F32)],
        [*pieces, *early],
    )
    own, send = call(
        functools.partial(down_kernel, len(late), count),
        [shape((near * n, model), F32), shape((near * n, model), BF)],
        [zs, act, *down_blocks],
        [pltpu.VMEM((groups * near * n, model), F32)],
    )
    got = moved(send, rep=1)
    moves = list(itertools.product(range(near), range(n_head)))
    parts = call(
        functools.partial(pair_kernel, moves), [shape((n, dh), BF)] * len(moves), [own, got]
    )
    parts = [dealt(x, *m) for m, x in zip(moves, parts)]
    keep, send = call(
        sum_kernel, [shape((n, wide), F32), shape((n, wide), BF)], [*parts, mixed], [pltpu.VMEM((n, dh), F32)]
    )
    total = keep + moved(send, rep=1).astype(F32)
    live = jnp.arange(n, dtype=jnp.int32) < counts[0]
    return jnp.where(live[:, None], total, 0.0).astype(BF)


def solution(mesh):
    placed = (
        P(("groups", "tok"), "head"),
        P(("groups", "tok"), "head"),
        P(("groups", "tok"), "head"),
        P(("groups", "tok"), "head"),
        P(("groups", "tok"), "head"),
        P("head"),
        P(("groups", "tok")),
        P("head", None, "rep"),
        P("head", None, "rep"),
        P("head", "rep", None),
        P("tok", ("head", "rep")),
        P(("head", "rep"), "tok"),
    )
    return jax.shard_map(
        on_device,
        mesh=mesh,
        in_specs=placed,
        out_specs=P(("groups", "tok"), ("head", "rep")),
        check_vma=False,
    )
```

```python
import functools
import itertools

import jax
import jax.numpy as jnp
import numpy as np
from jax import lax
from jax.experimental import pallas as pl
from jax.experimental.pallas import tpu as pltpu
from jax.sharding import PartitionSpec as P

BF, F32 = jnp.bfloat16, jnp.float32


def dot(a, b, dims=((1,), (0,))):
    return lax.dot_general(a, b, (dims, ((), ())), preferred_element_type=F32)


def moved(x, groups=0, tok=0, head=0, rep=0):
    shifts = {"groups": groups, "tok": tok, "head": head, "rep": rep}
    axes = [a for a, s in shifts.items() if s]
    if not axes:
        return x
    sizes = [lax.axis_size(a) for a in axes]
    pairs = []
    for here in range(int(np.prod(sizes))):
        at = np.unravel_index(here, sizes)
        there = [i ^ tok if a == "tok" else (i + shifts[a]) % n for a, i, n in zip(axes, at, sizes)]
        pairs.append((int(np.ravel_multi_index(there, sizes)), here))
    return lax.ppermute(x, tuple(axes), pairs)


def shape(dims, dtype):
    return jax.ShapeDtypeStruct(dims, dtype)


def call(kernel, outs, args, scratch=(), fetched=0, unmoved=0):
    touched = sum(int(np.prod(x.shape)) * x.dtype.itemsize for x in (*args, *outs))
    kept = sum(int(np.prod(x.shape)) * 4 for x in scratch if hasattr(x, "shape"))
    args = [pltpu.with_memory_space_constraint(x, pltpu.HBM) if i < fetched else x for i, x in enumerate(args)]
    return pl.pallas_call(
        kernel,
        out_shape=outs,
        in_specs=[pl.BlockSpec(memory_space=pltpu.HBM if i < fetched + unmoved else pltpu.VMEM) for i in range(len(args))],
        out_specs=[pl.BlockSpec(memory_space=pltpu.VMEM)] * len(outs),
        scratch_shapes=list(scratch),
        compiler_params=pltpu.CompilerParams(vmem_limit_bytes=touched + kept + (10 << 20)),
        cost_estimate=pl.CostEstimate(flops=1, bytes_accessed=1, transcendentals=0),
    )(*args)


def local(arrays):
    return [pltpu.VMEM(x.shape, x.dtype) for x in arrays]


def window(index, size):
    return pl.ds(pl.multiple_of(index * size, size), size)


def fetch(pairs, sems):
    copies = [pltpu.make_async_copy(src, dst, sems.at[i]) for i, (src, dst) in enumerate(pairs)]
    for c in copies:
        c.start()
    return copies


def side_by_side(pair, keys, values, rates):
    n, dh = keys.shape
    pair[:, :dh] = keys[...]
    rate = jnp.broadcast_to(rates[...], (128, n)).T
    for c in range(0, dh, 128):
        pair[:, dh + c : dh + c + 128] = (values[:, c : c + 128].astype(F32) * rate).astype(BF)


def message_kernel(n_far, *refs):
    far, refs = refs[:n_far], refs[n_far:]
    outs, near, (pair, sems) = refs[: -n_far - 2], refs[-n_far - 2 : -2], refs[-2:]
    for c in fetch(list(zip(far, near)), sems):
        c.wait()
    side_by_side(pair, *near[:3])
    if len(outs) == 1:
        outs[0][...] = pair[...]
        return
    share, full = outs
    q, s = near[3:]
    me, (rows, width) = lax.axis_index("rep"), share.shape
    part = pair[window(me, rows), :]
    share[...] = part
    full[:, :width] = part
    dh = width // 2
    full[:, width : width + dh] = q[window(me, rows), :]
    wide = dh // 2
    for i in range(q.shape[0] // rows):
        at = width + dh + i * wide
        full[:, at : at + wide] = s[i * rows : (i + 1) * rows, window(me, wide)]


def pack_kernel(up, down, out):
    deep, wide = up.shape[0], out.shape[2]
    for t in range(out.shape[0]):
        part = window(lax.axis_index("groups") * 2 + t % 2, wide)
        out[t, :deep, :] = up[:, part]
        out[t, deep:, :] = down[part, :]


def gradients(k, e, w1b, w3b, w2b):
    a1, a3, b = dot(k, w1b), dot(k, w3b), dot(e, w2b, ((1,), (1,)))
    sig = jax.nn.sigmoid(a1)
    act = a1 * sig
    g = (act * a3).astype(BF)
    r1 = (b * a3 * (sig * (1.0 + a1 * (1.0 - sig)))).astype(BF)
    r3 = (b * act).astype(BF)
    first = ((0,), (0,))
    return dot(k, r1, first), dot(k, r3, first), dot(g, e, first)


def squares(x):
    return jnp.sum(x * x, axis=0, keepdims=True)


def fast_kernel(n_pieces, near, *refs):
    far, refs = refs[:7], refs[7:]
    pieces, refs = refs[:n_pieces], refs[n_pieces:]
    own_out, own_sq, send, ks, es, hp, qs, pair, *local, sems = refs
    w1, w3, w2, keys, values, rates, q = local
    copies = fetch(list(zip(far, local)), sems)
    dh, hidden = w1.shape
    me = lax.axis_index("rep")
    n = q.shape[0]
    at = 0
    for p in pieces:
        rows = p.shape[0]
        ks[at : at + rows, :] = p[:, :dh]
        es[at : at + rows, :] = p[:, dh : 2 * dh]
        at += rows
    if near > 1:
        mine, theirs = pieces[0], pieces[n_pieces // 2]
        rows = mine.shape[0]
        qs[pl.ds(pl.multiple_of(n + me * rows, rows), rows), :] = mine[:, 2 * dh : 3 * dh]
        qs[pl.ds(pl.multiple_of(n + (1 - me) * rows, rows), rows), :] = theirs[:, 2 * dh : 3 * dh]
    for c in copies[3:]:
        c.wait()
    if near > 1:
        side_by_side(pair, keys, values, rates)
        ks[at : at + n, :] = pair[:, :dh]
        es[at : at + n, :] = pair[:, dh:]
        at += n
    qs[:n, :] = q[...]
    asked = qs[...]
    tokens, step, block = at, min(at, 512), min(hidden, 256)
    for c in copies[:3]:
        c.wait()
    old_sq = squares(w2[...])
    new_sq = jnp.zeros((1, dh), F32)
    for j in range(0, hidden, block):
        js = slice(j, j + block)
        x1, x3, x2 = w1[:, js], w3[:, js], w2[js, :]
        b1, b3, b2 = x1.astype(BF), x3.astype(BF), x2.astype(BF)

        def add(i, sums):
            rows = pl.ds(pl.multiple_of(i * step, step), step)
            return tuple(s + p for s, p in zip(sums, gradients(ks[rows, :], es[rows, :], b1, b3, b2)))

        sums = (x1, x3, x2)
        sums = add(0, sums) if tokens == step else lax.fori_loop(0, tokens // step, add, sums)

        def normed(old, new):
            return (new * (jnp.sqrt(squares(old)) * lax.rsqrt(squares(new) + 1e-06))).astype(BF)

        new_sq = new_sq + squares(sums[2])
        qa, qc = dot(asked, normed(x1, sums[0])), dot(asked, normed(x3, sums[1]))
        part = dot((qa * jax.nn.sigmoid(qa) * qc).astype(BF), sums[2].astype(BF))
        hp[...] = part if j == 0 else hp[...] + part
    rows, wide = own_out.shape
    own_out[...] = hp[:, window(me, wide)]
    send[:rows, :] = hp[:, window(1 - me, wide)].astype(BF)
    row = lax.broadcasted_iota(jnp.int32, (8, dh), 0)
    hp[:8, :] = jnp.where(row == 0, old_sq, jnp.where(row == 1, new_sq, 0.0))
    own_sq[...] = hp[:8, window(me, wide)]
    sq = hp[:8, window(1 - me, wide)]
    top = sq.astype(BF).astype(F32)
    send[rows:, :] = jnp.concatenate([top, sq - top], axis=0).astype(BF)


def mix_kernel(stream_far, gain_far, own, own_sq, got, *refs):
    *asks, mixed, low, stream, gain, sems = refs
    copies = fetch([(stream_far, stream), (gain_far, gain)], sems)
    n, wide = mixed.shape
    rows, me = own.shape[0], lax.axis_index("rep")
    tail = got[rows:, :].astype(F32)
    sq = own_sq[...] + tail[:8] + tail[8:]
    y = (own[...] + got[:rows, :].astype(F32)) * (jnp.sqrt(sq[0:1]) * lax.rsqrt(sq[1:2] + 1e-06))
    for c in copies:
        c.wait()
    mixed[...] = y[:n] + stream[:, window(me, wide)].astype(F32)
    low[:n, :] = mixed[...].astype(BF)
    for message in asks:
        part = message.shape[0]
        for i in range(n // part):
            at, there = n + i * part, message.shape[1] - n // part * wide + i * wide
            low[at : at + part, :] = (y[at : at + part] + message[:, there : there + wide].astype(F32)).astype(BF)
    x = jnp.broadcast_to(gain[:, window(me, wide)], (16, wide))
    row = lax.broadcasted_iota(jnp.int32, x.shape, 0)
    top = x.astype(BF).astype(F32)
    mid = (x - top).astype(BF).astype(F32)
    low[rows:, :] = jnp.where(row == 0, top, jnp.where(row == 1, mid, jnp.where(row == 2, x - top - mid, 0.0))).astype(BF)


def norm_kernel(places, *refs):
    pieces, zs = refs[:-1], refs[-1]
    me_h, me_r = lax.axis_index("head"), lax.axis_index("rep")
    n_head = lax.axis_size("head")
    n, wide = pieces[0].shape[0] - 16, pieces[0].shape[1]
    for dg in range(lax.axis_size("groups")):
        here = [(p, dh, dr) for p, (g, dh, dr) in zip(pieces, places) if g == dg]
        norm = jnp.zeros((n, 1), F32)
        for p, _, _ in here:
            x = p[:n, :].astype(F32)
            norm = norm + jnp.sum(x * x, axis=1, keepdims=True)
        inv = lax.rsqrt(norm / zs.shape[1] + 1e-06)
        for p, dh, dr in here:
            r = lax.rem(me_r + dr, 2)
            head = lax.rem(me_h + dh, n_head)
            gain = jnp.sum(p[n:, :].astype(F32), axis=0, keepdims=True)
            zs[dg * n : (dg + 1) * n, window(head * 2 + r, wide)] = (p[:n, :].astype(F32) * inv * gain).astype(BF)


def blocks_of(mlp, width):
    if len(mlp) > 1:
        return [mlp[0]], [mlp[1]]
    deep = width // mlp[0].shape[0]
    each = range(mlp[0].shape[0])
    return [mlp[0].at[t, :deep, :] for t in each], [mlp[0].at[t, deep:, :] for t in each]


def feed(z, ups, downs, os, wait=lambda: None):
    deep = z.shape[1] // len(ups)
    total = None
    for t, x in enumerate(ups):
        term = dot(z[:, t * deep : (t + 1) * deep], x[...])
        total = term if total is None else total + term
    h = (0.5 * total * (1.0 + lax.erf(total * np.float32(0.5**0.5)))).astype(BF)
    wait()
    for t, x in enumerate(downs):
        os[:, t * deep : (t + 1) * deep] = dot(h, x[...])


def turned(os, out):
    n_head = lax.axis_size("head")
    part = os.shape[1] // n_head
    for dh in range(n_head):
        cols = window(lax.rem(lax.axis_index("head") + dh, n_head), part)
        out[:, dh * part : (dh + 1) * part] = os[:, cols].astype(out.dtype)


def theirs_kernel(n_mlp, *refs):
    far, (zs, send, *near), (os, sems) = refs[:n_mlp], refs[n_mlp:-2], refs[-2:]
    width = zs.shape[1]
    pairs = [p for f, n in zip(blocks_of(far, width), blocks_of(near, width)) for p in zip(f, n)]
    copies = fetch(pairs, sems)
    ups, downs = blocks_of(near, width)
    for c in copies[: len(ups)]:
        c.wait()

    def rest():
        for c in copies[len(ups) :]:
            c.wait()

    rows = send.shape[0]
    feed(zs[window(1 - lax.axis_index("rep"), rows), :], ups, downs, os, rest)
    turned(os, send)


def ours_kernel(zs, *refs):
    *mlp, own, os = refs
    ups, downs = blocks_of(mlp, zs.shape[1])
    feed(zs[window(lax.axis_index("rep"), own.shape[0]), :], ups, downs, os)
    turned(os, own)


def pair_kernel(moves, own, got, *outs):
    n, wide = outs[0].shape
    for (dz, dh), out in zip(moves, outs):
        rows, cols = slice(dz * n, (dz + 1) * n), slice(dh * wide, (dh + 1) * wide)
        out[...] = (own[rows, cols] + got[rows, cols].astype(F32)).astype(BF)


def sum_kernel(*refs):
    *parts, mixed, keep, send, acc = refs
    total = parts[0][...].astype(F32)
    for p in parts[1:]:
        total = total + p[...].astype(F32)
    acc[...] = total
    me, wide = lax.axis_index("rep"), keep.shape[1]
    keep[...] = mixed[...] + acc[:, window(me, wide)]
    send[...] = acc[:, window(1 - me, wide)].astype(BF)


def dealt(x, tok, head):
    axes = ("groups", "tok", "head", "rep")
    sizes = [lax.axis_size(a) for a in axes]
    pairs = []
    for here in range(int(np.prod(sizes))):
        g, t, h, r = np.unravel_index(here, sizes)
        there = ((g + r) % sizes[0], t ^ tok, (h + head) % sizes[2], r)
        pairs.append((here, int(np.ravel_multi_index(there, sizes))))
    return lax.ppermute(x, axes, pairs)


def on_device(
    keys, values, rates, queries, stream, gain, counts, fw_one, fw_three, fw_two, mlp_up, mlp_down
):
    n_tok, n_head = lax.axis_size("tok"), lax.axis_size("head")
    groups, reps = lax.axis_size("groups"), lax.axis_size("rep")
    dh, n_key, n = keys.shape[1], keys.shape[0], queries.shape[0]
    wide = dh // reps
    paired = n_tok == 4 and n_key == n
    near = 2 if paired else 1
    units = mlp_up.shape[1] // groups // near
    barrier = lax.optimization_barrier

    rows = n_key // reps
    rate_row, gain = rates.reshape(1, n_key), gain[None, :]
    sources = [keys, values, rate_row]
    outs = [shape((n_key, 2 * dh), BF)]
    if paired:
        sources += [queries, stream]
        outs = [shape((rows, 2 * dh), BF), shape((rows, 4 * dh), BF)]
    messages = call(
        functools.partial(message_kernel, len(sources)),
        outs,
        sources,
        [*local(sources), pltpu.VMEM((n_key, 2 * dh), BF), pltpu.SemaphoreType.DMA((len(sources),))],
        fetched=len(sources),
    )
    asks = []
    if paired:
        share, full = messages
        others = [moved(full, tok=1), moved(share, tok=2), moved(share, tok=3)]
        (blocks,) = call(
            pack_kernel, [shape((n_tok, mlp_up.shape[0] + units, units), BF)], [mlp_up, mlp_down]
        )
        others, blocks = barrier((others, blocks))
        mlp = [lax.all_to_all(blocks, "tok", 0, 0)]
        tokens = [*others, *[moved(x, rep=1) for x in others]]
        asks = others[:1]
    else:
        me_g = lax.axis_index("groups")
        up_own = lax.dynamic_slice_in_dim(mlp_up, me_g * units, units, 1)
        down_own = lax.dynamic_slice_in_dim(mlp_down, me_g * units, units, 0)
        tokens = [lax.all_gather(messages[0], "tok", axis=0, tiled=True)]
        mlp = [
            lax.all_gather(up_own, "tok", axis=0, tiled=True),
            lax.all_gather(down_own, "tok", axis=1, tiled=True),
        ]

    n_all = sum(x.shape[0] for x in tokens) + (n_key if paired else 0)
    tokens = barrier(tokens)
    sources = [fw_one[0], fw_three[0], fw_two[0], keys, values, rate_row, queries]
    own, own_sq, send = call(
        functools.partial(fast_kernel, len(tokens), near),
        [shape((near * n, wide), F32), shape((8, wide), F32), shape((near * n + 16, wide), BF)],
        [*sources, *tokens],
        [
            pltpu.VMEM((n_all, dh), BF),
            pltpu.VMEM((n_all, dh), BF),
            pltpu.VMEM((near * n, dh), F32),
            pltpu.VMEM((near * n, dh), BF),
            pltpu.VMEM((n_key, 2 * dh), BF),
            *local(sources),
            pltpu.SemaphoreType.DMA((len(sources),)),
        ],
        fetched=len(sources),
    )
    got = moved(send, rep=1)
    sources = [stream, gain]
    mixed, low = call(
        mix_kernel,
        [shape((n, wide), F32), shape((near * n + 16, wide), BF)],
        [*sources, own, own_sq, got, *asks],
        [*local(sources), pltpu.SemaphoreType.DMA((2,))],
        fetched=2,
    )
    pieces, places = [], []
    for dg, h in itertools.product(range(groups), range(n_head)):
        x = moved(low, groups=dg, head=h)
        pieces += [x, moved(x, rep=1)]
        places += [(dg, h, 0), (dg, h, 1)]
    model = n_head * dh
    (zs,) = call(
        functools.partial(norm_kernel, places), [shape((groups * near * n, model), BF)], pieces
    )
    send, *mlp = call(
        functools.partial(theirs_kernel, len(mlp)),
        [shape((near * n, model), BF), *[shape(x.shape, BF) for x in mlp]],
        [*mlp, zs],
        [pltpu.VMEM((near * n, model), F32), pltpu.SemaphoreType.DMA((2 * n_tok if paired else 2,))],
        unmoved=len(mlp),
    )
    got = moved(send, rep=1)
    (own,) = call(
        ours_kernel, [shape((near * n, model), F32)], [zs, *mlp], [pltpu.VMEM((near * n, model), F32)]
    )
    moves = list(itertools.product(range(near), range(n_head)))
    parts = call(
        functools.partial(pair_kernel, moves), [shape((n, dh), BF)] * len(moves), [own, got]
    )
    parts = [dealt(x, *m) for m, x in zip(moves, parts)]
    keep, send = call(
        sum_kernel, [shape((n, wide), F32), shape((n, wide), BF)], [*parts, mixed], [pltpu.VMEM((n, dh), F32)]
    )
    total = keep + moved(send, rep=1).astype(F32)
    live = jnp.arange(n, dtype=jnp.int32) < counts[0]
    return jnp.where(live[:, None], total, 0.0).astype(BF)


def solution(mesh):
    placed = (
        P(("groups", "tok"), "head"),
        P(("groups", "tok"), "head"),
        P(("groups", "tok"), "head"),
        P(("groups", "tok"), "head"),
        P(("groups", "tok"), "head"),
        P("head"),
        P(("groups", "tok")),
        P("head", None, "rep"),
        P("head", None, "rep"),
        P("head", "rep", None),
        P("tok", ("head", "rep")),
        P(("head", "rep"), "tok"),
    )
    return jax.shard_map(
        on_device,
        mesh=mesh,
        in_specs=placed,
        out_specs=P(("groups", "tok"), ("head", "rep")),
        check_vma=False,
    )
```

```python
import functools
import itertools

import jax
import jax.numpy as jnp
import numpy as np
from jax import lax
from jax.experimental import pallas as pl
from jax.experimental.pallas import tpu as pltpu
from jax.sharding import PartitionSpec as P

BF, F32 = jnp.bfloat16, jnp.float32


def dot(a, b, dims=((1,), (0,))):
    return lax.dot_general(a, b, (dims, ((), ())), preferred_element_type=F32)


def moved(x, groups=0, tok=0, head=0, rep=0):
    shifts = {"groups": groups, "tok": tok, "head": head, "rep": rep}
    axes = [a for a, s in shifts.items() if s]
    if not axes:
        return x
    sizes = [lax.axis_size(a) for a in axes]
    pairs = []
    for here in range(int(np.prod(sizes))):
        at = np.unravel_index(here, sizes)
        there = [i ^ tok if a == "tok" else (i + shifts[a]) % n for a, i, n in zip(axes, at, sizes)]
        pairs.append((int(np.ravel_multi_index(there, sizes)), here))
    return lax.ppermute(x, tuple(axes), pairs)


def shape(dims, dtype):
    return jax.ShapeDtypeStruct(dims, dtype)


def call(kernel, outs, args, scratch=(), fetched=0, unmoved=0):
    touched = sum(int(np.prod(x.shape)) * x.dtype.itemsize for x in (*args, *outs))
    kept = sum(int(np.prod(x.shape)) * 4 for x in scratch if hasattr(x, "shape"))
    args = [pltpu.with_memory_space_constraint(x, pltpu.HBM) if i < fetched else x for i, x in enumerate(args)]
    return pl.pallas_call(
        kernel,
        out_shape=outs,
        in_specs=[pl.BlockSpec(memory_space=pltpu.HBM if i < fetched + unmoved else pltpu.VMEM) for i in range(len(args))],
        out_specs=[pl.BlockSpec(memory_space=pltpu.VMEM)] * len(outs),
        scratch_shapes=list(scratch),
        compiler_params=pltpu.CompilerParams(vmem_limit_bytes=touched + kept + (10 << 20)),
        cost_estimate=pl.CostEstimate(flops=1, bytes_accessed=1, transcendentals=0),
    )(*args)


def local(arrays):
    return [pltpu.VMEM(x.shape, x.dtype) for x in arrays]


def window(index, size):
    return pl.ds(pl.multiple_of(index * size, size), size)


def fetch(pairs, sems):
    copies = [pltpu.make_async_copy(src, dst, sems.at[i]) for i, (src, dst) in enumerate(pairs)]
    for c in copies:
        c.start()
    return copies


def side_by_side(pair, keys, values, rates):
    n, dh = keys.shape
    pair[:, :dh] = keys[...]
    rate = jnp.broadcast_to(rates[...], (128, n)).T
    for c in range(0, dh, 128):
        pair[:, dh + c : dh + c + 128] = (values[:, c : c + 128].astype(F32) * rate).astype(BF)


def message_kernel(n_far, *refs):
    far, refs = refs[:n_far], refs[n_far:]
    outs, near, (pair, sems) = refs[: -n_far - 2], refs[-n_far - 2 : -2], refs[-2:]
    for c in fetch(list(zip(far, near)), sems):
        c.wait()
    side_by_side(pair, *near[:3])
    if len(outs) == 1:
        outs[0][...] = pair[...]
        return
    share, full = outs
    q, s = near[3:]
    me, (rows, width) = lax.axis_index("rep"), share.shape
    part = pair[window(me, rows), :]
    share[...] = part
    full[:, :width] = part
    dh = width // 2
    full[:, width : width + dh] = q[window(me, rows), :]
    wide = dh // 2
    for i in range(q.shape[0] // rows):
        at = width + dh + i * wide
        full[:, at : at + wide] = s[i * rows : (i + 1) * rows, window(me, wide)]


def pack_kernel(up, down, out):
    deep, wide = up.shape[0], out.shape[2]
    for t in range(out.shape[0]):
        part = window(lax.axis_index("groups") * 2 + t % 2, wide)
        out[t, :deep, :] = up[:, part]
        out[t, deep:, :] = down[part, :]


def gradients(k, e, w1b, w3b, w2b):
    a1, a3, b = dot(k, w1b), dot(k, w3b), dot(e, w2b, ((1,), (1,)))
    sig = jax.nn.sigmoid(a1)
    act = a1 * sig
    g = (act * a3).astype(BF)
    r1 = (b * a3 * (sig * (1.0 + a1 * (1.0 - sig)))).astype(BF)
    r3 = (b * act).astype(BF)
    first = ((0,), (0,))
    return dot(k, r1, first), dot(k, r3, first), dot(g, e, first)


def squares(x):
    return jnp.sum(x * x, axis=0, keepdims=True)


def fast_kernel(n_pieces, near, *refs):
    far, refs = refs[:7], refs[7:]
    pieces, refs = refs[:n_pieces], refs[n_pieces:]
    own_out, own_sq, send, ks, es, hp, qs, pair, *local, sems = refs
    w1, w3, w2, keys, values, rates, q = local
    copies = fetch(list(zip(far, local)), sems)
    dh, hidden = w1.shape
    me = lax.axis_index("rep")
    n = q.shape[0]
    at = 0
    for p in pieces:
        rows = p.shape[0]
        ks[at : at + rows, :] = p[:, :dh]
        es[at : at + rows, :] = p[:, dh : 2 * dh]
        at += rows
    if near > 1:
        mine, theirs = pieces[0], pieces[n_pieces // 2]
        rows = mine.shape[0]
        qs[pl.ds(pl.multiple_of(n + me * rows, rows), rows), :] = mine[:, 2 * dh : 3 * dh]
        qs[pl.ds(pl.multiple_of(n + (1 - me) * rows, rows), rows), :] = theirs[:, 2 * dh : 3 * dh]
    for c in copies[3:]:
        c.wait()
    if near > 1:
        side_by_side(pair, keys, values, rates)
        ks[at : at + n, :] = pair[:, :dh]
        es[at : at + n, :] = pair[:, dh:]
        at += n
    qs[:n, :] = q[...]
    asked = qs[...]
    tokens, step, block = at, min(at, 512), min(hidden, 256)
    for c in copies[:3]:
        c.wait()
    old_sq = squares(w2[...])
    new_sq = jnp.zeros((1, dh), F32)
    for j in range(0, hidden, block):
        js = slice(j, j + block)
        x1, x3, x2 = w1[:, js], w3[:, js], w2[js, :]
        b1, b3, b2 = x1.astype(BF), x3.astype(BF), x2.astype(BF)

        def add(i, sums):
            rows = pl.ds(pl.multiple_of(i * step, step), step)
            return tuple(s + p for s, p in zip(sums, gradients(ks[rows, :], es[rows, :], b1, b3, b2)))

        sums = (x1, x3, x2)
        sums = add(0, sums) if tokens == step else lax.fori_loop(0, tokens // step, add, sums)

        def normed(old, new):
            return (new * (jnp.sqrt(squares(old)) * lax.rsqrt(squares(new) + 1e-06))).astype(BF)

        new_sq = new_sq + squares(sums[2])
        qa, qc = dot(asked, normed(x1, sums[0])), dot(asked, normed(x3, sums[1]))
        part = dot((qa * jax.nn.sigmoid(qa) * qc).astype(BF), sums[2].astype(BF))
        hp[...] = part if j == 0 else hp[...] + part
    rows, wide = own_out.shape
    own_out[...] = hp[:, window(me, wide)]
    send[:rows, :] = hp[:, window(1 - me, wide)].astype(BF)
    row = lax.broadcasted_iota(jnp.int32, (8, dh), 0)
    hp[:8, :] = jnp.where(row == 0, old_sq, jnp.where(row == 1, new_sq, 0.0))
    own_sq[...] = hp[:8, window(me, wide)]
    sq = hp[:8, window(1 - me, wide)]
    top = sq.astype(BF).astype(F32)
    send[rows:, :] = jnp.concatenate([top, sq - top], axis=0).astype(BF)


def mix_kernel(stream_far, gain_far, own, own_sq, got, *refs):
    *asks, mixed, low, stream, gain, sems = refs
    copies = fetch([(stream_far, stream), (gain_far, gain)], sems)
    n, wide = mixed.shape
    rows, me = own.shape[0], lax.axis_index("rep")
    tail = got[rows:, :].astype(F32)
    sq = own_sq[...] + tail[:8] + tail[8:]
    y = (own[...] + got[:rows, :].astype(F32)) * (jnp.sqrt(sq[0:1]) * lax.rsqrt(sq[1:2] + 1e-06))
    for c in copies:
        c.wait()
    mixed[...] = y[:n] + stream[:, window(me, wide)].astype(F32)
    low[:n, :] = mixed[...].astype(BF)
    for message in asks:
        part = message.shape[0]
        for i in range(n // part):
            at, there = n + i * part, message.shape[1] - n // part * wide + i * wide
            low[at : at + part, :] = (y[at : at + part] + message[:, there : there + wide].astype(F32)).astype(BF)
    x = jnp.broadcast_to(gain[:, window(me, wide)], (16, wide))
    row = lax.broadcasted_iota(jnp.int32, x.shape, 0)
    top = x.astype(BF).astype(F32)
    mid = (x - top).astype(BF).astype(F32)
    low[rows:, :] = jnp.where(row == 0, top, jnp.where(row == 1, mid, jnp.where(row == 2, x - top - mid, 0.0))).astype(BF)


def norm_kernel(places, *refs):
    pieces, zs = refs[:-1], refs[-1]
    me_h, me_r = lax.axis_index("head"), lax.axis_index("rep")
    n_head = lax.axis_size("head")
    n, wide = pieces[0].shape[0] - 16, pieces[0].shape[1]
    for dg in range(lax.axis_size("groups")):
        here = [(p, dh, dr) for p, (g, dh, dr) in zip(pieces, places) if g == dg]
        norm = jnp.zeros((n, 1), F32)
        for p, _, _ in here:
            x = p[:n, :].astype(F32)
            norm = norm + jnp.sum(x * x, axis=1, keepdims=True)
        inv = lax.rsqrt(norm / zs.shape[1] + 1e-06)
        for p, dh, dr in here:
            r = lax.rem(me_r + dr, 2)
            head = lax.rem(me_h + dh, n_head)
            gain = jnp.sum(p[n:, :].astype(F32), axis=0, keepdims=True)
            zs[dg * n : (dg + 1) * n, window(head * 2 + r, wide)] = (p[:n, :].astype(F32) * inv * gain).astype(BF)


def blocks_of(mlp, width):
    if len(mlp) > 1:
        return [mlp[0]], [mlp[1]]
    deep = width // mlp[0].shape[0]
    each = range(mlp[0].shape[0])
    return [mlp[0].at[t, :deep, :] for t in each], [mlp[0].at[t, deep:, :] for t in each]


def feed(z, ups, downs, os, wait=lambda: None):
    deep = z.shape[1] // len(ups)
    total = None
    for t, x in enumerate(ups):
        term = dot(z[:, t * deep : (t + 1) * deep], x[...])
        total = term if total is None else total + term
    h = (0.5 * total * (1.0 + lax.erf(total * np.float32(0.5**0.5)))).astype(BF)
    wait()
    for t, x in enumerate(downs):
        os[:, t * deep : (t + 1) * deep] = dot(h, x[...])


def turned(os, out):
    n_head = lax.axis_size("head")
    part = os.shape[1] // n_head
    for dh in range(n_head):
        cols = window(lax.rem(lax.axis_index("head") + dh, n_head), part)
        out[:, dh * part : (dh + 1) * part] = os[:, cols].astype(out.dtype)


def theirs_kernel(n_mlp, *refs):
    far, (zs, send, *near), (os, sems) = refs[:n_mlp], refs[n_mlp:-2], refs[-2:]
    width = zs.shape[1]
    pairs = [p for f, n in zip(blocks_of(far, width), blocks_of(near, width)) for p in zip(f, n)]
    copies = fetch(pairs, sems)
    ups, downs = blocks_of(near, width)
    for c in copies[: len(ups)]:
        c.wait()

    def rest():
        for c in copies[len(ups) :]:
            c.wait()

    rows = send.shape[0]
    feed(zs[window(1 - lax.axis_index("rep"), rows), :], ups, downs, os, rest)
    turned(os, send)


def ours_kernel(zs, *refs):
    *mlp, own, os = refs
    ups, downs = blocks_of(mlp, zs.shape[1])
    feed(zs[window(lax.axis_index("rep"), own.shape[0]), :], ups, downs, os)
    turned(os, own)


def pair_kernel(moves, own, got, *outs):
    n, wide = outs[0].shape
    for (dz, dh), out in zip(moves, outs):
        rows, cols = slice(dz * n, (dz + 1) * n), slice(dh * wide, (dh + 1) * wide)
        out[...] = (own[rows, cols] + got[rows, cols].astype(F32)).astype(BF)


def sum_kernel(*refs):
    *parts, mixed, keep, send, acc = refs
    total = parts[0][...].astype(F32)
    for p in parts[1:]:
        total = total + p[...].astype(F32)
    acc[...] = total
    me, wide = lax.axis_index("rep"), keep.shape[1]
    keep[...] = mixed[...] + acc[:, window(me, wide)]
    send[...] = acc[:, window(1 - me, wide)].astype(BF)


def dealt(x, tok, head):
    axes = ("groups", "tok", "head", "rep")
    sizes = [lax.axis_size(a) for a in axes]
    pairs = []
    for here in range(int(np.prod(sizes))):
        g, t, h, r = np.unravel_index(here, sizes)
        there = ((g + r) % sizes[0], t ^ tok, (h + head) % sizes[2], r)
        pairs.append((here, int(np.ravel_multi_index(there, sizes))))
    return lax.ppermute(x, axes, pairs)


def on_device(
    keys, values, rates, queries, stream, gain, counts, fw_one, fw_three, fw_two, mlp_up, mlp_down
):
    n_tok, n_head = lax.axis_size("tok"), lax.axis_size("head")
    groups, reps = lax.axis_size("groups"), lax.axis_size("rep")
    dh, n_key, n = keys.shape[1], keys.shape[0], queries.shape[0]
    wide = dh // reps
    paired = n_tok == 4 and n_key == n
    near = 2 if paired else 1
    units = mlp_up.shape[1] // groups // near
    barrier = lax.optimization_barrier

    rows = n_key // reps
    rate_row, gain = rates.reshape(1, n_key), gain[None, :]
    sources = [keys, values, rate_row]
    outs = [shape((n_key, 2 * dh), BF)]
    if paired:
        sources += [queries, stream]
        outs = [shape((rows, 2 * dh), BF), shape((rows, 4 * dh), BF)]
    messages = call(
        functools.partial(message_kernel, len(sources)),
        outs,
        sources,
        [*local(sources), pltpu.VMEM((n_key, 2 * dh), BF), pltpu.SemaphoreType.DMA((len(sources),))],
        fetched=len(sources),
    )
    asks = []
    if paired:
        share, full = messages
        others = [moved(full, tok=1), moved(share, tok=2), moved(share, tok=3)]
        (blocks,) = call(
            pack_kernel, [shape((n_tok, mlp_up.shape[0] + units, units), BF)], [mlp_up, mlp_down]
        )
        others, blocks = barrier((others, blocks))
        mlp = [lax.all_to_all(blocks, "tok", 0, 0)]
        tokens = [*others, *[moved(x, rep=1) for x in others]]
        asks = others[:1]
    else:
        me_g = lax.axis_index("groups")
        up_own = lax.dynamic_slice_in_dim(mlp_up, me_g * units, units, 1)
        down_own = lax.dynamic_slice_in_dim(mlp_down, me_g * units, units, 0)
        tokens = [lax.all_gather(messages[0], "tok", axis=0, tiled=True)]
        mlp = [
            lax.all_gather(up_own, "tok", axis=0, tiled=True),
            lax.all_gather(down_own, "tok", axis=1, tiled=True),
        ]

    n_all = sum(x.shape[0] for x in tokens) + (n_key if paired else 0)
    tokens = barrier(tokens)
    sources = [fw_one[0], fw_three[0], fw_two[0], keys, values, rate_row, queries]
    own, own_sq, send = call(
        functools.partial(fast_kernel, len(tokens), near),
        [shape((near * n, wide), F32), shape((8, wide), F32), shape((near * n + 16, wide), BF)],
        [*sources, *tokens],
        [
            pltpu.VMEM((n_all, dh), BF),
            pltpu.VMEM((n_all, dh), BF),
            pltpu.VMEM((near * n, dh), F32),
            pltpu.VMEM((near * n, dh), BF),
            pltpu.VMEM((n_key, 2 * dh), BF),
            *local(sources),
            pltpu.SemaphoreType.DMA((len(sources),)),
        ],
        fetched=len(sources),
    )
    got = moved(send, rep=1)
    sources = [stream, gain]
    mixed, low = call(
        mix_kernel,
        [shape((n, wide), F32), shape((near * n + 16, wide), BF)],
        [*sources, own, own_sq, got, *asks],
        [*local(sources), pltpu.SemaphoreType.DMA((2,))],
        fetched=2,
    )
    pieces, places = [], []
    for dg, h in itertools.product(range(groups), range(n_head)):
        x = moved(low, groups=dg, head=h)
        pieces += [x, moved(x, rep=1)]
        places += [(dg, h, 0), (dg, h, 1)]
    model = n_head * dh
    (zs,) = call(
        functools.partial(norm_kernel, places), [shape((groups * near * n, model), BF)], pieces
    )
    send, *mlp = call(
        functools.partial(theirs_kernel, len(mlp)),
        [shape((near * n, model), BF), *[shape(x.shape, BF) for x in mlp]],
        [*mlp, zs],
        [pltpu.VMEM((near * n, model), F32), pltpu.SemaphoreType.DMA((2 * n_tok if paired else 2,))],
        unmoved=len(mlp),
    )
    got = moved(send, rep=1)
    (own,) = call(
        ours_kernel, [shape((near * n, model), F32)], [zs, *mlp], [pltpu.VMEM((near * n, model), F32)]
    )
    moves = sorted(itertools.product(range(near), range(n_head)), key=lambda m: (-m[0] - m[1], m[0]))
    parts = call(
        functools.partial(pair_kernel, moves), [shape((n, dh), BF)] * len(moves), [own, got]
    )
    parts = [dealt(x, *m) for m, x in zip(moves, parts)]
    keep, send = call(
        sum_kernel, [shape((n, wide), F32), shape((n, wide), BF)], [*parts, mixed], [pltpu.VMEM((n, dh), F32)]
    )
    total = keep + moved(send, rep=1).astype(F32)
    live = jnp.arange(n, dtype=jnp.int32) < counts[0]
    return jnp.where(live[:, None], total, 0.0).astype(BF)


def solution(mesh):
    placed = (
        P(("groups", "tok"), "head"),
        P(("groups", "tok"), "head"),
        P(("groups", "tok"), "head"),
        P(("groups", "tok"), "head"),
        P(("groups", "tok"), "head"),
        P("head"),
        P(("groups", "tok")),
        P("head", None, "rep"),
        P("head", None, "rep"),
        P("head", "rep", None),
        P("tok", ("head", "rep")),
        P(("head", "rep"), "tok"),
    )
    return jax.shard_map(
        on_device,
        mesh=mesh,
        in_specs=placed,
        out_specs=P(("groups", "tok"), ("head", "rep")),
        check_vma=False,
    )
```

```python
import functools
import itertools

import jax
import jax.numpy as jnp
import numpy as np
from jax import lax
from jax.experimental import pallas as pl
from jax.experimental.pallas import tpu as pltpu
from jax.sharding import PartitionSpec as P

BF, F32 = jnp.bfloat16, jnp.float32


def dot(a, b, dims=((1,), (0,))):
    return lax.dot_general(a, b, (dims, ((), ())), preferred_element_type=F32)


def moved(x, groups=0, tok=0, head=0, rep=0):
    shifts = {"groups": groups, "tok": tok, "head": head, "rep": rep}
    axes = [a for a, s in shifts.items() if s]
    if not axes:
        return x
    sizes = [lax.axis_size(a) for a in axes]
    pairs = []
    for here in range(int(np.prod(sizes))):
        at = np.unravel_index(here, sizes)
        there = [i ^ tok if a == "tok" else (i + shifts[a]) % n for a, i, n in zip(axes, at, sizes)]
        pairs.append((int(np.ravel_multi_index(there, sizes)), here))
    return lax.ppermute(x, tuple(axes), pairs)


def shape(dims, dtype):
    return jax.ShapeDtypeStruct(dims, dtype)


def call(kernel, outs, args, scratch=(), fetched=0, unmoved=0):
    touched = sum(int(np.prod(x.shape)) * x.dtype.itemsize for x in (*args, *outs))
    kept = sum(int(np.prod(x.shape)) * 4 for x in scratch if hasattr(x, "shape"))
    args = [pltpu.with_memory_space_constraint(x, pltpu.HBM) if i < fetched else x for i, x in enumerate(args)]
    return pl.pallas_call(
        kernel,
        out_shape=outs,
        in_specs=[pl.BlockSpec(memory_space=pltpu.HBM if i < fetched + unmoved else pltpu.VMEM) for i in range(len(args))],
        out_specs=[pl.BlockSpec(memory_space=pltpu.VMEM)] * len(outs),
        scratch_shapes=list(scratch),
        compiler_params=pltpu.CompilerParams(vmem_limit_bytes=touched + kept + (10 << 20)),
        cost_estimate=pl.CostEstimate(flops=1, bytes_accessed=1, transcendentals=0),
    )(*args)


def local(arrays):
    return [pltpu.VMEM(x.shape, x.dtype) for x in arrays]


def window(index, size):
    return pl.ds(pl.multiple_of(index * size, size), size)


def fetch(pairs, sems):
    copies = [pltpu.make_async_copy(src, dst, sems.at[i]) for i, (src, dst) in enumerate(pairs)]
    for c in copies:
        c.start()
    return copies


def side_by_side(pair, keys, values, rates):
    n, dh = keys.shape
    pair[:, :dh] = keys[...]
    rate = jnp.broadcast_to(rates[...], (128, n)).T
    for c in range(0, dh, 128):
        pair[:, dh + c : dh + c + 128] = (values[:, c : c + 128].astype(F32) * rate).astype(BF)


def message_kernel(n_far, *refs):
    far, refs = refs[:n_far], refs[n_far:]
    outs, near, (pair, sems) = refs[: -n_far - 2], refs[-n_far - 2 : -2], refs[-2:]
    for c in fetch(list(zip(far, near)), sems):
        c.wait()
    side_by_side(pair, *near[:3])
    if len(outs) == 1:
        outs[0][...] = pair[...]
        return
    share, full = outs
    q, s = near[3:]
    me, (rows, width) = lax.axis_index("rep"), share.shape
    part = pair[window(me, rows), :]
    share[...] = part
    full[:, :width] = part
    dh = width // 2
    full[:, width : width + dh] = q[window(me, rows), :]
    wide = dh // 2
    for i in range(q.shape[0] // rows):
        at = width + dh + i * wide
        full[:, at : at + wide] = s[i * rows : (i + 1) * rows, window(me, wide)]


def pack_kernel(up, down, out):
    deep, wide = up.shape[0], out.shape[2]
    for t in range(out.shape[0]):
        part = window(lax.axis_index("groups") * 2 + t % 2, wide)
        out[t, :deep, :] = up[:, part]
        out[t, deep:, :] = down[part, :]


def gradients(k, e, w1b, w3b, w2b):
    a1, a3, b = dot(k, w1b), dot(k, w3b), dot(e, w2b, ((1,), (1,)))
    sig = jax.nn.sigmoid(a1)
    act = a1 * sig
    g = (act * a3).astype(BF)
    r1 = (b * a3 * (sig * (1.0 + a1 * (1.0 - sig)))).astype(BF)
    r3 = (b * act).astype(BF)
    first = ((0,), (0,))
    return dot(k, r1, first), dot(k, r3, first), dot(g, e, first)


def squares(x):
    return jnp.sum(x * x, axis=0, keepdims=True)


def fast_kernel(n_pieces, near, *refs):
    far, refs = refs[:9], refs[9:]
    pieces, refs = refs[:n_pieces], refs[n_pieces:]
    own_out, own_sq, send, base, gains, ks, es, hp, qs, pair, *local, sems = refs
    w1, w3, w2, keys, values, rates, q, stream, gain = local
    copies = fetch(list(zip(far, local)), sems)
    dh, hidden = w1.shape
    me = lax.axis_index("rep")
    n = q.shape[0]
    at = 0
    for p in pieces:
        rows = p.shape[0]
        ks[at : at + rows, :] = p[:, :dh]
        es[at : at + rows, :] = p[:, dh : 2 * dh]
        at += rows
    if near > 1:
        mine, theirs = pieces[0], pieces[n_pieces // 2]
        rows = mine.shape[0]
        qs[pl.ds(pl.multiple_of(n + me * rows, rows), rows), :] = mine[:, 2 * dh : 3 * dh]
        qs[pl.ds(pl.multiple_of(n + (1 - me) * rows, rows), rows), :] = theirs[:, 2 * dh : 3 * dh]
    for c in copies[3:]:
        c.wait()
    if near > 1:
        side_by_side(pair, keys, values, rates)
        ks[at : at + n, :] = pair[:, :dh]
        es[at : at + n, :] = pair[:, dh:]
        at += n
    qs[:n, :] = q[...]
    asked = qs[...]
    tokens, step, block = at, min(at, 512), min(hidden, 256)
    for c in copies[:3]:
        c.wait()
    old_sq = squares(w2[...])
    new_sq = jnp.zeros((1, dh), F32)
    for j in range(0, hidden, block):
        js = slice(j, j + block)
        x1, x3, x2 = w1[:, js], w3[:, js], w2[js, :]
        b1, b3, b2 = x1.astype(BF), x3.astype(BF), x2.astype(BF)

        def add(i, sums):
            rows = pl.ds(pl.multiple_of(i * step, step), step)
            return tuple(s + p for s, p in zip(sums, gradients(ks[rows, :], es[rows, :], b1, b3, b2)))

        sums = (x1, x3, x2)
        sums = add(0, sums) if tokens == step else lax.fori_loop(0, tokens // step, add, sums)

        def normed(old, new):
            return (new * (jnp.sqrt(squares(old)) * lax.rsqrt(squares(new) + 1e-06))).astype(BF)

        new_sq = new_sq + squares(sums[2])
        qa, qc = dot(asked, normed(x1, sums[0])), dot(asked, normed(x3, sums[1]))
        part = dot((qa * jax.nn.sigmoid(qa) * qc).astype(BF), sums[2].astype(BF))
        hp[...] = part if j == 0 else hp[...] + part
    rows, wide = own_out.shape
    base[...] = stream[:, window(me, wide)]
    x = jnp.broadcast_to(gain[:, window(me, wide)], gains.shape)
    row = lax.broadcasted_iota(jnp.int32, x.shape, 0)
    top = x.astype(BF).astype(F32)
    mid = (x - top).astype(BF).astype(F32)
    gains[...] = jnp.where(row == 0, top, jnp.where(row == 1, mid, jnp.where(row == 2, x - top - mid, 0.0))).astype(BF)
    own_out[...] = hp[:, window(me, wide)]
    send[:rows, :] = hp[:, window(1 - me, wide)].astype(BF)
    row = lax.broadcasted_iota(jnp.int32, (8, dh), 0)
    hp[:8, :] = jnp.where(row == 0, old_sq, jnp.where(row == 1, new_sq, 0.0))
    own_sq[...] = hp[:8, window(me, wide)]
    sq = hp[:8, window(1 - me, wide)]
    top = sq.astype(BF).astype(F32)
    send[rows:, :] = jnp.concatenate([top, sq - top], axis=0).astype(BF)


def mix_kernel(own, own_sq, got, base, gains, *refs):
    *asks, mixed, low = refs
    n, wide = mixed.shape
    rows = own.shape[0]
    tail = got[rows:, :].astype(F32)
    sq = own_sq[...] + tail[:8] + tail[8:]
    y = (own[...] + got[:rows, :].astype(F32)) * (jnp.sqrt(sq[0:1]) * lax.rsqrt(sq[1:2] + 1e-06))
    mixed[...] = y[:n] + base[...].astype(F32)
    low[:n, :] = mixed[...].astype(BF)
    for message in asks:
        part = message.shape[0]
        for i in range(n // part):
            at, there = n + i * part, message.shape[1] - n // part * wide + i * wide
            low[at : at + part, :] = (y[at : at + part] + message[:, there : there + wide].astype(F32)).astype(BF)
    low[rows:, :] = gains[...]


def norm_kernel(places, *refs):
    pieces, zs = refs[:-1], refs[-1]
    me_h, me_r = lax.axis_index("head"), lax.axis_index("rep")
    n_head = lax.axis_size("head")
    n, wide = pieces[0].shape[0] - 16, pieces[0].shape[1]
    for dg in range(lax.axis_size("groups")):
        here = [(p, dh, dr) for p, (g, dh, dr) in zip(pieces, places) if g == dg]
        norm = jnp.zeros((n, 1), F32)
        for p, _, _ in here:
            x = p[:n, :].astype(F32)
            norm = norm + jnp.sum(x * x, axis=1, keepdims=True)
        inv = lax.rsqrt(norm / zs.shape[1] + 1e-06)
        for p, dh, dr in here:
            r = lax.rem(me_r + dr, 2)
            head = lax.rem(me_h + dh, n_head)
            gain = jnp.sum(p[n:, :].astype(F32), axis=0, keepdims=True)
            zs[dg * n : (dg + 1) * n, window(head * 2 + r, wide)] = (p[:n, :].astype(F32) * inv * gain).astype(BF)


def blocks_of(mlp, width):
    if len(mlp) > 1:
        return [mlp[0]], [mlp[1]]
    deep = width // mlp[0].shape[0]
    each = range(mlp[0].shape[0])
    return [mlp[0].at[t, :deep, :] for t in each], [mlp[0].at[t, deep:, :] for t in each]


def feed(z, ups, downs, out):
    n_head = lax.axis_size("head")
    part = z.shape[1] // n_head
    deep = z.shape[1] // len(ups)
    wide = min(deep, part)
    total = None
    for t, x in enumerate(ups):
        term = dot(z[:, t * deep : (t + 1) * deep], x[...])
        total = term if total is None else total + term
    h = (0.5 * total * (1.0 + lax.erf(total * np.float32(0.5**0.5)))).astype(BF)
    for t, x in enumerate(downs):
        for c in range(0, deep, wide):
            head, at = divmod(t * deep + c, part)
            place = lax.rem(head - lax.axis_index("head") + n_head, n_head) * part + at
            out[:, pl.ds(pl.multiple_of(place, wide), wide)] = dot(h, x[:, c : c + wide]).astype(out.dtype)


def feed_kernel(ours, zs, *refs):
    *mlp, out = refs
    ups, downs = blocks_of(mlp, zs.shape[1])
    me = lax.axis_index("rep")
    feed(zs[window(me if ours else 1 - me, out.shape[0]), :], ups, downs, out)


def pair_kernel(moves, own, got, *outs):
    n, wide = outs[0].shape
    for (dz, dh), out in zip(moves, outs):
        rows, cols = slice(dz * n, (dz + 1) * n), slice(dh * wide, (dh + 1) * wide)
        out[...] = (own[rows, cols] + got[rows, cols].astype(F32)).astype(BF)


def sum_kernel(*refs):
    *parts, mixed, keep, send, acc = refs
    total = parts[0][...].astype(F32)
    for p in parts[1:]:
        total = total + p[...].astype(F32)
    acc[...] = total
    me, wide = lax.axis_index("rep"), keep.shape[1]
    keep[...] = mixed[...] + acc[:, window(me, wide)]
    send[...] = acc[:, window(1 - me, wide)].astype(BF)


def dealt(x, tok, head):
    axes = ("groups", "tok", "head", "rep")
    sizes = [lax.axis_size(a) for a in axes]
    pairs = []
    for here in range(int(np.prod(sizes))):
        g, t, h, r = np.unravel_index(here, sizes)
        there = ((g + r) % sizes[0], t ^ tok, (h + head) % sizes[2], r)
        pairs.append((here, int(np.ravel_multi_index(there, sizes))))
    return lax.ppermute(x, axes, pairs)


def on_device(
    keys, values, rates, queries, stream, gain, counts, fw_one, fw_three, fw_two, mlp_up, mlp_down
):
    n_tok, n_head = lax.axis_size("tok"), lax.axis_size("head")
    groups, reps = lax.axis_size("groups"), lax.axis_size("rep")
    dh, n_key, n = keys.shape[1], keys.shape[0], queries.shape[0]
    wide = dh // reps
    paired = n_tok == 4 and n_key == n
    near = 2 if paired else 1
    units = mlp_up.shape[1] // groups // near
    barrier = lax.optimization_barrier

    rows = n_key // reps
    rate_row, gain = rates.reshape(1, n_key), gain[None, :]
    sources = [keys, values, rate_row]
    outs = [shape((n_key, 2 * dh), BF)]
    if paired:
        sources += [queries, stream]
        outs = [shape((rows, 2 * dh), BF), shape((rows, 4 * dh), BF)]
    messages = call(
        functools.partial(message_kernel, len(sources)),
        outs,
        sources,
        [*local(sources), pltpu.VMEM((n_key, 2 * dh), BF), pltpu.SemaphoreType.DMA((len(sources),))],
        fetched=len(sources),
    )
    asks = []
    if paired:
        share, full = messages
        others = [moved(share, tok=2), moved(full, tok=1)][::-1]
        others.append(moved(others[1], tok=1))
        (blocks,) = call(
            pack_kernel, [shape((n_tok, mlp_up.shape[0] + units, units), BF)], [mlp_up, mlp_down]
        )
        others, blocks = barrier((others, blocks))
        mlp = [lax.all_to_all(blocks, "tok", 0, 0)]
        tokens = [*others, *[moved(x, rep=1) for x in others]]
        asks = others[:1]
    else:
        me_g = lax.axis_index("groups")
        up_own = lax.dynamic_slice_in_dim(mlp_up, me_g * units, units, 1)
        down_own = lax.dynamic_slice_in_dim(mlp_down, me_g * units, units, 0)
        tokens = [lax.all_gather(messages[0], "tok", axis=0, tiled=True)]
        mlp = [
            lax.all_gather(up_own, "tok", axis=0, tiled=True),
            lax.all_gather(down_own, "tok", axis=1, tiled=True),
        ]

    n_all = sum(x.shape[0] for x in tokens) + (n_key if paired else 0)
    tokens = barrier(tokens)
    sources = [fw_one[0], fw_three[0], fw_two[0], keys, values, rate_row, queries, stream, gain]
    own, own_sq, send, base, gains = call(
        functools.partial(fast_kernel, len(tokens), near),
        [
            shape((near * n, wide), F32),
            shape((8, wide), F32),
            shape((near * n + 16, wide), BF),
            shape((n, wide), BF),
            shape((16, wide), BF),
        ],
        [*sources, *tokens],
        [
            pltpu.VMEM((n_all, dh), BF),
            pltpu.VMEM((n_all, dh), BF),
            pltpu.VMEM((near * n, dh), F32),
            pltpu.VMEM((near * n, dh), BF),
            pltpu.VMEM((n_key, 2 * dh), BF),
            *local(sources),
            pltpu.SemaphoreType.DMA((len(sources),)),
        ],
        fetched=len(sources),
    )
    got = moved(send, rep=1)
    mixed, low = call(
        mix_kernel,
        [shape((n, wide), F32), shape((near * n + 16, wide), BF)],
        [own, own_sq, got, base, gains, *asks],
    )
    pieces, places = [], []
    for dg, h in itertools.product(range(groups), range(n_head)):
        x = moved(low, groups=dg, head=h)
        pieces += [x, moved(x, rep=1)]
        places += [(dg, h, 0), (dg, h, 1)]
    model = n_head * dh
    (zs,) = call(
        functools.partial(norm_kernel, places), [shape((groups * near * n, model), BF)], pieces
    )
    (send,) = call(
        functools.partial(feed_kernel, False), [shape((near * n, model), BF)], [zs, *mlp]
    )
    got = moved(send, rep=1)
    (own,) = call(
        functools.partial(feed_kernel, True), [shape((near * n, model), F32)], [zs, *mlp]
    )
    moves = sorted(itertools.product(range(near), range(n_head)), key=lambda m: (-m[0] - m[1], m[0]))
    parts = call(
        functools.partial(pair_kernel, moves), [shape((n, dh), BF)] * len(moves), [own, got]
    )
    parts = [dealt(x, *m) for m, x in zip(moves, parts)]
    keep, send = call(
        sum_kernel, [shape((n, wide), F32), shape((n, wide), BF)], [*parts, mixed], [pltpu.VMEM((n, dh), F32)]
    )
    total = keep + moved(send, rep=1).astype(F32)
    live = jnp.arange(n, dtype=jnp.int32) < counts[0]
    return jnp.where(live[:, None], total, 0.0).astype(BF)


def solution(mesh):
    placed = (
        P(("groups", "tok"), "head"),
        P(("groups", "tok"), "head"),
        P(("groups", "tok"), "head"),
        P(("groups", "tok"), "head"),
        P(("groups", "tok"), "head"),
        P("head"),
        P(("groups", "tok")),
        P("head", None, "rep"),
        P("head", None, "rep"),
        P("head", "rep", None),
        P("tok", ("head", "rep")),
        P(("head", "rep"), "tok"),
    )
    return jax.shard_map(
        on_device,
        mesh=mesh,
        in_specs=placed,
        out_specs=P(("groups", "tok"), ("head", "rep")),
        check_vma=False,
    )
```

```python
import functools
import itertools

import jax
import jax.numpy as jnp
import numpy as np
from jax import lax
from jax.experimental import pallas as pl
from jax.experimental.pallas import tpu as pltpu
from jax.sharding import PartitionSpec as P

BF, F32 = jnp.bfloat16, jnp.float32


def dot(a, b, dims=((1,), (0,))):
    return lax.dot_general(a, b, (dims, ((), ())), preferred_element_type=F32)


def moved(x, groups=0, tok=0, head=0, rep=0):
    shifts = {"groups": groups, "tok": tok, "head": head, "rep": rep}
    axes = [a for a, s in shifts.items() if s]
    if not axes:
        return x
    sizes = [lax.axis_size(a) for a in axes]
    pairs = []
    for here in range(int(np.prod(sizes))):
        at = np.unravel_index(here, sizes)
        there = [i ^ tok if a == "tok" else (i + shifts[a]) % n for a, i, n in zip(axes, at, sizes)]
        pairs.append((int(np.ravel_multi_index(there, sizes)), here))
    return lax.ppermute(x, tuple(axes), pairs)


def shape(dims, dtype):
    return jax.ShapeDtypeStruct(dims, dtype)


def call(kernel, outs, args, scratch=(), fetched=0, unmoved=0):
    touched = sum(int(np.prod(x.shape)) * x.dtype.itemsize for x in (*args, *outs))
    kept = sum(int(np.prod(x.shape)) * 4 for x in scratch if hasattr(x, "shape"))
    args = [pltpu.with_memory_space_constraint(x, pltpu.HBM) if i < fetched else x for i, x in enumerate(args)]
    return pl.pallas_call(
        kernel,
        out_shape=outs,
        in_specs=[pl.BlockSpec(memory_space=pltpu.HBM if i < fetched + unmoved else pltpu.VMEM) for i in range(len(args))],
        out_specs=[pl.BlockSpec(memory_space=pltpu.VMEM)] * len(outs),
        scratch_shapes=list(scratch),
        compiler_params=pltpu.CompilerParams(vmem_limit_bytes=touched + kept + (10 << 20)),
        cost_estimate=pl.CostEstimate(flops=1, bytes_accessed=1, transcendentals=0),
    )(*args)


def local(arrays):
    return [pltpu.VMEM(x.shape, x.dtype) for x in arrays]


def window(index, size):
    return pl.ds(pl.multiple_of(index * size, size), size)


def fetch(pairs, sems):
    copies = [pltpu.make_async_copy(src, dst, sems.at[i]) for i, (src, dst) in enumerate(pairs)]
    for c in copies:
        c.start()
    return copies


def side_by_side(pair, keys, values, rates):
    n, dh = keys.shape
    pair[:, :dh] = keys[...]
    rate = jnp.broadcast_to(rates[...], (128, n)).T
    for c in range(0, dh, 128):
        pair[:, dh + c : dh + c + 128] = (values[:, c : c + 128].astype(F32) * rate).astype(BF)


def message_kernel(keys, values, rates, *refs):
    out, *near, sems = refs
    for c in fetch(list(zip((keys, values, rates), near)), sems):
        c.wait()
    side_by_side(out, *near)


def share_kernel(keys, values, rates, queries, stream, share, full, v, rate_row, rate, sems):
    rows, width = share.shape
    dh, n = width // 2, queries.shape[0]
    wide = dh // 2
    me = lax.axis_index("rep")
    mine = window(me, rows)
    pairs = [(keys.at[mine, :], share.at[:, :dh]), (values.at[mine, :], v), (rates, rate_row)]
    pairs.append((queries.at[mine, :], full.at[:, width : width + dh]))
    for i in range(n // rows):
        at = width + dh + i * wide
        pairs.append((stream.at[i * rows : (i + 1) * rows, window(me, wide)], full.at[:, at : at + wide]))
    copies = fetch(pairs, sems)
    for c in copies[:3]:
        c.wait()
    rate[...] = jnp.broadcast_to(rate_row[...], (128, rate.shape[0])).T
    by_row = rate[mine, :]
    for c in range(0, dh, 128):
        share[:, dh + c : dh + c + 128] = (v[:, c : c + 128].astype(F32) * by_row).astype(BF)
    full[:, :width] = share[...]
    for c in copies[3:]:
        c.wait()


def pack_kernel(up, down, out):
    deep, wide = up.shape[0], out.shape[2]
    for t in range(out.shape[0]):
        part = window(lax.axis_index("groups") * 2 + t % 2, wide)
        out[t, :deep, :] = up[:, part]
        out[t, deep:, :] = down[part, :]


def gradients(k, e, w1b, w3b, w2b):
    a1, a3, b = dot(k, w1b), dot(k, w3b), dot(e, w2b, ((1,), (1,)))
    sig = jax.nn.sigmoid(a1)
    act = a1 * sig
    g = (act * a3).astype(BF)
    r1 = (b * a3 * (sig * (1.0 + a1 * (1.0 - sig)))).astype(BF)
    r3 = (b * act).astype(BF)
    first = ((0,), (0,))
    return dot(k, r1, first), dot(k, r3, first), dot(g, e, first)


def squares(x):
    return jnp.sum(x * x, axis=0, keepdims=True)


def fast_kernel(n_pieces, near, *refs):
    far, refs = refs[:9], refs[9:]
    pieces, refs = refs[:n_pieces], refs[n_pieces:]
    own_out, own_sq, send, base, gains, ks, es, hp, qs, pair, *local, sems = refs
    w1, w3, w2, keys, values, rates, q, stream, gain = local
    copies = fetch(list(zip(far, local)), sems)
    dh, hidden = w1.shape
    me = lax.axis_index("rep")
    n = q.shape[0]
    at = 0
    for p in pieces:
        rows = p.shape[0]
        ks[at : at + rows, :] = p[:, :dh]
        es[at : at + rows, :] = p[:, dh : 2 * dh]
        at += rows
    if near > 1:
        mine, theirs = pieces[0], pieces[n_pieces // 2]
        rows = mine.shape[0]
        qs[pl.ds(pl.multiple_of(n + me * rows, rows), rows), :] = mine[:, 2 * dh : 3 * dh]
        qs[pl.ds(pl.multiple_of(n + (1 - me) * rows, rows), rows), :] = theirs[:, 2 * dh : 3 * dh]
    for c in copies[3:]:
        c.wait()
    if near > 1:
        side_by_side(pair, keys, values, rates)
        ks[at : at + n, :] = pair[:, :dh]
        es[at : at + n, :] = pair[:, dh:]
        at += n
    qs[:n, :] = q[...]
    asked = qs[...]
    tokens, step, block = at, min(at, 512), min(hidden, 256)
    for c in copies[:3]:
        c.wait()
    old_sq = squares(w2[...])
    new_sq = jnp.zeros((1, dh), F32)
    for j in range(0, hidden, block):
        js = slice(j, j + block)
        x1, x3, x2 = w1[:, js], w3[:, js], w2[js, :]
        b1, b3, b2 = x1.astype(BF), x3.astype(BF), x2.astype(BF)

        def add(i, sums):
            rows = pl.ds(pl.multiple_of(i * step, step), step)
            return tuple(s + p for s, p in zip(sums, gradients(ks[rows, :], es[rows, :], b1, b3, b2)))

        sums = (x1, x3, x2)
        sums = add(0, sums) if tokens == step else lax.fori_loop(0, tokens // step, add, sums)

        def normed(old, new):
            return (new * (jnp.sqrt(squares(old)) * lax.rsqrt(squares(new) + 1e-06))).astype(BF)

        new_sq = new_sq + squares(sums[2])
        qa, qc = dot(asked, normed(x1, sums[0])), dot(asked, normed(x3, sums[1]))
        part = dot((qa * jax.nn.sigmoid(qa) * qc).astype(BF), sums[2].astype(BF))
        hp[...] = part if j == 0 else hp[...] + part
    rows, wide = own_out.shape
    base[...] = stream[:, window(me, wide)]
    x = jnp.broadcast_to(gain[:, window(me, wide)], gains.shape)
    row = lax.broadcasted_iota(jnp.int32, x.shape, 0)
    top = x.astype(BF).astype(F32)
    mid = (x - top).astype(BF).astype(F32)
    gains[...] = jnp.where(row == 0, top, jnp.where(row == 1, mid, jnp.where(row == 2, x - top - mid, 0.0))).astype(BF)
    own_out[...] = hp[:, window(me, wide)]
    send[:rows, :] = hp[:, window(1 - me, wide)].astype(BF)
    row = lax.broadcasted_iota(jnp.int32, (8, dh), 0)
    hp[:8, :] = jnp.where(row == 0, old_sq, jnp.where(row == 1, new_sq, 0.0))
    own_sq[...] = hp[:8, window(me, wide)]
    sq = hp[:8, window(1 - me, wide)]
    top = sq.astype(BF).astype(F32)
    send[rows:, :] = jnp.concatenate([top, sq - top], axis=0).astype(BF)


def mix_kernel(own, own_sq, got, base, gains, *refs):
    *asks, mixed, low = refs
    n, wide = mixed.shape
    rows = own.shape[0]
    tail = got[rows:, :].astype(F32)
    sq = own_sq[...] + tail[:8] + tail[8:]
    y = (own[...] + got[:rows, :].astype(F32)) * (jnp.sqrt(sq[0:1]) * lax.rsqrt(sq[1:2] + 1e-06))
    mixed[...] = y[:n] + base[...].astype(F32)
    low[:n, :] = mixed[...].astype(BF)
    for message in asks:
        part = message.shape[0]
        for i in range(n // part):
            at, there = n + i * part, message.shape[1] - n // part * wide + i * wide
            low[at : at + part, :] = (y[at : at + part] + message[:, there : there + wide].astype(F32)).astype(BF)
    low[rows:, :] = gains[...]


def norm_kernel(places, *refs):
    pieces, zs = refs[:-1], refs[-1]
    me_h, me_r = lax.axis_index("head"), lax.axis_index("rep")
    n_head = lax.axis_size("head")
    n, wide = pieces[0].shape[0] - 16, pieces[0].shape[1]
    for dg in range(lax.axis_size("groups")):
        here = [(p, dh, dr) for p, (g, dh, dr) in zip(pieces, places) if g == dg]
        norm = jnp.zeros((n, 1), F32)
        for p, _, _ in here:
            x = p[:n, :].astype(F32)
            norm = norm + jnp.sum(x * x, axis=1, keepdims=True)
        inv = lax.rsqrt(norm / zs.shape[1] + 1e-06)
        for p, dh, dr in here:
            r = lax.rem(me_r + dr, 2)
            head = lax.rem(me_h + dh, n_head)
            gain = jnp.sum(p[n:, :].astype(F32), axis=0, keepdims=True)
            zs[dg * n : (dg + 1) * n, window(head * 2 + r, wide)] = (p[:n, :].astype(F32) * inv * gain).astype(BF)


def blocks_of(mlp, width):
    if len(mlp) > 1:
        return [mlp[0]], [mlp[1]]
    deep = width // mlp[0].shape[0]
    each = range(mlp[0].shape[0])
    return [mlp[0].at[t, :deep, :] for t in each], [mlp[0].at[t, deep:, :] for t in each]


def feed(z, ups, downs, out):
    n_head = lax.axis_size("head")
    part = z.shape[1] // n_head
    deep = z.shape[1] // len(ups)
    wide = min(deep, part)
    total = None
    for t, x in enumerate(ups):
        term = dot(z[:, t * deep : (t + 1) * deep], x[...])
        total = term if total is None else total + term
    h = (0.5 * total * (1.0 + lax.erf(total * np.float32(0.5**0.5)))).astype(BF)
    for t, x in enumerate(downs):
        for c in range(0, deep, wide):
            head, at = divmod(t * deep + c, part)
            place = lax.rem(head - lax.axis_index("head") + n_head, n_head) * part + at
            out[:, pl.ds(pl.multiple_of(place, wide), wide)] = dot(h, x[:, c : c + wide]).astype(out.dtype)


def feed_kernel(ours, zs, *refs):
    *mlp, out = refs
    ups, downs = blocks_of(mlp, zs.shape[1])
    me = lax.axis_index("rep")
    feed(zs[window(me if ours else 1 - me, out.shape[0]), :], ups, downs, out)


def pair_kernel(moves, own, got, *outs):
    n, wide = outs[0].shape
    for (dz, dh), out in zip(moves, outs):
        rows, cols = slice(dz * n, (dz + 1) * n), slice(dh * wide, (dh + 1) * wide)
        out[...] = (own[rows, cols] + got[rows, cols].astype(F32)).astype(BF)


def sum_kernel(*refs):
    *parts, mixed, keep, send, acc = refs
    total = parts[0][...].astype(F32)
    for p in parts[1:]:
        total = total + p[...].astype(F32)
    acc[...] = total
    me, wide = lax.axis_index("rep"), keep.shape[1]
    keep[...] = mixed[...] + acc[:, window(me, wide)]
    send[...] = acc[:, window(1 - me, wide)].astype(BF)


def dealt(x, tok, head):
    axes = ("groups", "tok", "head", "rep")
    sizes = [lax.axis_size(a) for a in axes]
    pairs = []
    for here in range(int(np.prod(sizes))):
        g, t, h, r = np.unravel_index(here, sizes)
        there = ((g + r) % sizes[0], t ^ tok, (h + head) % sizes[2], r)
        pairs.append((here, int(np.ravel_multi_index(there, sizes))))
    return lax.ppermute(x, axes, pairs)


def on_device(
    keys, values, rates, queries, stream, gain, counts, fw_one, fw_three, fw_two, mlp_up, mlp_down
):
    n_tok, n_head = lax.axis_size("tok"), lax.axis_size("head")
    groups, reps = lax.axis_size("groups"), lax.axis_size("rep")
    dh, n_key, n = keys.shape[1], keys.shape[0], queries.shape[0]
    wide = dh // reps
    paired = n_tok == 4 and n_key == n
    near = 2 if paired else 1
    units = mlp_up.shape[1] // groups // near
    barrier = lax.optimization_barrier

    rows = n_key // reps
    rate_row, gain = rates.reshape(1, n_key), gain[None, :]
    sources = [keys, values, rate_row]
    if paired:
        sources += [queries, stream]
        messages = call(
            share_kernel,
            [shape((rows, 2 * dh), BF), shape((rows, 4 * dh), BF)],
            sources,
            [
                pltpu.VMEM((rows, dh), BF),
                pltpu.VMEM((1, n_key), F32),
                pltpu.VMEM((n_key, 128), F32),
                pltpu.SemaphoreType.DMA((4 + n // rows,)),
            ],
            fetched=len(sources),
        )
    else:
        messages = call(
            message_kernel,
            [shape((n_key, 2 * dh), BF)],
            sources,
            [*local(sources), pltpu.SemaphoreType.DMA((len(sources),))],
            fetched=len(sources),
        )
    asks = []
    if paired:
        share, full = messages
        others = [moved(share, tok=2), moved(full, tok=1)][::-1]
        others.append(moved(others[1], tok=1))
        (blocks,) = call(
            pack_kernel, [shape((n_tok, mlp_up.shape[0] + units, units), BF)], [mlp_up, mlp_down]
        )
        others, blocks = barrier((others, blocks))
        mlp = [lax.all_to_all(blocks, "tok", 0, 0)]
        tokens = [*others, *[moved(x, rep=1) for x in others]]
        asks = others[:1]
    else:
        me_g = lax.axis_index("groups")
        up_own = lax.dynamic_slice_in_dim(mlp_up, me_g * units, units, 1)
        down_own = lax.dynamic_slice_in_dim(mlp_down, me_g * units, units, 0)
        tokens = [lax.all_gather(messages[0], "tok", axis=0, tiled=True)]
        mlp = [
            lax.all_gather(up_own, "tok", axis=0, tiled=True),
            lax.all_gather(down_own, "tok", axis=1, tiled=True),
        ]

    n_all = sum(x.shape[0] for x in tokens) + (n_key if paired else 0)
    tokens = barrier(tokens)
    sources = [fw_one[0], fw_three[0], fw_two[0], keys, values, rate_row, queries, stream, gain]
    own, own_sq, send, base, gains = call(
        functools.partial(fast_kernel, len(tokens), near),
        [
            shape((near * n, wide), F32),
            shape((8, wide), F32),
            shape((near * n + 16, wide), BF),
            shape((n, wide), BF),
            shape((16, wide), BF),
        ],
        [*sources, *tokens],
        [
            pltpu.VMEM((n_all, dh), BF),
            pltpu.VMEM((n_all, dh), BF),
            pltpu.VMEM((near * n, dh), F32),
            pltpu.VMEM((near * n, dh), BF),
            pltpu.VMEM((n_key, 2 * dh), BF),
            *local(sources),
            pltpu.SemaphoreType.DMA((len(sources),)),
        ],
        fetched=len(sources),
    )
    got = moved(send, rep=1)
    mixed, low = call(
        mix_kernel,
        [shape((n, wide), F32), shape((near * n + 16, wide), BF)],
        [own, own_sq, got, base, gains, *asks],
    )
    pieces, places = [], []
    for dg, h in itertools.product(range(groups), range(n_head)):
        x = moved(low, groups=dg, head=h)
        pieces += [x, moved(x, rep=1)]
        places += [(dg, h, 0), (dg, h, 1)]
    model = n_head * dh
    (zs,) = call(
        functools.partial(norm_kernel, places), [shape((groups * near * n, model), BF)], pieces
    )
    (send,) = call(
        functools.partial(feed_kernel, False), [shape((near * n, model), BF)], [zs, *mlp]
    )
    got = moved(send, rep=1)
    (own,) = call(
        functools.partial(feed_kernel, True), [shape((near * n, model), F32)], [zs, *mlp]
    )
    moves = sorted(itertools.product(range(near), range(n_head)), key=lambda m: (-m[0] - m[1], m[0]))
    parts = call(
        functools.partial(pair_kernel, moves), [shape((n, dh), BF)] * len(moves), [own, got]
    )
    parts = [dealt(x, *m) for m, x in zip(moves, parts)]
    keep, send = call(
        sum_kernel, [shape((n, wide), F32), shape((n, wide), BF)], [*parts, mixed], [pltpu.VMEM((n, dh), F32)]
    )
    total = keep + moved(send, rep=1).astype(F32)
    live = jnp.arange(n, dtype=jnp.int32) < counts[0]
    return jnp.where(live[:, None], total, 0.0).astype(BF)


def solution(mesh):
    placed = (
        P(("groups", "tok"), "head"),
        P(("groups", "tok"), "head"),
        P(("groups", "tok"), "head"),
        P(("groups", "tok"), "head"),
        P(("groups", "tok"), "head"),
        P("head"),
        P(("groups", "tok")),
        P("head", None, "rep"),
        P("head", None, "rep"),
        P("head", "rep", None),
        P("tok", ("head", "rep")),
        P(("head", "rep"), "tok"),
    )
    return jax.shard_map(
        on_device,
        mesh=mesh,
        in_specs=placed,
        out_specs=P(("groups", "tok"), ("head", "rep")),
        check_vma=False,
    )
```

```python
import functools
import itertools

import jax
import jax.numpy as jnp
import numpy as np
from jax import lax
from jax.experimental import pallas as pl
from jax.experimental.pallas import tpu as pltpu
from jax.sharding import PartitionSpec as P

BF, F32 = jnp.bfloat16, jnp.float32


def dot(a, b, dims=((1,), (0,))):
    return lax.dot_general(a, b, (dims, ((), ())), preferred_element_type=F32)


def moved(x, groups=0, tok=0, head=0, rep=0):
    shifts = {"groups": groups, "tok": tok, "head": head, "rep": rep}
    axes = [a for a, s in shifts.items() if s]
    if not axes:
        return x
    sizes = [lax.axis_size(a) for a in axes]
    pairs = []
    for here in range(int(np.prod(sizes))):
        at = np.unravel_index(here, sizes)
        there = [i ^ tok if a == "tok" else (i + shifts[a]) % n for a, i, n in zip(axes, at, sizes)]
        pairs.append((int(np.ravel_multi_index(there, sizes)), here))
    return lax.ppermute(x, tuple(axes), pairs)


def shape(dims, dtype):
    return jax.ShapeDtypeStruct(dims, dtype)


def call(kernel, outs, args, scratch=(), fetched=0, unmoved=0):
    touched = sum(int(np.prod(x.shape)) * x.dtype.itemsize for x in (*args, *outs))
    kept = sum(int(np.prod(x.shape)) * 4 for x in scratch if hasattr(x, "shape"))
    args = [pltpu.with_memory_space_constraint(x, pltpu.HBM) if i < fetched else x for i, x in enumerate(args)]
    return pl.pallas_call(
        kernel,
        out_shape=outs,
        in_specs=[pl.BlockSpec(memory_space=pltpu.HBM if i < fetched + unmoved else pltpu.VMEM) for i in range(len(args))],
        out_specs=[pl.BlockSpec(memory_space=pltpu.VMEM)] * len(outs),
        scratch_shapes=list(scratch),
        compiler_params=pltpu.CompilerParams(vmem_limit_bytes=touched + kept + (10 << 20)),
        cost_estimate=pl.CostEstimate(flops=1, bytes_accessed=1, transcendentals=0),
    )(*args)


def local(arrays):
    return [pltpu.VMEM(x.shape, x.dtype) for x in arrays]


def window(index, size):
    return pl.ds(pl.multiple_of(index * size, size), size)


def fetch(pairs, sems):
    copies = [pltpu.make_async_copy(src, dst, sems.at[i]) for i, (src, dst) in enumerate(pairs)]
    for c in copies:
        c.start()
    return copies


def side_by_side(pair, keys, values, rates):
    n, dh = keys.shape
    pair[:, :dh] = keys[...]
    rate = jnp.broadcast_to(rates[...], (128, n)).T
    for c in range(0, dh, 128):
        pair[:, dh + c : dh + c + 128] = (values[:, c : c + 128].astype(F32) * rate).astype(BF)


def message_kernel(keys, values, rates, *refs):
    out, *near, sems = refs
    for c in fetch(list(zip((keys, values, rates), near)), sems):
        c.wait()
    side_by_side(out, *near)


def share_kernel(keys, values, rates, queries, stream, share, full, v, rate_row, rate, sems):
    rows, width = share.shape
    dh, n = width // 2, queries.shape[0]
    wide = dh // 2
    me = lax.axis_index("rep")
    mine = window(me, rows)
    pairs = [(keys.at[mine, :], share.at[:, :dh]), (values.at[mine, :], v), (rates, rate_row)]
    pairs.append((queries.at[mine, :], full.at[:, width : width + dh]))
    for i in range(n // rows):
        at = width + dh + i * wide
        pairs.append((stream.at[i * rows : (i + 1) * rows, window(me, wide)], full.at[:, at : at + wide]))
    copies = fetch(pairs, sems)
    for c in copies[:3]:
        c.wait()
    rate[...] = jnp.broadcast_to(rate_row[...], (128, rate.shape[0])).T
    by_row = rate[mine, :]
    for c in range(0, dh, 128):
        share[:, dh + c : dh + c + 128] = (v[:, c : c + 128].astype(F32) * by_row).astype(BF)
    full[:, :width] = share[...]
    for c in copies[3:]:
        c.wait()


def pack_kernel(up, down, out):
    deep, wide = up.shape[0], out.shape[2]
    for t in range(out.shape[0]):
        part = window(lax.axis_index("groups") * 2 + t % 2, wide)
        out[t, :deep, :] = up[:, part]
        out[t, deep:, :] = down[part, :]


def gradients(k, e, w1b, w3b, w2b):
    a1, a3, b = dot(k, w1b), dot(k, w3b), dot(e, w2b, ((1,), (1,)))
    sig = jax.nn.sigmoid(a1)
    act = a1 * sig
    g = (act * a3).astype(BF)
    r1 = (b * a3 * (sig * (1.0 + a1 * (1.0 - sig)))).astype(BF)
    r3 = (b * act).astype(BF)
    first = ((0,), (0,))
    return dot(k, r1, first), dot(k, r3, first), dot(g, e, first)


def squares(x):
    return jnp.sum(x * x, axis=0, keepdims=True)


def fast_kernel(n_pieces, near, *refs):
    far, refs = refs[:9], refs[9:]
    pieces, refs = refs[:n_pieces], refs[n_pieces:]
    own_out, own_sq, send, base, gains, ks, es, hp, qs, pair, *local, sems = refs
    w1, w3, w2, keys, values, rates, q, stream, gain = local
    copies = fetch(list(zip(far, local)), sems)
    dh, hidden = w1.shape
    me = lax.axis_index("rep")
    n = q.shape[0]
    at = 0
    for p in pieces:
        rows = p.shape[0]
        ks[at : at + rows, :] = p[:, :dh]
        es[at : at + rows, :] = p[:, dh : 2 * dh]
        at += rows
    if near > 1:
        mine, theirs = pieces[0], pieces[n_pieces // 2]
        rows = mine.shape[0]
        qs[pl.ds(pl.multiple_of(n + me * rows, rows), rows), :] = mine[:, 2 * dh : 3 * dh]
        qs[pl.ds(pl.multiple_of(n + (1 - me) * rows, rows), rows), :] = theirs[:, 2 * dh : 3 * dh]
    for c in copies[3:]:
        c.wait()
    if near > 1:
        side_by_side(pair, keys, values, rates)
        ks[at : at + n, :] = pair[:, :dh]
        es[at : at + n, :] = pair[:, dh:]
        at += n
    qs[:n, :] = q[...]
    asked = qs[...]
    tokens, step, block = at, min(at, 512), min(hidden, 256)
    for c in copies[:3]:
        c.wait()
    old_sq = squares(w2[...])
    new_sq = jnp.zeros((1, dh), F32)
    for j in range(0, hidden, block):
        js = slice(j, j + block)
        x1, x3, x2 = w1[:, js], w3[:, js], w2[js, :]
        b1, b3, b2 = x1.astype(BF), x3.astype(BF), x2.astype(BF)

        def add(i, sums):
            rows = pl.ds(pl.multiple_of(i * step, step), step)
            return tuple(s + p for s, p in zip(sums, gradients(ks[rows, :], es[rows, :], b1, b3, b2)))

        sums = (x1, x3, x2)
        sums = add(0, sums) if tokens == step else lax.fori_loop(0, tokens // step, add, sums)

        def normed(old, new):
            return (new * (jnp.sqrt(squares(old)) * lax.rsqrt(squares(new) + 1e-06))).astype(BF)

        new_sq = new_sq + squares(sums[2])
        qa, qc = dot(asked, normed(x1, sums[0])), dot(asked, normed(x3, sums[1]))
        part = dot((qa * jax.nn.sigmoid(qa) * qc).astype(BF), sums[2].astype(BF))
        hp[...] = part if j == 0 else hp[...] + part
    rows, wide = own_out.shape
    base[...] = stream[:, window(me, wide)]
    x = jnp.broadcast_to(gain[:, window(me, wide)], gains.shape)
    row = lax.broadcasted_iota(jnp.int32, x.shape, 0)
    top = x.astype(BF).astype(F32)
    mid = (x - top).astype(BF).astype(F32)
    gains[...] = jnp.where(row == 0, top, jnp.where(row == 1, mid, jnp.where(row == 2, x - top - mid, 0.0))).astype(BF)
    own_out[...] = hp[:, window(me, wide)]
    send[:rows, :] = hp[:, window(1 - me, wide)].astype(BF)
    row = lax.broadcasted_iota(jnp.int32, (8, dh), 0)
    hp[:8, :] = jnp.where(row == 0, old_sq, jnp.where(row == 1, new_sq, 0.0))
    own_sq[...] = hp[:8, window(me, wide)]
    sq = hp[:8, window(1 - me, wide)]
    top = sq.astype(BF).astype(F32)
    send[rows:, :] = jnp.concatenate([top, sq - top], axis=0).astype(BF)


def mix_kernel(own, own_sq, got, base, gains, *refs):
    *asks, mixed, low = refs
    n, wide = mixed.shape
    rows = own.shape[0]
    tail = got[rows:, :].astype(F32)
    sq = own_sq[...] + tail[:8] + tail[8:]
    y = (own[...] + got[:rows, :].astype(F32)) * (jnp.sqrt(sq[0:1]) * lax.rsqrt(sq[1:2] + 1e-06))
    mixed[...] = y[:n] + base[...].astype(F32)
    low[:n, :] = mixed[...].astype(BF)
    for message in asks:
        part = message.shape[0]
        for i in range(n // part):
            at, there = n + i * part, message.shape[1] - n // part * wide + i * wide
            low[at : at + part, :] = (y[at : at + part] + message[:, there : there + wide].astype(F32)).astype(BF)
    low[rows:, :] = gains[...]


def norm_kernel(places, *refs):
    pieces, zs = refs[:-1], refs[-1]
    me_h, me_r = lax.axis_index("head"), lax.axis_index("rep")
    n_head = lax.axis_size("head")
    n, wide = pieces[0].shape[0] - 16, pieces[0].shape[1]
    for dg in range(lax.axis_size("groups")):
        here = [(p, dh, dr) for p, (g, dh, dr) in zip(pieces, places) if g == dg]
        norm = jnp.zeros((n, 1), F32)
        for p, _, _ in here:
            x = p[:n, :].astype(F32)
            norm = norm + jnp.sum(x * x, axis=1, keepdims=True)
        inv = lax.rsqrt(norm / zs.shape[1] + 1e-06)
        for p, dh, dr in here:
            r = lax.rem(me_r + dr, 2)
            head = lax.rem(me_h + dh, n_head)
            gain = jnp.sum(p[n:, :].astype(F32), axis=0, keepdims=True)
            zs[dg * n : (dg + 1) * n, window(head * 2 + r, wide)] = (p[:n, :].astype(F32) * inv * gain).astype(BF)


def blocks_of(mlp, width):
    if len(mlp) > 1:
        return [mlp[0]], [mlp[1]]
    deep = width // mlp[0].shape[0]
    each = range(mlp[0].shape[0])
    return [mlp[0].at[t, :deep, :] for t in each], [mlp[0].at[t, deep:, :] for t in each]


def feed(z, ups, downs, out):
    n_head = lax.axis_size("head")
    part = z.shape[1] // n_head
    deep = z.shape[1] // len(ups)
    wide = min(deep, part)
    total = None
    for t, x in enumerate(ups):
        term = dot(z[:, t * deep : (t + 1) * deep], x[...])
        total = term if total is None else total + term
    h = (0.5 * total * (1.0 + lax.erf(total * np.float32(0.5**0.5)))).astype(BF)
    for t, x in enumerate(downs):
        for c in range(0, deep, wide):
            head, at = divmod(t * deep + c, part)
            place = lax.rem(head - lax.axis_index("head") + n_head, n_head) * part + at
            out[:, pl.ds(pl.multiple_of(place, wide), wide)] = dot(h, x[:, c : c + wide]).astype(out.dtype)


def feed_kernel(ours, zs, *refs):
    *mlp, out = refs
    ups, downs = blocks_of(mlp, zs.shape[1])
    me = lax.axis_index("rep")
    feed(zs[window(me if ours else 1 - me, out.shape[0]), :], ups, downs, out)


def pair_kernel(moves, own, got, *outs):
    n, wide = outs[0].shape
    for (dz, dh), out in zip(moves, outs):
        rows, cols = slice(dz * n, (dz + 1) * n), slice(dh * wide, (dh + 1) * wide)
        out[...] = (own[rows, cols] + got[rows, cols].astype(F32)).astype(BF)


def sum_kernel(*refs):
    *parts, own, mixed, keep, send, acc = refs
    me = lax.axis_index("rep")
    total = jnp.where(me == 0, own[...].astype(F32), 0.0)
    for p in parts:
        total = total + p[...].astype(F32)
    acc[...] = total
    wide = keep.shape[1]
    keep[...] = mixed[...] + acc[:, window(me, wide)]
    send[...] = acc[:, window(1 - me, wide)].astype(BF)


def dealt(x, tok, head):
    axes = ("groups", "tok", "head", "rep")
    sizes = [lax.axis_size(a) for a in axes]
    pairs = []
    for here in range(int(np.prod(sizes))):
        g, t, h, r = np.unravel_index(here, sizes)
        there = ((g + r) % sizes[0], t ^ tok, (h + head) % sizes[2], r)
        pairs.append((here, int(np.ravel_multi_index(there, sizes))))
    return lax.ppermute(x, axes, [p for p in pairs if p[0] != p[1]])


def on_device(
    keys, values, rates, queries, stream, gain, counts, fw_one, fw_three, fw_two, mlp_up, mlp_down
):
    n_tok, n_head = lax.axis_size("tok"), lax.axis_size("head")
    groups, reps = lax.axis_size("groups"), lax.axis_size("rep")
    dh, n_key, n = keys.shape[1], keys.shape[0], queries.shape[0]
    wide = dh // reps
    paired = n_tok == 4 and n_key == n
    near = 2 if paired else 1
    units = mlp_up.shape[1] // groups // near
    barrier = lax.optimization_barrier

    rows = n_key // reps
    rate_row, gain = rates.reshape(1, n_key), gain[None, :]
    sources = [keys, values, rate_row]
    if paired:
        sources += [queries, stream]
        messages = call(
            share_kernel,
            [shape((rows, 2 * dh), BF), shape((rows, 4 * dh), BF)],
            sources,
            [
                pltpu.VMEM((rows, dh), BF),
                pltpu.VMEM((1, n_key), F32),
                pltpu.VMEM((n_key, 128), F32),
                pltpu.SemaphoreType.DMA((4 + n // rows,)),
            ],
            fetched=len(sources),
        )
    else:
        messages = call(
            message_kernel,
            [shape((n_key, 2 * dh), BF)],
            sources,
            [*local(sources), pltpu.SemaphoreType.DMA((len(sources),))],
            fetched=len(sources),
        )
    asks = []
    if paired:
        share, full = messages
        others = [moved(share, tok=2), moved(full, tok=1)][::-1]
        others.append(moved(others[1], tok=1))
        (blocks,) = call(
            pack_kernel, [shape((n_tok, mlp_up.shape[0] + units, units), BF)], [mlp_up, mlp_down]
        )
        others, blocks = barrier((others, blocks))
        mlp = [lax.all_to_all(blocks, "tok", 0, 0)]
        tokens = [*others, *[moved(x, rep=1) for x in others]]
        asks = others[:1]
    else:
        me_g = lax.axis_index("groups")
        up_own = lax.dynamic_slice_in_dim(mlp_up, me_g * units, units, 1)
        down_own = lax.dynamic_slice_in_dim(mlp_down, me_g * units, units, 0)
        tokens = [lax.all_gather(messages[0], "tok", axis=0, tiled=True)]
        mlp = [
            lax.all_gather(up_own, "tok", axis=0, tiled=True),
            lax.all_gather(down_own, "tok", axis=1, tiled=True),
        ]

    n_all = sum(x.shape[0] for x in tokens) + (n_key if paired else 0)
    tokens = barrier(tokens)
    sources = [fw_one[0], fw_three[0], fw_two[0], keys, values, rate_row, queries, stream, gain]
    own, own_sq, send, base, gains = call(
        functools.partial(fast_kernel, len(tokens), near),
        [
            shape((near * n, wide), F32),
            shape((8, wide), F32),
            shape((near * n + 16, wide), BF),
            shape((n, wide), BF),
            shape((16, wide), BF),
        ],
        [*sources, *tokens],
        [
            pltpu.VMEM((n_all, dh), BF),
            pltpu.VMEM((n_all, dh), BF),
            pltpu.VMEM((near * n, dh), F32),
            pltpu.VMEM((near * n, dh), BF),
            pltpu.VMEM((n_key, 2 * dh), BF),
            *local(sources),
            pltpu.SemaphoreType.DMA((len(sources),)),
        ],
        fetched=len(sources),
    )
    got = moved(send, rep=1)
    mixed, low = call(
        mix_kernel,
        [shape((n, wide), F32), shape((near * n + 16, wide), BF)],
        [own, own_sq, got, base, gains, *asks],
    )
    pieces, places = [], []
    for dg, h in itertools.product(range(groups), range(n_head)):
        x = moved(low, groups=dg, head=h)
        pieces += [x, moved(x, rep=1)]
        places += [(dg, h, 0), (dg, h, 1)]
    model = n_head * dh
    (zs,) = call(
        functools.partial(norm_kernel, places), [shape((groups * near * n, model), BF)], pieces
    )
    (send,) = call(
        functools.partial(feed_kernel, False), [shape((near * n, model), BF)], [zs, *mlp]
    )
    got = moved(send, rep=1)
    (own,) = call(
        functools.partial(feed_kernel, True), [shape((near * n, model), F32)], [zs, *mlp]
    )
    moves = sorted(itertools.product(range(near), range(n_head)), key=lambda m: (m[0] + m[1] < 2, m[0], -m[1]))
    parts = call(
        functools.partial(pair_kernel, moves), [shape((n, dh), BF)] * len(moves), [own, got]
    )
    own = parts[moves.index((0, 0))]
    parts = [dealt(x, *m) for m, x in zip(moves, parts)]
    keep, send = call(
        sum_kernel, [shape((n, wide), F32), shape((n, wide), BF)], [*parts, own, mixed], [pltpu.VMEM((n, dh), F32)]
    )
    total = keep + moved(send, rep=1).astype(F32)
    live = jnp.arange(n, dtype=jnp.int32) < counts[0]
    return jnp.where(live[:, None], total, 0.0).astype(BF)


def solution(mesh):
    placed = (
        P(("groups", "tok"), "head"),
        P(("groups", "tok"), "head"),
        P(("groups", "tok"), "head"),
        P(("groups", "tok"), "head"),
        P(("groups", "tok"), "head"),
        P("head"),
        P(("groups", "tok")),
        P("head", None, "rep"),
        P("head", None, "rep"),
        P("head", "rep", None),
        P("tok", ("head", "rep")),
        P(("head", "rep"), "tok"),
    )
    return jax.shard_map(
        on_device,
        mesh=mesh,
        in_specs=placed,
        out_specs=P(("groups", "tok"), ("head", "rep")),
        check_vma=False,
    )
```

```python
import functools
import itertools

import jax
import jax.numpy as jnp
import numpy as np
from jax import lax
from jax.experimental import pallas as pl
from jax.experimental.pallas import tpu as pltpu
from jax.sharding import PartitionSpec as P

BF, F32 = jnp.bfloat16, jnp.float32


def dot(a, b, dims=((1,), (0,))):
    return lax.dot_general(a, b, (dims, ((), ())), preferred_element_type=F32)


def moved(x, groups=0, tok=0, head=0, rep=0):
    shifts = {"groups": groups, "tok": tok, "head": head, "rep": rep}
    axes = [a for a, s in shifts.items() if s]
    if not axes:
        return x
    sizes = [lax.axis_size(a) for a in axes]
    pairs = []
    for here in range(int(np.prod(sizes))):
        at = np.unravel_index(here, sizes)
        there = [i ^ tok if a == "tok" else (i + shifts[a]) % n for a, i, n in zip(axes, at, sizes)]
        pairs.append((int(np.ravel_multi_index(there, sizes)), here))
    return lax.ppermute(x, tuple(axes), pairs)


def shape(dims, dtype):
    return jax.ShapeDtypeStruct(dims, dtype)


def call(kernel, outs, args, scratch=(), fetched=0, unmoved=0):
    touched = sum(int(np.prod(x.shape)) * x.dtype.itemsize for x in (*args, *outs))
    kept = sum(int(np.prod(x.shape)) * 4 for x in scratch if hasattr(x, "shape"))
    args = [pltpu.with_memory_space_constraint(x, pltpu.HBM) if i < fetched else x for i, x in enumerate(args)]
    return pl.pallas_call(
        kernel,
        out_shape=outs,
        in_specs=[pl.BlockSpec(memory_space=pltpu.HBM if i < fetched + unmoved else pltpu.VMEM) for i in range(len(args))],
        out_specs=[pl.BlockSpec(memory_space=pltpu.VMEM)] * len(outs),
        scratch_shapes=list(scratch),
        compiler_params=pltpu.CompilerParams(vmem_limit_bytes=touched + kept + (10 << 20)),
        cost_estimate=pl.CostEstimate(flops=1, bytes_accessed=1, transcendentals=0),
    )(*args)


def local(arrays):
    return [pltpu.VMEM(x.shape, x.dtype) for x in arrays]


def window(index, size):
    return pl.ds(pl.multiple_of(index * size, size), size)


def fetch(pairs, sems):
    copies = [pltpu.make_async_copy(src, dst, sems.at[i]) for i, (src, dst) in enumerate(pairs)]
    for c in copies:
        c.start()
    return copies


def side_by_side(pair, keys, values, rates):
    n, dh = keys.shape
    pair[:, :dh] = keys[...]
    rate = jnp.broadcast_to(rates[...], (128, n)).T
    for c in range(0, dh, 128):
        pair[:, dh + c : dh + c + 128] = (values[:, c : c + 128].astype(F32) * rate).astype(BF)


def message_kernel(keys, values, rates, *refs):
    out, *near, sems = refs
    for c in fetch(list(zip((keys, values, rates), near)), sems):
        c.wait()
    side_by_side(out, *near)


def share_kernel(keys, values, rates, queries, stream, share, full, v, rate_row, rate, sems):
    rows, width = share.shape
    dh, n = width // 2, queries.shape[0]
    wide = dh // 2
    me = lax.axis_index("rep")
    mine = window(me, rows)
    pairs = [(keys.at[mine, :], share.at[:, :dh]), (values.at[mine, :], v), (rates, rate_row)]
    pairs.append((queries.at[mine, :], full.at[:, width : width + dh]))
    for i in range(n // rows):
        at = width + dh + i * wide
        pairs.append((stream.at[i * rows : (i + 1) * rows, window(me, wide)], full.at[:, at : at + wide]))
    copies = fetch(pairs, sems)
    for c in copies[:3]:
        c.wait()
    rate[...] = jnp.broadcast_to(rate_row[...], (128, rate.shape[0])).T
    by_row = rate[mine, :]
    for c in range(0, dh, 128):
        share[:, dh + c : dh + c + 128] = (v[:, c : c + 128].astype(F32) * by_row).astype(BF)
    full[:, :width] = share[...]
    for c in copies[3:]:
        c.wait()


def pack_kernel(up, down, out):
    deep, wide = up.shape[0], out.shape[2]
    for t in range(out.shape[0]):
        part = window(lax.axis_index("groups") * 2 + t % 2, wide)
        out[t, :deep, :] = up[:, part]
        out[t, deep:, :] = down[part, :]


def gradients(k, e, w1b, w3b, w2b):
    a1, a3, b = dot(k, w1b), dot(k, w3b), dot(e, w2b, ((1,), (1,)))
    sig = jax.nn.sigmoid(a1)
    act = a1 * sig
    g = (act * a3).astype(BF)
    r1 = (b * a3 * (sig * (1.0 + a1 * (1.0 - sig)))).astype(BF)
    r3 = (b * act).astype(BF)
    first = ((0,), (0,))
    return dot(k, r1, first), dot(k, r3, first), dot(g, e, first)


def squares(x):
    return jnp.sum(x * x, axis=0, keepdims=True)


def fast_kernel(n_pieces, near, *refs):
    far, refs = refs[:9], refs[9:]
    pieces, refs = refs[:n_pieces], refs[n_pieces:]
    own_out, own_sq, send, base, gains, ks, es, hp, qs, pair, *local, sems = refs
    w1, w3, w2, keys, values, rates, q, stream, gain = local
    copies = fetch(list(zip(far, local)), sems)
    dh, hidden = w1.shape
    me = lax.axis_index("rep")
    n = q.shape[0]
    at = 0
    for p in pieces:
        rows = p.shape[0]
        ks[at : at + rows, :] = p[:, :dh]
        es[at : at + rows, :] = p[:, dh : 2 * dh]
        at += rows
    if near > 1:
        mine, theirs = pieces[0], pieces[n_pieces // 2]
        rows = mine.shape[0]
        qs[pl.ds(pl.multiple_of(n + me * rows, rows), rows), :] = mine[:, 2 * dh : 3 * dh]
        qs[pl.ds(pl.multiple_of(n + (1 - me) * rows, rows), rows), :] = theirs[:, 2 * dh : 3 * dh]
    for c in copies[3:]:
        c.wait()
    if near > 1:
        side_by_side(pair, keys, values, rates)
        ks[at : at + n, :] = pair[:, :dh]
        es[at : at + n, :] = pair[:, dh:]
        at += n
    qs[:n, :] = q[...]
    asked = qs[...]
    tokens, step, block = at, min(at, 512), min(hidden, 256)
    for c in copies[:3]:
        c.wait()
    old_sq = squares(w2[...])
    new_sq = jnp.zeros((1, dh), F32)
    for j in range(0, hidden, block):
        js = slice(j, j + block)
        x1, x3, x2 = w1[:, js], w3[:, js], w2[js, :]
        b1, b3, b2 = x1.astype(BF), x3.astype(BF), x2.astype(BF)

        def add(i, sums):
            rows = pl.ds(pl.multiple_of(i * step, step), step)
            return tuple(s + p for s, p in zip(sums, gradients(ks[rows, :], es[rows, :], b1, b3, b2)))

        sums = (x1, x3, x2)
        sums = add(0, sums) if tokens == step else lax.fori_loop(0, tokens // step, add, sums)

        def normed(old, new):
            return (new * (jnp.sqrt(squares(old)) * lax.rsqrt(squares(new) + 1e-06))).astype(BF)

        new_sq = new_sq + squares(sums[2])
        qa, qc = dot(asked, normed(x1, sums[0])), dot(asked, normed(x3, sums[1]))
        part = dot((qa * jax.nn.sigmoid(qa) * qc).astype(BF), sums[2].astype(BF))
        hp[...] = part if j == 0 else hp[...] + part
    rows, wide = own_out.shape
    base[...] = stream[:, window(me, wide)]
    x = jnp.broadcast_to(gain[:, window(me, wide)], gains.shape)
    row = lax.broadcasted_iota(jnp.int32, x.shape, 0)
    top = x.astype(BF).astype(F32)
    mid = (x - top).astype(BF).astype(F32)
    gains[...] = jnp.where(row == 0, top, jnp.where(row == 1, mid, jnp.where(row == 2, x - top - mid, 0.0))).astype(BF)
    own_out[...] = hp[:, window(me, wide)]
    send[:rows, :] = hp[:, window(1 - me, wide)].astype(BF)
    row = lax.broadcasted_iota(jnp.int32, (8, dh), 0)
    hp[:8, :] = jnp.where(row == 0, old_sq, jnp.where(row == 1, new_sq, 0.0))
    own_sq[...] = hp[:8, window(me, wide)]
    sq = hp[:8, window(1 - me, wide)]
    top = sq.astype(BF).astype(F32)
    send[rows:, :] = jnp.concatenate([top, sq - top], axis=0).astype(BF)


def mix_kernel(own, own_sq, got, base, gains, *refs):
    *asks, mixed, low = refs
    n, wide = mixed.shape
    rows = own.shape[0]
    tail = got[rows:, :].astype(F32)
    sq = own_sq[...] + tail[:8] + tail[8:]
    y = (own[...] + got[:rows, :].astype(F32)) * (jnp.sqrt(sq[0:1]) * lax.rsqrt(sq[1:2] + 1e-06))
    mixed[...] = y[:n] + base[...].astype(F32)
    low[:n, :] = mixed[...].astype(BF)
    for message in asks:
        part = message.shape[0]
        for i in range(n // part):
            at, there = n + i * part, message.shape[1] - n // part * wide + i * wide
            low[at : at + part, :] = (y[at : at + part] + message[:, there : there + wide].astype(F32)).astype(BF)
    low[rows:, :] = gains[...]


def norm_kernel(places, *refs):
    pieces, zs = refs[:-1], refs[-1]
    me_h, me_r = lax.axis_index("head"), lax.axis_index("rep")
    n_head = lax.axis_size("head")
    n, wide = pieces[0].shape[0] - 16, pieces[0].shape[1]
    for dg in range(lax.axis_size("groups")):
        here = [(p, dh, dr) for p, (g, dh, dr) in zip(pieces, places) if g == dg]
        norm = jnp.zeros((n, 1), F32)
        for p, _, _ in here:
            x = p[:n, :].astype(F32)
            norm = norm + jnp.sum(x * x, axis=1, keepdims=True)
        inv = lax.rsqrt(norm / zs.shape[1] + 1e-06)
        for p, dh, dr in here:
            r = lax.rem(me_r + dr, 2)
            head = lax.rem(me_h + dh, n_head)
            gain = jnp.sum(p[n:, :].astype(F32), axis=0, keepdims=True)
            zs[dg * n : (dg + 1) * n, window(head * 2 + r, wide)] = (p[:n, :].astype(F32) * inv * gain).astype(BF)


def blocks_of(mlp, width):
    if len(mlp) > 1:
        return [mlp[0]], [mlp[1]]
    deep = width // mlp[0].shape[0]
    each = range(mlp[0].shape[0])
    return [mlp[0].at[t, :deep, :] for t in each], [mlp[0].at[t, deep:, :] for t in each]


def feed(z, ups, downs, out):
    n_head = lax.axis_size("head")
    part = z.shape[1] // n_head
    deep = z.shape[1] // len(ups)
    wide = min(deep, part)
    total = None
    for t, x in enumerate(ups):
        term = dot(z[:, t * deep : (t + 1) * deep], x[...])
        total = term if total is None else total + term
    h = (0.5 * total * (1.0 + lax.erf(total * np.float32(0.5**0.5)))).astype(BF)
    for t, x in enumerate(downs):
        for c in range(0, deep, wide):
            head, at = divmod(t * deep + c, part)
            place = lax.rem(head - lax.axis_index("head") + n_head, n_head) * part + at
            out[:, pl.ds(pl.multiple_of(place, wide), wide)] = dot(h, x[:, c : c + wide]).astype(out.dtype)


def feed_kernel(ours, zs, *refs):
    *mlp, out = refs
    ups, downs = blocks_of(mlp, zs.shape[1])
    me = lax.axis_index("rep")
    feed(zs[window(me if ours else 1 - me, out.shape[0]), :], ups, downs, out)


def pair_kernel(moves, own, got, *outs):
    n, wide = outs[0].shape
    for (dz, dh), out in zip(moves, outs):
        rows, cols = slice(dz * n, (dz + 1) * n), slice(dh * wide, (dh + 1) * wide)
        out[...] = (own[rows, cols] + got[rows, cols].astype(F32)).astype(BF)


def sum_kernel(*refs):
    *parts, own, mixed, keep, send, acc = refs
    me = lax.axis_index("rep")
    total = jnp.where(me == 0, own[...].astype(F32), 0.0)
    for p in parts:
        total = total + p[...].astype(F32)
    acc[...] = total
    wide = keep.shape[1]
    keep[...] = mixed[...] + acc[:, window(me, wide)]
    send[...] = acc[:, window(1 - me, wide)].astype(BF)


def dealt(x, tok, head):
    axes = ("groups", "tok", "head", "rep")
    sizes = [lax.axis_size(a) for a in axes]
    pairs = []
    for here in range(int(np.prod(sizes))):
        g, t, h, r = np.unravel_index(here, sizes)
        there = ((g + r) % sizes[0], t ^ tok, (h + head) % sizes[2], r)
        pairs.append((here, int(np.ravel_multi_index(there, sizes))))
    return lax.ppermute(x, axes, [p for p in pairs if p[0] != p[1]])


def on_device(
    keys, values, rates, queries, stream, gain, counts, fw_one, fw_three, fw_two, mlp_up, mlp_down
):
    n_tok, n_head = lax.axis_size("tok"), lax.axis_size("head")
    groups, reps = lax.axis_size("groups"), lax.axis_size("rep")
    dh, n_key, n = keys.shape[1], keys.shape[0], queries.shape[0]
    wide = dh // reps
    paired = n_tok == 4 and n_key == n
    near = 2 if paired else 1
    units = mlp_up.shape[1] // groups // near
    barrier = lax.optimization_barrier

    rows = n_key // reps
    rate_row, gain = rates.reshape(1, n_key), gain[None, :]
    sources = [keys, values, rate_row]
    if paired:
        sources += [queries, stream]
        messages = call(
            share_kernel,
            [shape((rows, 2 * dh), BF), shape((rows, 4 * dh), BF)],
            sources,
            [
                pltpu.VMEM((rows, dh), BF),
                pltpu.VMEM((1, n_key), F32),
                pltpu.VMEM((n_key, 128), F32),
                pltpu.SemaphoreType.DMA((4 + n // rows,)),
            ],
            fetched=len(sources),
        )
    else:
        messages = call(
            message_kernel,
            [shape((n_key, 2 * dh), BF)],
            sources,
            [*local(sources), pltpu.SemaphoreType.DMA((len(sources),))],
            fetched=len(sources),
        )
    asks = []
    if paired:
        share, full = messages
        others = [moved(full, tok=1), moved(share, tok=2)]
        others.append(moved(others[1], tok=1))
        (blocks,) = call(
            pack_kernel, [shape((n_tok, mlp_up.shape[0] + units, units), BF)], [mlp_up, mlp_down]
        )
        others, blocks = barrier((others, blocks))
        mlp = [lax.all_to_all(blocks, "tok", 0, 0)]
        tokens = [*others, *[moved(x, rep=1) for x in others]]
        asks = others[:1]
    else:
        me_g = lax.axis_index("groups")
        up_own = lax.dynamic_slice_in_dim(mlp_up, me_g * units, units, 1)
        down_own = lax.dynamic_slice_in_dim(mlp_down, me_g * units, units, 0)
        tokens = [lax.all_gather(messages[0], "tok", axis=0, tiled=True)]
        mlp = [
            lax.all_gather(up_own, "tok", axis=0, tiled=True),
            lax.all_gather(down_own, "tok", axis=1, tiled=True),
        ]

    n_all = sum(x.shape[0] for x in tokens) + (n_key if paired else 0)
    tokens = barrier(tokens)
    sources = [fw_one[0], fw_three[0], fw_two[0], keys, values, rate_row, queries, stream, gain]
    own, own_sq, send, base, gains = call(
        functools.partial(fast_kernel, len(tokens), near),
        [
            shape((near * n, wide), F32),
            shape((8, wide), F32),
            shape((near * n + 16, wide), BF),
            shape((n, wide), BF),
            shape((16, wide), BF),
        ],
        [*sources, *tokens],
        [
            pltpu.VMEM((n_all, dh), BF),
            pltpu.VMEM((n_all, dh), BF),
            pltpu.VMEM((near * n, dh), F32),
            pltpu.VMEM((near * n, dh), BF),
            pltpu.VMEM((n_key, 2 * dh), BF),
            *local(sources),
            pltpu.SemaphoreType.DMA((len(sources),)),
        ],
        fetched=len(sources),
    )
    got = moved(send, rep=1)
    mixed, low = call(
        mix_kernel,
        [shape((n, wide), F32), shape((near * n + 16, wide), BF)],
        [own, own_sq, got, base, gains, *asks],
    )
    pieces, places = [], []
    for dg, h in itertools.product(range(groups), range(n_head)):
        x = moved(low, groups=dg, head=h)
        pieces += [x, moved(x, rep=1)]
        places += [(dg, h, 0), (dg, h, 1)]
    model = n_head * dh
    (zs,) = call(
        functools.partial(norm_kernel, places), [shape((groups * near * n, model), BF)], pieces
    )
    (send,) = call(
        functools.partial(feed_kernel, False), [shape((near * n, model), BF)], [zs, *mlp]
    )
    got = moved(send, rep=1)
    (own,) = call(
        functools.partial(feed_kernel, True), [shape((near * n, model), F32)], [zs, *mlp]
    )
    moves = sorted(itertools.product(range(near), range(n_head)), key=lambda m: (m[0] + m[1] < 2, m[0], -m[1]))
    parts = call(
        functools.partial(pair_kernel, moves), [shape((n, dh), BF)] * len(moves), [own, got]
    )
    own = parts[moves.index((0, 0))]
    parts = [dealt(x, *m) for m, x in zip(moves, parts)]
    keep, send = call(
        sum_kernel, [shape((n, wide), F32), shape((n, wide), BF)], [*parts, own, mixed], [pltpu.VMEM((n, dh), F32)]
    )
    total = keep + moved(send, rep=1).astype(F32)
    live = jnp.arange(n, dtype=jnp.int32) < counts[0]
    return jnp.where(live[:, None], total, 0.0).astype(BF)


def solution(mesh):
    placed = (
        P(("groups", "tok"), "head"),
        P(("groups", "tok"), "head"),
        P(("groups", "tok"), "head"),
        P(("groups", "tok"), "head"),
        P(("groups", "tok"), "head"),
        P("head"),
        P(("groups", "tok")),
        P("head", None, "rep"),
        P("head", None, "rep"),
        P("head", "rep", None),
        P("tok", ("head", "rep")),
        P(("head", "rep"), "tok"),
    )
    return jax.shard_map(
        on_device,
        mesh=mesh,
        in_specs=placed,
        out_specs=P(("groups", "tok"), ("head", "rep")),
        check_vma=False,
    )
```
